512 devices in a mesh: member: 16 (over z), tile: 32 (over x, y, core).
Axes of the slice: x: 4, y: 4, z: 16, core: 2. Of those that a mesh axis runs over, the one named last changes fastest.
Arguments:
- adjoint_final: bfloat16 [16, 32, 1024, 192], P('member', None, 'tile'), may hold values from -6 to 6
- states: bfloat16 [2, 16, 32, 1024, 192], P(None, 'member', None, 'tile'), may hold values from -12 to 12
- kernel: float32 [7, 7, 192], replicated, may hold values from -0.875 to 0.875
- norm_gain: float32 [192], replicated, may hold values from 0.1 to 1.9
- up_weight: bfloat16 [192, 768], replicated, may hold values from -0.4375 to 0.4375
- up_bias: float32 [768], replicated, may hold values from -4 to 4
- down_weight: bfloat16 [768, 192], replicated, may hold values from -0.21875 to 0.21875
- obs_cell: int32 [2, 32, 32, 16], P(None, 'tile'), may hold values from 0 to 31
- obs_count: int32 [2, 32, 32], P(None, 'tile'), may hold values from 1 to 16, 256 in all within a row
- obs_value: bfloat16 [2, 32, 32, 16, 192], P(None, 'tile'), may hold values from -6 to 6
- obs_error: bfloat16 [2, 32, 32, 16], P(None, 'tile'), may hold values from 0.099609375 to 1
Outputs:
- adjoint_initial: bfloat16 [16, 32, 1024, 192], P('member', None, 'tile')
The draws below stay inside these ranges and needn't reach their ends.
Inputs may be any that keep to these rules, and one draw needn't show every extreme that they name: `obs_cell`: a cell number is latitude offset within the band times 32 plus longitude offset within the tile. `obs_count`: the counts of one band and time add up to 256, and the largest of them is 16.
All inputs are finite; a program needn't handle non-finite values.
Results may differ from the reference program's by a relative error of at most 0.006.
Values may be sent and summed in bfloat16 or wider, within the bound.
No kernel may reach another device: no remote copies, remote signals or barrier semaphores. Data moves between devices by JAX's collectives and lax.ppermute only.
A program may use at most 64 MiB of HBM per device.

```python
import math
import jax
import jax.numpy as jnp
import numpy as np
from jax import lax

C = 192
HID = 768
STEPS = 2
LAT = 32
LON_DEV = 32
CAP = 16
MEMBERS = 16
NLON = 1024
BAND = 1
N_TILE = 32


def draw_states(key, part):
    base_key, chan_key, member_key, noise_key = jax.random.split(jax.random.fold_in(key, 7), 4)
    full_shape = (STEPS, MEMBERS, LAT, NLON, C)
    base_field = jax.random.normal(base_key, (STEPS, 1, LAT, NLON, C), jnp.float32)
    chan_scale = jnp.exp(jax.random.uniform(chan_key, (C,), jnp.float32, math.log(0.3), math.log(2.0)))
    noise_part = jax.random.normal(noise_key, full_shape, jnp.float32)
    member_scale = jnp.exp(jax.random.uniform(member_key, (1, MEMBERS, 1, 1, 1), jnp.float32, math.log(0.4), math.log(4.0)))
    return jnp.clip(base_field + chan_scale * member_scale * noise_part, -12.0, 12.0).astype(jnp.bfloat16)


def place_ends(drawn, own_key, low, top_value):
    spot = [jax.random.randint(jax.random.fold_in(own_key, axis), (), 0, length) for axis, length in enumerate(drawn.shape)]
    main_axis = drawn.shape.index(max(drawn.shape))
    neighbour = spot[:main_axis] + [(spot[main_axis] + 1) % drawn.shape[main_axis]] + spot[main_axis + 1:]
    return drawn.at[tuple(spot)].set(low).at[tuple(neighbour)].set(top_value)


def block_scale(key, extent, pieces, low, high):
    loudness = 1.0
    for dim, parts in pieces:
        heights = jax.random.uniform(jax.random.fold_in(jax.random.fold_in(key, 6), dim), (parts,), jnp.float32, low / len(pieces), high / len(pieces))
        loudness = loudness * jnp.repeat(jnp.exp(heights), extent[dim] // parts).reshape((-1,) + (1,) * (len(extent) - 1 - dim))
    return loudness


def profile(count, total, bound, lean):
    loads = [(1 << 20) // math.isqrt(rank ** lean) + 1 for rank in range(2, count + 1)]
    spare, given = total - bound - (count - 1), [1] * (count - 1)
    while spare > 0:
        free = [i for i in range(count - 1) if given[i] < bound]
        pool, remaining = sum([loads[i] for i in free]), spare
        for i in free:
            addition = min(bound - given[i], max(1, remaining * loads[i] // pool), spare)
            given[i] = given[i] + addition
            spare = spare - addition
    return np.array([bound] + given)


def ragged_sizes(own_key, amount, total, reach, slope):
    if amount == 2:
        one = jax.random.randint(own_key, (), max(1, total - reach), min(reach, total - 1) + 1)
        return jnp.stack([one, total - one])
    tallies = jnp.asarray(profile(amount, total, reach, slope), jnp.int32)
    couples = (amount - 1) // 2
    source_of, taker = tallies[1:1 + 2 * couples:2], tallies[2:2 + 2 * couples:2]
    room = jnp.minimum(source_of - 1, reach - taker)
    shifted = jax.random.randint(jax.random.fold_in(own_key, 1), (couples,), 0, 1 << 20) % (room + 1)
    tallies = tallies.at[1:1 + 2 * couples:2].set(source_of - shifted).at[2:2 + 2 * couples:2].set(taker + shifted)
    return tallies[jax.random.permutation(jax.random.fold_in(own_key, 2), amount)]


def gaussian(key, extent, scale, reach, cuts=(), kind=jnp.bfloat16):
    entries = jax.random.normal(key, extent, jnp.float32) * scale
    if len(cuts) > 0:
        entries = block_scale(key, extent, cuts, -0.22, 0.18) * entries
    return jnp.clip(entries, min=-reach, max=reach).astype(kind)


def setup_inputs(seed: int = 0) -> dict:
    streams_of = jax.random.split(jax.random.key(seed), 12)
    return {
        "adjoint_final": gaussian(streams_of[0], (MEMBERS, LAT, NLON, C), 1.0, 6.0, ((0, 16), (2, 32))),
        "states": draw_states(jax.random.fold_in(streams_of[11], 71), 0),
        "kernel": gaussian(streams_of[2], (7, 7, C), 49 ** -0.5, 0.875, (), jnp.float32),
        "norm_gain": jnp.clip(1.0 + 0.18 * jax.random.normal(streams_of[3], (C,), jnp.float32), 0.1, 1.9),
        "up_weight": gaussian(streams_of[4], (C, HID), C ** -0.5, 0.4375),
        "up_bias": gaussian(streams_of[5], (HID,), 1.0, 4.0, (), jnp.float32),
        "down_weight": gaussian(streams_of[6], (HID, C), HID ** -0.5, 0.21875),
        "obs_cell": place_ends(jax.random.randint(streams_of[7], (STEPS, N_TILE, N_TILE, CAP), 0, BAND * LON_DEV), jax.random.fold_in(streams_of[7], 1), 0, (BAND * LON_DEV) - 1).astype(jnp.int32),
        "obs_count": jax.vmap(lambda own: ragged_sizes(own, N_TILE, N_TILE * CAP // 2, CAP, 2))(jax.random.split(streams_of[8], STEPS * N_TILE)).reshape((STEPS, N_TILE, N_TILE)).astype(jnp.int32),
        "obs_value": gaussian(streams_of[9], (STEPS, N_TILE, N_TILE, CAP, C), 1.0, 6.0, ((1, 32),)),
        "obs_error": jnp.clip(jnp.exp(math.log(1.0) - 2.306499 * jax.random.uniform(streams_of[10], (STEPS, N_TILE, N_TILE, CAP), jnp.float32) ** block_scale(streams_of[10], (STEPS, N_TILE, N_TILE, CAP), ((1, 32),), -0.2, 0.2)), 0.099609375, 1.0).astype(jnp.bfloat16),
    }


slope_coef = math.sqrt(2.0 / math.pi)
cubic_coef = 0.044715
norm_eps = 1e-06

def gelu_slope(preact):
    inner_arg = slope_coef * (preact + cubic_coef * preact * preact * preact)
    tanh_val = jnp.tanh(inner_arg)
    return 0.5 * (1.0 + tanh_val) + 0.5 * preact * (1.0 - tanh_val * tanh_val) * slope_coef * (1.0 + 3.0 * cubic_coef * preact * preact)

def wrap_lon(field_in):
    return jnp.concatenate([field_in[:, -3:], field_in, field_in[:, :3]], axis=1)

def pad_rows(field_in):
    return jnp.pad(field_in, ((3, 3), (0, 0), (0, 0)))

def depthwise(padded, kernel, lat_count, lon_width):
    summed = jnp.zeros((lat_count, lon_width, padded.shape[2]), jnp.float32)
    for row_tap in range(7):
        for col_tap in range(7):
            summed = summed + kernel[row_tap, col_tap] * padded[row_tap:row_tap + lat_count, col_tap:col_tap + lon_width]
    return summed

def depthwise_adjoint(padded, kernel, lat_count, lon_width):
    summed = jnp.zeros((lat_count, lon_width, padded.shape[2]), jnp.float32)
    for row_tap in range(7):
        for col_tap in range(7):
            summed = summed + kernel[row_tap, col_tap] * padded[6 - row_tap:6 - row_tap + lat_count, 6 - col_tap:6 - col_tap + lon_width]
    return summed

def member_step(adjoint, state, forcing, kernel, norm_gain, up_weight, up_bias, down_weight):
    lat_count, lon_width, channels = state.shape
    hidden = depthwise(pad_rows(wrap_lon(state.astype(jnp.float32))), kernel, lat_count, lon_width)
    centred = hidden - lax.optimization_barrier(jnp.mean(hidden, axis=-1, keepdims=True))
    inv_std = lax.rsqrt(lax.optimization_barrier(jnp.mean(centred * centred, axis=-1, keepdims=True)) + norm_eps)
    unit_norm = centred * inv_std
    normed = (unit_norm * norm_gain).astype(jnp.bfloat16)
    preact = jnp.dot(normed.reshape(-1, channels), up_weight, preferred_element_type=jnp.float32) + up_bias
    adj_act = jnp.dot(adjoint.reshape(-1, channels), down_weight.T, preferred_element_type=jnp.float32)
    adj_pre = (adj_act * gelu_slope(preact)).astype(jnp.bfloat16)
    adj_norm = jnp.dot(adj_pre, up_weight.T, preferred_element_type=jnp.float32).reshape(state.shape)
    scaled = adj_norm * norm_gain
    adj_hidden = (inv_std * (scaled - lax.optimization_barrier(jnp.mean(scaled, axis=-1, keepdims=True)) - unit_norm * lax.optimization_barrier(jnp.mean(scaled * unit_norm, axis=-1, keepdims=True)))).astype(jnp.bfloat16)
    spread_back = depthwise_adjoint(pad_rows(wrap_lon(adj_hidden.astype(jnp.float32))), kernel, lat_count, lon_width)
    return (adjoint.astype(jnp.float32) + spread_back + forcing).astype(jnp.bfloat16)

def reference(adjoint_final, states, kernel, norm_gain, up_weight, up_bias, down_weight, obs_cell, obs_count, obs_value, obs_error):
    band_ids = jnp.arange(N_TILE, dtype=jnp.int32)[:, None, None]
    tile_ids = jnp.arange(N_TILE, dtype=jnp.int32)[None, :, None]
    adjoint = adjoint_final
    for section_idx in range(STEPS):
        cell_ids = obs_cell[section_idx]
        lat_ids = band_ids * BAND + cell_ids // LON_DEV
        lon_ids = tile_ids * LON_DEV + cell_ids % LON_DEV
        live_mask = jnp.arange(CAP, dtype=jnp.int32)[None, None, :] < obs_count[section_idx][:, :, None]
        sampled = states[section_idx][:, lat_ids, lon_ids, :].astype(jnp.float32)
        ens_mean = lax.optimization_barrier(jnp.sum(sampled, axis=0)) / MEMBERS
        ens_var = lax.optimization_barrier(jnp.sum(sampled * sampled, axis=0)) / MEMBERS - ens_mean * ens_mean
        ratio = (sampled - obs_value[section_idx].astype(jnp.float32)) / (obs_error[section_idx].astype(jnp.float32)[..., None] + ens_var)
        dep_rows = jnp.where(live_mask[None, :, :, :, None], ratio, 0.0).astype(jnp.bfloat16)

        def per_member(packed):
            adjoint_m, state_m, rows_m = packed
            forcing = jnp.zeros((LAT, NLON, C), jnp.float32).at[lat_ids, lon_ids].add(rows_m.astype(jnp.float32))
            return member_step(adjoint_m, state_m, forcing, kernel, norm_gain, up_weight, up_bias, down_weight)
        adjoint = lax.map(per_member, (adjoint, states[section_idx], dep_rows))
    return adjoint
```

```python
import functools
import math

import jax
import jax.numpy as jnp
from jax import lax
from jax.experimental import pallas as pl
from jax.experimental.pallas import tpu as pltpu
from jax.sharding import PartitionSpec as P

slope_coef = math.sqrt(2.0 / math.pi)
cubic_coef = 0.044715
norm_eps = 1e-06

LAT = 32
WID = 32
CH = 192
HID = 768
CAP = 16
CELLS = LAT * WID
SLOTS = LAT * CAP
BLK = 8
ROWS = BLK * WID
f32 = jnp.float32
bf16 = jnp.bfloat16
NT = (((1,), (1,)), ((), ()))
TN = (((0,), (0,)), ((), ()))


def gelu_slope(preact):
    square = preact * preact
    tanh_val = jnp.tanh(preact * (slope_coef + (slope_coef * cubic_coef) * square))
    tail = preact * (0.5 * slope_coef + (1.5 * slope_coef * cubic_coef) * square)
    return (0.5 + 0.5 * tanh_val) + tail * (1.0 - tanh_val * tanh_val)


def mean_lanes(value):
    return jnp.sum(value, axis=-1, keepdims=True) * (1.0 / CH)


def build_shifts(shifts, padded, centre, left, right):
    for edge in range(3):
        zeros = jnp.zeros((WID, CH), f32)
        for col in range(7):
            shifts[col, edge] = zeros
            shifts[col, LAT + 3 + edge] = zeros

    def one_row(row, carry):
        padded[0:3] = left(row).astype(f32)
        padded[3 : WID + 3] = centre(row).astype(f32)
        padded[WID + 3 : WID + 6] = right(row).astype(f32)
        for col in range(7):
            shifts[col, row + 3] = padded[col : col + WID]
        return carry

    lax.fori_loop(0, LAT, one_row, 0)


def convolve(shifts, kernel_ref, first, flip, emit):
    for low, high in ((0, 128), (128, CH)):
        sums = [None] * BLK
        for col in range(7):
            taps = []
            for row in range(7):
                index = (6 - row) * 7 + 6 - col if flip else row * 7 + col
                taps.append(jnp.broadcast_to(kernel_ref[index : index + 1, low:high], (WID, high - low)))
            for source in range(BLK + 6):
                field = shifts[col, first + source, :, low:high]
                for row in range(7):
                    target = source - row
                    if 0 <= target < BLK:
                        term = taps[row] * field
                        sums[target] = term if sums[target] is None else sums[target] + term
        for target in range(BLK):
            emit(target, low, high, sums[target])


def gather_kernel(got_ref, state_ref, out_ref, hot_ref):
    for step in range(2):
        cells = got_ref[:, step, CH : CH + CAP].astype(f32)
        lane = lax.broadcasted_iota(jnp.int32, (LAT, CELLS), 1)
        band = lax.broadcasted_iota(jnp.int32, (LAT, CELLS), 0)
        offset = (lane - band * WID).astype(f32)
        for slot in range(CAP):
            hot = jnp.where(offset == cells[:, slot : slot + 1], 1.0, 0.0)
            hot_ref[slot * LAT : (slot + 1) * LAT] = hot.astype(bf16)
        rows = jnp.dot(hot_ref[...], state_ref[step], preferred_element_type=f32)
        out_ref[:, :, step * CH : (step + 1) * CH] = rows.astype(bf16).reshape(CAP, LAT, CH)


def gather_rows(got, states):
    return pl.pallas_call(
        gather_kernel,
        out_shape=jax.ShapeDtypeStruct((CAP, LAT, 2 * CH), bf16),
        scratch_shapes=[pltpu.VMEM((SLOTS, CELLS), bf16)],
        cost_estimate=pl.CostEstimate(flops=2 * 2 * SLOTS * CELLS * CH, bytes_accessed=2000000, transcendentals=0),
    )(got, states)


def departure_kernel(step, rows_ref, got_ref, out_ref):
    sampled = rows_ref[:, :, step * CH : (step + 1) * CH].astype(f32)
    members = sampled.shape[0]
    own = got_ref[:, step, :].astype(f32)
    ens_mean = jnp.sum(sampled, axis=0) * (1.0 / members)
    ens_var = jnp.sum(sampled * sampled, axis=0) * (1.0 / members) - ens_mean * ens_mean
    weight = 1.0 / (own[:, CH + CAP : CH + CAP + 1] + ens_var)
    ratio = (sampled - own[None, :, :CH]) * weight[None]
    live = own[:, CH + CAP + 1 : CH + CAP + 2] >= 0.0
    out_ref[...] = jnp.where(live[None], ratio, 0.0).astype(bf16)


def departures(step, rows, got):
    return pl.pallas_call(
        functools.partial(departure_kernel, step),
        out_shape=jax.ShapeDtypeStruct((CAP, LAT, CH), bf16),
        cost_estimate=pl.CostEstimate(flops=600000, bytes_accessed=600000, transcendentals=0),
    )(rows, got)


def forcing_of(step, rows_ref, got_ref, hot_ref, first, count):
    cells = got_ref[:, step, CH : CH + CAP].astype(f32)
    lane = lax.broadcasted_iota(jnp.int32, (LAT, count), 1) + first
    band = lax.broadcasted_iota(jnp.int32, (LAT, count), 0)
    offset = (lane - band * WID).astype(f32)
    for slot in range(CAP):
        hot = jnp.where(offset == cells[:, slot : slot + 1], 1.0, 0.0)
        hot_ref[slot * LAT : (slot + 1) * LAT] = hot.astype(bf16)
    rows = rows_ref[...].reshape(SLOTS, CH)
    return lax.dot_general(hot_ref[...], rows, TN, preferred_element_type=f32)


def normalise(hidden):
    centred = hidden - mean_lanes(hidden)
    inv_std = lax.rsqrt(mean_lanes(centred * centred) + norm_eps)
    return centred * inv_std, inv_std


def backward(adjoint, slope_at, down_ref, up_ref, gain, unit, inv_std):
    adj_norm = jnp.zeros((ROWS, CH), f32)
    for part in range(3):
        cols = slice(part * 256, (part + 1) * 256)
        act = lax.dot_general(adjoint, down_ref[cols, :], NT, preferred_element_type=f32)
        pre = (act * slope_at(cols)).astype(bf16)
        adj_norm = adj_norm + lax.dot_general(pre, up_ref[:, cols], NT, preferred_element_type=f32)
    scaled = adj_norm * gain
    return inv_std * (scaled - mean_lanes(scaled) - unit * mean_lanes(scaled * unit))


def put_hidden(adj_hidden, first, out_ref, head_ref, tail_ref):
    block = adj_hidden.astype(bf16).reshape(BLK, WID, CH)
    out_ref[pl.ds(first, BLK)] = block
    head_ref[pl.ds(first, BLK)] = block[:, 0:3]
    tail_ref[pl.ds(first, BLK)] = block[:, WID - 3 : WID]


def forward_kernel(
    state_ref, left_ref, right_ref, adjoint_ref, kernel_ref, gain_ref, up_ref, bias_ref, down_ref,
    hidden_out, head_out, tail_out, slope_out, unit_out,
    shifts, padded, hidden,
):
    gain = gain_ref[...]
    for step in range(2):
        build_shifts(
            shifts, padded,
            lambda row: state_ref[step, row],
            lambda row: left_ref[step, row],
            lambda row: right_ref[step, row],
        )

        def block(index, carry):
            first = index * BLK

            def emit(target, low, high, value):
                hidden[target, :, low:high] = value

            convolve(shifts, kernel_ref, first, False, emit)
            unit, inv_std = normalise(hidden[...].reshape(ROWS, CH))
            normed = (unit * gain).astype(bf16)

            def slope_at(cols):
                preact = jnp.dot(normed, up_ref[:, cols], preferred_element_type=f32)
                return gelu_slope(preact + bias_ref[:, cols])

            if step == 0:
                adjoint = adjoint_ref[pl.ds(first, BLK)].reshape(ROWS, CH)
                result = backward(adjoint, slope_at, down_ref, up_ref, gain, unit, inv_std)
                put_hidden(result, first, hidden_out, head_out, tail_out)
            else:
                rows = pl.ds(pl.multiple_of(index * ROWS, ROWS), ROWS)
                for part in range(3):
                    cols = slice(part * 256, (part + 1) * 256)
                    slope_out[rows, cols] = slope_at(cols).astype(bf16)
                unit_out[rows, 0:CH] = unit
                unit_out[rows, CH:256] = jnp.broadcast_to(inv_std, (ROWS, 256 - CH))
            return carry

        lax.fori_loop(0, LAT // BLK, block, 0)


EDGE = jax.ShapeDtypeStruct((LAT, 3, CH), bf16)
FIELD = jax.ShapeDtypeStruct((LAT, WID, CH), bf16)
SHIFT_SCRATCH = [pltpu.VMEM((7, LAT + 6, WID, CH), f32), pltpu.VMEM((WID + 8, CH), f32)]
BIG = pltpu.CompilerParams(vmem_limit_bytes=40 * 1024 * 1024)


def forward_both(states, left, right, adjoint, kernel, gain, up, bias, down):
    return pl.pallas_call(
        forward_kernel,
        out_shape=(
            FIELD, EDGE, EDGE,
            jax.ShapeDtypeStruct((CELLS, HID), bf16),
            jax.ShapeDtypeStruct((CELLS, 256), f32),
        ),
        scratch_shapes=SHIFT_SCRATCH + [pltpu.VMEM((BLK, WID, CH), f32)],
        compiler_params=BIG,
        cost_estimate=pl.CostEstimate(flops=8 * CELLS * CH * HID, bytes_accessed=8000000, transcendentals=2 * CELLS * HID),
    )(states, left, right, adjoint, kernel, gain, up, bias, down)


def spread_kernel(hidden_ref, left_ref, right_ref, base_ref, kernel_ref, out_ref, shifts, padded):
    build_shifts(
        shifts, padded,
        lambda row: hidden_ref[row],
        lambda row: left_ref[row],
        lambda row: right_ref[row],
    )

    def block(index, carry):
        first = index * BLK

        def emit(target, low, high, value):
            base = base_ref[first + target, :, low:high].astype(f32)
            out_ref[first + target, :, low:high] = (base + value).astype(out_ref.dtype)

        convolve(shifts, kernel_ref, first, True, emit)
        return carry

    lax.fori_loop(0, LAT // BLK, block, 0)


def spread_back(hidden, left, right, base, kernel, dtype):
    return pl.pallas_call(
        spread_kernel,
        out_shape=jax.ShapeDtypeStruct((LAT, WID, CH), dtype),
        scratch_shapes=SHIFT_SCRATCH,
        compiler_params=BIG,
        cost_estimate=pl.CostEstimate(flops=98 * CELLS * CH, bytes_accessed=3000000, transcendentals=0),
    )(hidden, left, right, base, kernel)


def second_kernel(
    partial_ref, rows_ref, got_ref, slope_ref, unit_ref, gain_ref, up_ref, down_ref,
    hidden_out, head_out, tail_out, adjoint_out, hot,
):
    gain = gain_ref[...]
    forcing = forcing_of(0, rows_ref, got_ref, hot, 0, CELLS)
    adjoint_all = (partial_ref[...].reshape(CELLS, CH) + forcing).astype(bf16)
    adjoint_out[...] = adjoint_all.reshape(LAT, WID, CH)

    def block(index, carry):
        first = index * BLK
        rows = pl.ds(pl.multiple_of(index * ROWS, ROWS), ROWS)
        adjoint = adjoint_out[pl.ds(first, BLK)].reshape(ROWS, CH)
        result = backward(
            adjoint,
            lambda cols: slope_ref[rows, cols].astype(f32),
            down_ref, up_ref, gain,
            unit_ref[rows, 0:CH], unit_ref[rows, CH : CH + 1],
        )
        put_hidden(result, first, hidden_out, head_out, tail_out)
        return carry

    lax.fori_loop(0, LAT // BLK, block, 0)


def second_step(partial, rows, got, slope, unit, gain, up, down):
    return pl.pallas_call(
        second_kernel,
        out_shape=(FIELD, EDGE, EDGE, FIELD),
        scratch_shapes=[pltpu.VMEM((SLOTS, CELLS), bf16)],
        compiler_params=BIG,
        cost_estimate=pl.CostEstimate(flops=4 * CELLS * CH * HID, bytes_accessed=5000000, transcendentals=0),
    )(partial, rows, got, slope, unit, gain, up, down)


def base_kernel(adjoint_ref, rows_ref, got_ref, out_ref, hot):
    forcing = forcing_of(1, rows_ref, got_ref, hot, 0, CELLS)
    out_ref[...] = adjoint_ref[...].astype(f32) + forcing.reshape(LAT, WID, CH)


def last_base(adjoint, rows, got):
    return pl.pallas_call(
        base_kernel,
        out_shape=jax.ShapeDtypeStruct((LAT, WID, CH), f32),
        scratch_shapes=[pltpu.VMEM((SLOTS, CELLS), bf16)],
        compiler_params=BIG,
        cost_estimate=pl.CostEstimate(flops=2 * SLOTS * CELLS * CH, bytes_accessed=1500000, transcendentals=0),
    )(adjoint, rows, got)


def swap_edges(head, tail):
    peers = lax.axis_size("tile")
    up = [(i, (i + 1) % peers) for i in range(peers)]
    down = [(j, i) for i, j in up]
    return lax.ppermute(tail, "tile", up), lax.ppermute(head, "tile", down)


def pack_observations(cells, counts, values, errors):
    member = lax.axis_index("member")
    live = lax.broadcasted_iota(jnp.int32, cells.shape, 2) < counts[:, :, None]
    masked = jnp.where(live, cells, -1).astype(bf16)
    pick = lambda array: lax.dynamic_slice_in_dim(array, member, 1, axis=2)
    packed = jnp.concatenate(
        [pick(values)[:, :, 0], masked, pick(errors), pick(masked), jnp.zeros(cells.shape[:2] + (256 - CH - CAP - 2,), bf16)],
        axis=2,
    )
    return packed.transpose(1, 0, 2)


def exchange(array, axis):
    return lax.all_to_all(array, axis, split_axis=0, concat_axis=0, tiled=True)


def per_device(
    adjoint_final, states, kernel, norm_gain, up_weight, up_bias, down_weight,
    obs_cell, obs_count, obs_value, obs_error,
):
    adjoint = adjoint_final[0]
    states = states[:, 0]
    taps = kernel.reshape(49, CH)
    gain = norm_gain[None]
    bias = up_bias[None]

    packed = pack_observations(obs_cell[:, 0], obs_count[:, 0], obs_value[:, 0], obs_error[:, 0])
    got = exchange(packed, "tile")
    left, right = swap_edges(states[:, :, 0:3], states[:, :, WID - 3 : WID])

    rows = gather_rows(got, states.reshape(2, CELLS, CH))
    owned = exchange(rows, "member")

    hidden, head, tail, slope, unit = forward_both(
        states, left, right, adjoint, taps, gain, up_weight, bias, down_weight
    )
    partial = spread_back(hidden, *swap_edges(head, tail), adjoint, taps, f32)

    back0 = exchange(departures(0, owned, got), "member")
    back1 = exchange(departures(1, owned, got), "member")

    hidden, head, tail, adjoint = second_step(partial, back0, got, slope, unit, gain, up_weight, down_weight)
    base = last_base(adjoint, back1, got)
    return spread_back(hidden, *swap_edges(head, tail), base, taps, bf16)[None]


def solution(mesh):
    placed = (
        P("member", None, "tile", None),
        P(None, "member", None, "tile", None),
        P(),
        P(),
        P(),
        P(),
        P(),
        P(None, "tile", None, None),
        P(None, "tile", None),
        P(None, "tile", None, None, None),
        P(None, "tile", None, None),
    )
    return jax.shard_map(
        per_device,
        mesh=mesh,
        in_specs=placed,
        out_specs=P("member", None, "tile", None),
        check_vma=False,
    )
```

```python
import functools
import math

import jax
import jax.numpy as jnp
from jax import lax
from jax.experimental import pallas as pl
from jax.experimental.pallas import tpu as pltpu
from jax.sharding import PartitionSpec as P

slope_coef = math.sqrt(2.0 / math.pi)
cubic_coef = 0.044715
norm_eps = 1e-06

LAT = 32
WID = 32
CH = 192
HID = 768
CAP = 16
CELLS = LAT * WID
SLOTS = LAT * CAP
BLK = 8
ROWS = BLK * WID
f32 = jnp.float32
bf16 = jnp.bfloat16
NT = (((1,), (1,)), ((), ()))
TN = (((0,), (0,)), ((), ()))


def gelu_slope(preact):
    square = preact * preact
    tanh_val = jnp.tanh(preact * (slope_coef + (slope_coef * cubic_coef) * square))
    tail = preact * (0.5 * slope_coef + (1.5 * slope_coef * cubic_coef) * square)
    return (0.5 + 0.5 * tanh_val) + tail * (1.0 - tanh_val * tanh_val)


def mean_lanes(value):
    return jnp.sum(value, axis=-1, keepdims=True) * (1.0 / CH)


def build_shifts(shifts, padded, centre, left, right):
    for edge in range(3):
        zeros = jnp.zeros((WID, CH), f32)
        for col in range(7):
            shifts[col, edge] = zeros
            shifts[col, LAT + 3 + edge] = zeros

    def one_row(row, carry):
        padded[0:3] = left(row).astype(f32)
        padded[3 : WID + 3] = centre(row).astype(f32)
        padded[WID + 3 : WID + 6] = right(row).astype(f32)
        for col in range(7):
            shifts[col, row + 3] = padded[col : col + WID]
        return carry

    lax.fori_loop(0, LAT, one_row, 0)


def convolve(shifts, kernel_ref, first, flip, emit):
    for low, high in ((0, 128), (128, CH)):
        sums = [None] * BLK
        for col in range(7):
            taps = []
            for row in range(7):
                index = (6 - row) * 7 + 6 - col if flip else row * 7 + col
                taps.append(jnp.broadcast_to(kernel_ref[index : index + 1, low:high], (WID, high - low)))
            for source in range(BLK + 6):
                field = shifts[col, first + source, :, low:high]
                for row in range(7):
                    target = source - row
                    if 0 <= target < BLK:
                        term = taps[row] * field
                        sums[target] = term if sums[target] is None else sums[target] + term
        for target in range(BLK):
            emit(target, low, high, sums[target])


def cut_kernel(state_ref, head_ref, tail_ref):
    head_ref[...] = state_ref[:, :, 0:3]
    tail_ref[...] = state_ref[:, :, WID - 3 : WID]


def cut_edges(states):
    edge = jax.ShapeDtypeStruct((2, LAT, 3, CH), bf16)
    return pl.pallas_call(cut_kernel, out_shape=(edge, edge))(states)


def pack_kernel(cell_ref, count_ref, value_ref, error_ref, out_ref):
    member = lax.axis_index("member")
    tiles = cell_ref.shape[1]
    slot = lax.broadcasted_iota(jnp.int32, (tiles, CAP), 1)
    same = lax.broadcasted_iota(jnp.int32, (tiles, tiles), 0) == lax.broadcasted_iota(jnp.int32, (tiles, tiles), 1)
    deep = lax.broadcasted_iota(jnp.int32, (tiles, CAP, CH), 1)
    for step in range(2):
        counts = count_ref[step : step + 1, :].astype(f32)
        count = jnp.sum(jnp.where(same, jnp.broadcast_to(counts, (tiles, tiles)), 0.0), axis=1, keepdims=True)
        cells = jnp.where(slot.astype(f32) < count, cell_ref[step].astype(f32), -1.0)
        pick = lambda array: jnp.sum(jnp.where(slot == member, array, 0.0), axis=1, keepdims=True)
        values = jnp.sum(jnp.where(deep == member, value_ref[step].astype(f32), 0.0), axis=1)
        out_ref[:, 2 * step, :] = values[:, 0:128]
        out_ref[:, 2 * step + 1, :] = jnp.concatenate(
            [values[:, 128:CH], cells, jnp.broadcast_to(pick(error_ref[step].astype(f32)), (tiles, CAP)),
             jnp.broadcast_to(pick(cells), (tiles, 2 * CAP))], axis=1)


def pack_observations(cells, counts, values, errors):
    return pl.pallas_call(
        pack_kernel,
        out_shape=jax.ShapeDtypeStruct((cells.shape[1], 4, 128), f32),
    )(cells, counts, values, errors)


def one_hot(step, got_ref, hot_ref):
    cells = got_ref[:, 2 * step + 1, 64 : 64 + CAP]
    lane = lax.broadcasted_iota(jnp.int32, (LAT, CELLS), 1)
    band = lax.broadcasted_iota(jnp.int32, (LAT, CELLS), 0)
    offset = (lane - band * WID).astype(f32)
    for slot in range(CAP):
        hot = jnp.where(offset == cells[:, slot : slot + 1], 1.0, 0.0)
        hot_ref[slot * LAT : (slot + 1) * LAT] = hot.astype(bf16)


def gather_kernel(got_ref, state_ref, out_ref, *hots):
    for step in range(2):
        one_hot(step, got_ref, hots[step])
        rows = jnp.dot(hots[step][...], state_ref[step].reshape(CELLS, CH), preferred_element_type=f32)
        out_ref[:, :, step * CH : (step + 1) * CH] = rows.astype(bf16).reshape(CAP, LAT, CH)


def gather_rows(got, states):
    hot = jax.ShapeDtypeStruct((SLOTS, CELLS), bf16)
    return pl.pallas_call(
        gather_kernel,
        out_shape=(jax.ShapeDtypeStruct((CAP, LAT, 2 * CH), bf16), hot, hot),
        cost_estimate=pl.CostEstimate(flops=4 * SLOTS * CELLS * CH, bytes_accessed=4000000, transcendentals=0),
    )(got, states)


def departure_kernel(rows_ref, got_ref, out_ref):
    for step in range(2):
        lanes = slice(step * CH, (step + 1) * CH)
        sampled = rows_ref[:, :, lanes].astype(f32)
        members = sampled.shape[0]
        other = got_ref[:, 2 * step + 1, :]
        values = jnp.concatenate([got_ref[:, 2 * step, :], other[:, 0:64]], axis=1)
        ens_mean = jnp.sum(sampled, axis=0) * (1.0 / members)
        ens_var = jnp.sum(sampled * sampled, axis=0) * (1.0 / members) - ens_mean * ens_mean
        weight = 1.0 / (other[:, 64 + CAP : 65 + CAP] + ens_var)
        ratio = (sampled - values[None]) * weight[None]
        live = other[:, 64 + 2 * CAP : 65 + 2 * CAP] >= 0.0
        out_ref[:, :, lanes] = jnp.where(live[None], ratio, 0.0).astype(bf16)


def departures(rows, got):
    return pl.pallas_call(
        departure_kernel,
        out_shape=jax.ShapeDtypeStruct((CAP, LAT, 2 * CH), bf16),
        cost_estimate=pl.CostEstimate(flops=1200000, bytes_accessed=1200000, transcendentals=0),
    )(rows, got)


def forcing_of(step, rows_ref, hot_ref):
    rows = rows_ref[:, :, step * CH : (step + 1) * CH].reshape(SLOTS, CH)
    return lax.dot_general(hot_ref[...], rows, TN, preferred_element_type=f32)


def normalise(hidden):
    centred = hidden - mean_lanes(hidden)
    inv_std = lax.rsqrt(mean_lanes(centred * centred) + norm_eps)
    return centred * inv_std, inv_std


def backward(adjoint, slope_at, down_ref, up_ref, gain, unit, inv_std):
    adj_norm = jnp.zeros((ROWS, CH), f32)
    for part in range(3):
        cols = slice(part * 256, (part + 1) * 256)
        act = lax.dot_general(adjoint, down_ref[cols, :], NT, preferred_element_type=f32)
        pre = (act * slope_at(cols)).astype(bf16)
        adj_norm = adj_norm + lax.dot_general(pre, up_ref[:, cols], NT, preferred_element_type=f32)
    scaled = adj_norm * gain
    return inv_std * (scaled - mean_lanes(scaled) - unit * mean_lanes(scaled * unit))


def put_hidden(adj_hidden, first, out_ref, head_ref, tail_ref):
    block = adj_hidden.astype(bf16).reshape(BLK, WID, CH)
    out_ref[pl.ds(first, BLK)] = block
    head_ref[pl.ds(first, BLK)] = block[:, 0:3]
    tail_ref[pl.ds(first, BLK)] = block[:, WID - 3 : WID]


def forward_kernel(step, state_ref, left_ref, right_ref, kernel_ref, gain_ref, up_ref, bias_ref, *rest):
    shifts, padded, hidden = rest[-3:]
    gain = gain_ref[...]
    build_shifts(
        shifts, padded,
        lambda row: state_ref[step, row],
        lambda row: left_ref[step, row],
        lambda row: right_ref[step, row],
    )

    def block(index, carry):
        first = index * BLK

        def emit(target, low, high, value):
            hidden[target, :, low:high] = value

        convolve(shifts, kernel_ref, first, False, emit)
        unit, inv_std = normalise(hidden[...].reshape(ROWS, CH))
        normed = (unit * gain).astype(bf16)

        def slope_at(cols):
            preact = jnp.dot(normed, up_ref[:, cols], preferred_element_type=f32)
            return gelu_slope(preact + bias_ref[:, cols])

        if step == 0:
            down_ref, adjoint_ref, hidden_out, head_out, tail_out = rest[:5]
            adjoint = adjoint_ref[pl.ds(first, BLK)].reshape(ROWS, CH)
            result = backward(adjoint, slope_at, down_ref, up_ref, gain, unit, inv_std)
            put_hidden(result, first, hidden_out, head_out, tail_out)
        else:
            slope_out, unit_out = rest[:2]
            rows = pl.ds(pl.multiple_of(index * ROWS, ROWS), ROWS)
            for part in range(3):
                cols = slice(part * 256, (part + 1) * 256)
                slope_out[rows, cols] = slope_at(cols).astype(bf16)
            unit_out[rows, 0:CH] = unit
            unit_out[rows, CH:256] = jnp.broadcast_to(inv_std, (ROWS, 256 - CH))
        return carry

    lax.fori_loop(0, LAT // BLK, block, 0)


EDGE = jax.ShapeDtypeStruct((LAT, 3, CH), bf16)
FIELD = jax.ShapeDtypeStruct((LAT, WID, CH), bf16)
SHIFT_SCRATCH = [pltpu.VMEM((7, LAT + 6, WID, CH), f32), pltpu.VMEM((WID + 8, CH), f32)]
BIG = pltpu.CompilerParams(vmem_limit_bytes=24 * 1024 * 1024)


def forward(step, *operands):
    shapes = (FIELD, EDGE, EDGE) if step == 0 else (
        jax.ShapeDtypeStruct((CELLS, HID), bf16),
        jax.ShapeDtypeStruct((CELLS, 256), f32),
    )
    return pl.pallas_call(
        functools.partial(forward_kernel, step),
        out_shape=shapes,
        scratch_shapes=SHIFT_SCRATCH + [pltpu.VMEM((BLK, WID, CH), f32)],
        compiler_params=BIG,
        cost_estimate=pl.CostEstimate(flops=6 * CELLS * CH * HID, bytes_accessed=8000000, transcendentals=CELLS * HID),
    )(*operands)


def spread_kernel(hidden_ref, left_ref, right_ref, base_ref, kernel_ref, out_ref, shifts, padded):
    build_shifts(
        shifts, padded,
        lambda row: hidden_ref[row],
        lambda row: left_ref[row],
        lambda row: right_ref[row],
    )

    def block(index, carry):
        first = index * BLK

        def emit(target, low, high, value):
            base = base_ref[first + target, :, low:high].astype(f32)
            out_ref[first + target, :, low:high] = (base + value).astype(out_ref.dtype)

        convolve(shifts, kernel_ref, first, True, emit)
        return carry

    lax.fori_loop(0, LAT // BLK, block, 0)


def spread_back(hidden, left, right, base, kernel, dtype):
    return pl.pallas_call(
        spread_kernel,
        out_shape=jax.ShapeDtypeStruct((LAT, WID, CH), dtype),
        scratch_shapes=SHIFT_SCRATCH,
        compiler_params=BIG,
        cost_estimate=pl.CostEstimate(flops=98 * CELLS * CH, bytes_accessed=3000000, transcendentals=0),
    )(hidden, left, right, base, kernel)


def second_kernel(
    partial_ref, rows_ref, hot_ref, slope_ref, unit_ref, gain_ref, up_ref, down_ref,
    hidden_out, head_out, tail_out, adjoint_out,
):
    gain = gain_ref[...]
    forcing = forcing_of(0, rows_ref, hot_ref)
    adjoint_all = (partial_ref[...].reshape(CELLS, CH) + forcing).astype(bf16)
    adjoint_out[...] = adjoint_all.reshape(LAT, WID, CH)

    def block(index, carry):
        first = index * BLK
        rows = pl.ds(pl.multiple_of(index * ROWS, ROWS), ROWS)
        adjoint = adjoint_out[pl.ds(first, BLK)].reshape(ROWS, CH)
        result = backward(
            adjoint,
            lambda cols: slope_ref[rows, cols].astype(f32),
            down_ref, up_ref, gain,
            unit_ref[rows, 0:CH], unit_ref[rows, CH : CH + 1],
        )
        put_hidden(result, first, hidden_out, head_out, tail_out)
        return carry

    lax.fori_loop(0, LAT // BLK, block, 0)


def second_step(partial, rows, hot, slope, unit, gain, up, down):
    return pl.pallas_call(
        second_kernel,
        out_shape=(FIELD, EDGE, EDGE, FIELD),
        compiler_params=BIG,
        cost_estimate=pl.CostEstimate(flops=4 * CELLS * CH * HID, bytes_accessed=5000000, transcendentals=0),
    )(partial, rows, hot, slope, unit, gain, up, down)


def base_kernel(adjoint_ref, rows_ref, hot_ref, out_ref):
    forcing = forcing_of(1, rows_ref, hot_ref)
    out_ref[...] = adjoint_ref[...].astype(f32) + forcing.reshape(LAT, WID, CH)


def last_base(adjoint, rows, hot):
    return pl.pallas_call(
        base_kernel,
        out_shape=jax.ShapeDtypeStruct((LAT, WID, CH), f32),
        compiler_params=BIG,
        cost_estimate=pl.CostEstimate(flops=2 * SLOTS * CELLS * CH, bytes_accessed=1500000, transcendentals=0),
    )(adjoint, rows, hot)


def swap_edges(head, tail):
    peers = lax.axis_size("tile")
    up = [(i, (i + 1) % peers) for i in range(peers)]
    down = [(j, i) for i, j in up]
    return lax.ppermute(tail, "tile", up), lax.ppermute(head, "tile", down)


def after(array, other):
    return lax.optimization_barrier((array, other))[0]


def exchange(array, axis):
    return lax.all_to_all(array, axis, split_axis=0, concat_axis=0, tiled=True)


def per_device(
    adjoint_final, states, kernel, norm_gain, up_weight, up_bias, down_weight,
    obs_cell, obs_count, obs_value, obs_error,
):
    adjoint = adjoint_final[0]
    states = states[:, 0]
    taps = kernel.reshape(49, CH)
    gain = norm_gain[None]
    bias = up_bias[None]

    packed = pack_observations(obs_cell[:, 0], obs_count[:, 0], obs_value[:, 0], obs_error[:, 0])
    got = exchange(packed, "tile")
    left, right = swap_edges(*cut_edges(after(states, packed)))

    rows, hot0, hot1 = gather_rows(got, states)
    owned = exchange(rows, "member")

    hidden, head, tail = forward(
        0, states, left, after(right, rows), taps, gain, up_weight, bias, down_weight, adjoint
    )
    before, behind = swap_edges(head, tail)

    deps = departures(after(owned, hidden), got)
    back = exchange(deps, "member")

    slope, unit = forward(1, states, left, after(right, deps), taps, gain, up_weight, bias)
    partial = spread_back(hidden, before, after(behind, deps), adjoint, taps, f32)

    hidden, head, tail, adjoint = second_step(
        partial, after(back, (slope, partial)), hot0, slope, unit, gain, up_weight, down_weight
    )
    base = last_base(adjoint, back, hot1)
    return spread_back(hidden, *swap_edges(head, tail), base, taps, bf16)[None]


def solution(mesh):
    placed = (
        P("member", None, "tile", None),
        P(None, "member", None, "tile", None),
        P(),
        P(),
        P(),
        P(),
        P(),
        P(None, "tile", None, None),
        P(None, "tile", None),
        P(None, "tile", None, None, None),
        P(None, "tile", None, None),
    )
    return jax.shard_map(
        per_device,
        mesh=mesh,
        in_specs=placed,
        out_specs=P("member", None, "tile", None),
        check_vma=False,
    )
```

```python
import functools
import math

import jax
import jax.numpy as jnp
from jax import lax
from jax.experimental import pallas as pl
from jax.experimental.pallas import tpu as pltpu
from jax.sharding import PartitionSpec as P

slope_coef = math.sqrt(2.0 / math.pi)
cubic_coef = 0.044715
norm_eps = 1e-06

LAT = 32
WID = 32
CH = 192
HID = 768
CAP = 16
CELLS = LAT * WID
SLOTS = LAT * CAP
BLK = 8
ROWS = BLK * WID
f32 = jnp.float32
bf16 = jnp.bfloat16
NT = (((1,), (1,)), ((), ()))
TN = (((0,), (0,)), ((), ()))


def gelu_slope(preact):
    square = preact * preact
    tanh_val = jnp.tanh(preact * (slope_coef + (slope_coef * cubic_coef) * square))
    tail = preact * (0.5 * slope_coef + (1.5 * slope_coef * cubic_coef) * square)
    return (0.5 + 0.5 * tanh_val) + tail * (1.0 - tanh_val * tanh_val)


def mean_lanes(value):
    return jnp.sum(value, axis=-1, keepdims=True) * (1.0 / CH)


def clear_rims(shifts, count, width):
    for edge in range(3):
        zeros = jnp.zeros((width, CH), f32)
        for col in range(count):
            shifts[col, edge] = zeros
            shifts[col, LAT + 3 + edge] = zeros


def build_shifts(shifts, padded, centre, left=None, right=None):
    clear_rims(shifts, 7, WID)
    if left is None:
        padded[...] = jnp.zeros(padded.shape, f32)

    def one_row(row, carry):
        if left is not None:
            padded[0:3] = left(row).astype(f32)
            padded[WID + 3 : WID + 6] = right(row).astype(f32)
        padded[3 : WID + 3] = centre(row).astype(f32)
        for col in range(7):
            shifts[col, row + 3] = padded[col : col + WID]
        return carry

    lax.fori_loop(0, LAT, one_row, 0)


def convolve(shifts, kernel_ref, first, flip, emit, cols=range(7), width=WID):
    for low, high in ((0, 128), (128, CH)):
        sums = [None] * BLK
        for place, col in enumerate(cols):
            taps = []
            for row in range(7):
                down, across = (6 - row, 6 - col) if flip else (row, col)
                taps.append(jnp.broadcast_to(kernel_ref[down, across : across + 1, low:high], (width, high - low)))
            for source in range(BLK + 6):
                field = shifts[place, first + source, :, low:high]
                for row in range(7):
                    target = source - row
                    if 0 <= target < BLK:
                        term = taps[row] * field
                        sums[target] = term if sums[target] is None else sums[target] + term
        for target in range(BLK):
            emit(target, low, high, sums[target])


def cut_kernel(first_ref, last_ref, head_ref, tail_ref):
    head_ref[...] = first_ref[:, 0, :, 0:3]
    tail_ref[...] = last_ref[:, 0, :, 5:8]


def cut_edges(states):
    edge = jax.ShapeDtypeStruct((2, LAT, 3, CH), bf16)
    whole = pl.BlockSpec((2, LAT, 3, CH), lambda i: (0, 0, 0, 0))
    part = lambda block: pl.BlockSpec((2, 1, LAT, 8, CH), lambda i: (0, 0, 0, block, 0))
    return pl.pallas_call(
        cut_kernel, grid=(1,), in_specs=[part(0), part(3)], out_specs=[whole, whole], out_shape=(edge, edge)
    )(states, states)


def pack_kernel(cell_ref, count_ref, value_ref, error_ref, out_ref):
    member = lax.axis_index("member")
    tiles = cell_ref.shape[2]
    slot = lax.broadcasted_iota(jnp.int32, (CAP, tiles), 0)
    across = lax.broadcasted_iota(jnp.int32, (CAP, CAP), 1)
    same = jnp.where(lax.broadcasted_iota(jnp.int32, (CAP, CAP), 0) == across, 1.0, 0.0).astype(bf16)
    own = jnp.where(lax.broadcasted_iota(jnp.int32, (CAP, CAP), 0) == member, 1.0, 0.0).astype(bf16)
    deep = lax.broadcasted_iota(jnp.int32, (tiles, CAP, CH), 1)
    for step in range(2):
        live = slot < count_ref[step]
        cells = jnp.where(live, cell_ref[step], -1).astype(f32).astype(bf16)
        values = jnp.sum(jnp.where(deep == member, value_ref[step, 0].astype(f32), 0.0), axis=1)
        turn = lambda array, pick: lax.dot_general(array, pick, TN, preferred_element_type=f32)
        out_ref[:, 2 * step, :] = values[:, 0:128]
        out_ref[:, 2 * step + 1, :] = jnp.concatenate(
            [values[:, 128:CH], turn(cells, same), turn(error_ref[step], own), turn(cells, own), jnp.zeros((tiles, CAP), f32)],
            axis=1)


def pack_observations(cells, counts, values, errors):
    return pl.pallas_call(
        pack_kernel,
        out_shape=jax.ShapeDtypeStruct((cells.shape[2], 4, 128), f32),
    )(cells, counts, values, errors)


def one_hot(step, got_ref, group):
    cells = got_ref[group * BLK : (group + 1) * BLK, 2 * step + 1, 64 : 64 + CAP]
    lane = lax.broadcasted_iota(jnp.int32, (BLK, ROWS), 1)
    band = lax.broadcasted_iota(jnp.int32, (BLK, ROWS), 0)
    offset = (lane - band * WID).astype(f32)
    rows = [jnp.where(offset == cells[:, slot : slot + 1], 1.0, 0.0) for slot in range(CAP)]
    return jnp.concatenate(rows, axis=0).astype(bf16)


def gather_kernel(got_ref, state_ref, out_ref):
    for step in range(2):
        for pair in range(2):
            found = []
            for group in (2 * pair, 2 * pair + 1):
                field = state_ref[step, 0, group * BLK : (group + 1) * BLK].reshape(ROWS, CH)
                rows = jnp.dot(one_hot(step, got_ref, group), field, preferred_element_type=f32)
                found.append(rows.reshape(CAP, BLK, CH))
            both = jnp.concatenate(found, axis=1).astype(bf16)
            out_ref[:, 2 * BLK * pair : 2 * BLK * (pair + 1), step * CH : (step + 1) * CH] = both


def gather_rows(got, states):
    return pl.pallas_call(
        gather_kernel,
        out_shape=jax.ShapeDtypeStruct((CAP, LAT, 2 * CH), bf16),
        cost_estimate=pl.CostEstimate(flops=1000000, bytes_accessed=2000000, transcendentals=0),
    )(got, states)


def departure_kernel(rows_ref, got_ref, out_ref):
    for step in range(2):
        lanes = slice(step * CH, (step + 1) * CH)
        sampled = rows_ref[:, :, lanes].astype(f32)
        members = sampled.shape[0]
        other = got_ref[:, 2 * step + 1, :]
        values = jnp.concatenate([got_ref[:, 2 * step, :], other[:, 0:64]], axis=1)
        ens_mean = jnp.sum(sampled, axis=0) * (1.0 / members)
        ens_var = jnp.sum(sampled * sampled, axis=0) * (1.0 / members) - ens_mean * ens_mean
        weight = 1.0 / (other[:, 64 + CAP : 65 + CAP] + ens_var)
        ratio = (sampled - values[None]) * weight[None]
        live = other[:, 64 + 2 * CAP : 65 + 2 * CAP] >= 0.0
        out_ref[:, :, lanes] = jnp.where(live[None], ratio, 0.0).astype(bf16)


def departures(rows, got):
    return pl.pallas_call(
        departure_kernel,
        out_shape=jax.ShapeDtypeStruct((CAP, LAT, 2 * CH), bf16),
        cost_estimate=pl.CostEstimate(flops=1200000, bytes_accessed=1200000, transcendentals=0),
    )(rows, got)


def forcing_of(step, rows_ref, got_ref, group):
    rows = rows_ref[:, :, step * CH : (step + 1) * CH].astype(f32)[:, group * BLK : (group + 1) * BLK]
    rows = rows.reshape(CAP * BLK, CH).astype(bf16)
    return lax.dot_general(one_hot(step, got_ref, group), rows, TN, preferred_element_type=f32)


def normalise(hidden):
    centred = hidden - mean_lanes(hidden)
    inv_std = lax.rsqrt(mean_lanes(centred * centred) + norm_eps)
    return centred * inv_std, inv_std


def backward(adjoint, slope_at, down_ref, up_ref, gain, unit):
    adj_norm = jnp.zeros((ROWS, CH), f32)
    for part in range(3):
        cols = slice(part * 256, (part + 1) * 256)
        act = jnp.dot(adjoint, down_ref[:, cols], preferred_element_type=f32)
        pre = (act * slope_at(cols)).astype(bf16)
        adj_norm = adj_norm + lax.dot_general(pre, up_ref[:, cols], NT, preferred_element_type=f32)
    scaled = adj_norm * gain
    return scaled - mean_lanes(scaled) - unit * mean_lanes(scaled * unit)


def put_hidden(adj_hidden, first, out_ref, head_ref, tail_ref):
    block = adj_hidden.astype(bf16).reshape(BLK, WID, CH)
    out_ref[pl.ds(first, BLK)] = block
    head_ref[pl.ds(first, BLK)] = block[:, 0:3]
    tail_ref[pl.ds(first, BLK)] = block[:, WID - 3 : WID]


def forward_kernel(step, state_ref, left_ref, right_ref, kernel_ref, gain_ref, up_ref, bias_ref, *rest):
    shifts, padded, hidden = rest[-3:]
    gain = gain_ref[...]
    build_shifts(
        shifts, padded,
        lambda row: state_ref[step, 0, row],
        lambda row: left_ref[step, row],
        lambda row: right_ref[step, row],
    )

    def block(index, carry):
        first = index * BLK

        def emit(target, low, high, value):
            hidden[target, :, low:high] = value

        convolve(shifts, kernel_ref, first, False, emit)
        unit, inv_std = normalise(hidden[...].reshape(ROWS, CH))
        normed = (unit * gain).astype(bf16)

        def slope_at(cols):
            preact = jnp.dot(normed, up_ref[:, cols], preferred_element_type=f32)
            return gelu_slope(preact + bias_ref[:, cols]) * inv_std

        if step == 0:
            down_ref, adjoint_ref, hidden_out, head_out, tail_out = rest[:5]
            adjoint = adjoint_ref[0, pl.ds(first, BLK)].reshape(ROWS, CH)
            result = backward(adjoint, slope_at, down_ref, up_ref, gain, unit)
            put_hidden(result, first, hidden_out, head_out, tail_out)
        else:
            slope_out, unit_out = rest[:2]
            rows = pl.ds(pl.multiple_of(index * ROWS, ROWS), ROWS)
            for part in range(3):
                cols = slice(part * 256, (part + 1) * 256)
                slope_out[rows, cols] = slope_at(cols).astype(bf16)
            unit_out[rows, :] = unit.astype(bf16)
        return carry

    lax.fori_loop(0, LAT // BLK, block, 0)


EDGE = jax.ShapeDtypeStruct((LAT, 3, CH), bf16)
FIELD = jax.ShapeDtypeStruct((LAT, WID, CH), bf16)
SHIFT_SCRATCH = [pltpu.VMEM((7, LAT + 6, WID, CH), f32), pltpu.VMEM((WID + 8, CH), f32)]
BIG = pltpu.CompilerParams(vmem_limit_bytes=16 * 1024 * 1024)


def forward(step, *operands):
    shapes = (FIELD, EDGE, EDGE) if step == 0 else (
        jax.ShapeDtypeStruct((CELLS, HID), bf16),
        jax.ShapeDtypeStruct((CELLS, CH), bf16),
    )
    return pl.pallas_call(
        functools.partial(forward_kernel, step),
        out_shape=shapes,
        scratch_shapes=SHIFT_SCRATCH + [pltpu.VMEM((BLK, WID, CH), f32)],
        compiler_params=BIG,
        cost_estimate=pl.CostEstimate(flops=6 * CELLS * CH * HID, bytes_accessed=8000000, transcendentals=CELLS * HID),
    )(*operands)


def spread_kernel(hidden_ref, left_ref, right_ref, base_ref, kernel_ref, out_ref, shifts, padded):
    build_shifts(
        shifts, padded,
        lambda row: hidden_ref[row],
        lambda row: left_ref[row],
        lambda row: right_ref[row],
    )

    def block(index, carry):
        first = index * BLK

        def emit(target, low, high, value):
            base = base_ref[0, first + target, :, low:high].astype(f32)
            out_ref[first + target, :, low:high] = base + value

        convolve(shifts, kernel_ref, first, True, emit)
        return carry

    lax.fori_loop(0, LAT // BLK, block, 0)


def spread_back(hidden, left, right, base, kernel):
    return pl.pallas_call(
        spread_kernel,
        out_shape=jax.ShapeDtypeStruct((LAT, WID, CH), f32),
        scratch_shapes=SHIFT_SCRATCH,
        compiler_params=BIG,
        cost_estimate=pl.CostEstimate(flops=98 * CELLS * CH, bytes_accessed=3000000, transcendentals=0),
    )(hidden, left, right, base, kernel)


def second_kernel(
    partial_ref, rows_ref, got_ref, slope_ref, unit_ref, gain_ref, up_ref, down_ref,
    hidden_out, head_out, tail_out, adjoint_out,
):
    gain = gain_ref[...]
    for group in range(LAT // BLK):
        first = group * BLK
        rows = slice(group * ROWS, (group + 1) * ROWS)
        forcing = forcing_of(0, rows_ref, got_ref, group)
        adjoint = (partial_ref[first : first + BLK].reshape(ROWS, CH) + forcing).astype(bf16)
        adjoint_out[first : first + BLK] = adjoint.reshape(BLK, WID, CH)
        result = backward(
            adjoint,
            lambda cols: slope_ref[rows, cols].astype(f32),
            down_ref, up_ref, gain,
            unit_ref[rows, :].astype(f32),
        )
        put_hidden(result, first, hidden_out, head_out, tail_out)


def second_step(partial, rows, got, slope, unit, gain, up, down):
    return pl.pallas_call(
        second_kernel,
        out_shape=(FIELD, EDGE, EDGE, FIELD),
        compiler_params=pltpu.CompilerParams(vmem_limit_bytes=12 * 1024 * 1024),
        cost_estimate=pl.CostEstimate(flops=4 * CELLS * CH * HID, bytes_accessed=5000000, transcendentals=0),
    )(partial, rows, got, slope, unit, gain, up, down)


def interior_kernel(hidden_ref, adjoint_ref, rows_ref, got_ref, kernel_ref, out_ref, west_ref, east_ref, shifts, padded, total):
    build_shifts(shifts, padded, lambda row: hidden_ref[row])
    for group in range(LAT // BLK):
        first = group * BLK
        forcing = forcing_of(1, rows_ref, got_ref, group).reshape(BLK, WID, CH)
        total[first : first + BLK] = adjoint_ref[first : first + BLK].astype(f32) + forcing

    def block(index, carry):
        first = index * BLK

        def emit(target, low, high, value):
            value = total[first + target, :, low:high] + value
            out_ref[first + target, :, low:high] = value.astype(bf16)
            west_ref[first + target, :, low:high] = value[0:8]
            east_ref[first + target, :, low:high] = value[WID - 8 : WID]

        convolve(shifts, kernel_ref, first, True, emit)
        return carry

    lax.fori_loop(0, LAT // BLK, block, 0)


STRIP = jax.ShapeDtypeStruct((LAT, 8, CH), f32)


def interior(hidden, adjoint, rows, got, kernel):
    return pl.pallas_call(
        interior_kernel,
        out_shape=(FIELD, STRIP, STRIP),
        scratch_shapes=SHIFT_SCRATCH + [pltpu.VMEM((LAT, WID, CH), f32)],
        compiler_params=BIG,
        cost_estimate=pl.CostEstimate(flops=98 * CELLS * CH, bytes_accessed=3000000, transcendentals=0),
    )(hidden, adjoint, rows, got, kernel)


def edge_kernel(inner_ref, west_ref, east_ref, left_ref, right_ref, kernel_ref, out_ref, shifts, padded):
    def side(halo_ref, strip_ref, place, offset, cols):
        clear_rims(shifts, 3, 8)
        padded[...] = jnp.zeros(padded.shape, f32)

        def one_row(row, carry):
            padded[place : place + 3] = halo_ref[row].astype(f32)
            for col in range(3):
                shifts[col, row + 3] = padded[col + offset : col + offset + 8]
            return carry

        lax.fori_loop(0, LAT, one_row, 0)

        def block(index, carry):
            first = index * BLK

            def emit(target, low, high, value):
                out_ref[first + target, :, low:high] = (strip_ref[first + target, :, low:high] + value).astype(bf16)

            convolve(shifts, kernel_ref, first, True, emit, cols, 8)
            return carry

        lax.fori_loop(0, LAT // BLK, block, 0)

    @pl.when(pl.program_id(0) == 0)
    def _():
        side(left_ref, west_ref, 0, 0, range(0, 3))

    @pl.when(pl.program_id(0) == 1)
    def _():
        side(right_ref, east_ref, 8, 1, range(4, 7))


def finish_edges(inner, west, east, left, right, kernel):
    whole = lambda array: pl.BlockSpec(array.shape, lambda i: (0,) * array.ndim)
    return pl.pallas_call(
        edge_kernel,
        grid=(2,),
        in_specs=[pl.BlockSpec(memory_space=pl.ANY)] + [whole(x) for x in (west, east, left, right, kernel)],
        out_specs=pl.BlockSpec((LAT, 8, CH), lambda i: (0, 3 * i, 0)),
        out_shape=FIELD,
        input_output_aliases={0: 0},
        scratch_shapes=[pltpu.VMEM((3, LAT + 6, 8, CH), f32), pltpu.VMEM((16, CH), f32)],
        cost_estimate=pl.CostEstimate(flops=5000000, bytes_accessed=700000, transcendentals=0),
    )(inner, west, east, left, right, kernel)


def swap_edges(head, tail):
    peers = lax.axis_size("tile")
    up = [(i, (i + 1) % peers) for i in range(peers)]
    down = [(j, i) for i, j in up]
    return lax.ppermute(tail, "tile", up), lax.ppermute(head, "tile", down)


def after(array, other):
    return lax.optimization_barrier((array, other))[0]


def exchange(array, axis):
    return lax.all_to_all(array, axis, split_axis=0, concat_axis=0, tiled=True)


def per_device(
    adjoint_final, states, kernel, norm_gain, up_weight, up_bias, down_weight,
    obs_cell, obs_count, obs_value, obs_error,
):
    gain = norm_gain[None]
    bias = up_bias[None]
    down = down_weight.T

    packed = pack_observations(
        obs_cell[:, 0].transpose(0, 2, 1), obs_count, obs_value, obs_error[:, 0].transpose(0, 2, 1)
    )
    got = exchange(packed, "tile")
    head, tail = cut_edges(after(states, packed))
    left, right = swap_edges(head, tail)

    rows = gather_rows(after(got, head), states)
    owned = exchange(rows, "member")

    hidden, head, tail = forward(
        0, states, left, after(right, rows), kernel, gain, up_weight, bias, down, adjoint_final
    )
    before, behind = swap_edges(head, tail)

    deps = departures(after(owned, hidden), got)
    back = exchange(deps, "member")

    slope, unit = forward(1, states, left, after(right, deps), kernel, gain, up_weight, bias)
    partial = spread_back(hidden, before, after(behind, slope), adjoint_final, kernel)

    hidden, head, tail, adjoint = second_step(
        partial, after(back, partial), got, slope, unit, gain, up_weight, down
    )
    left, right = swap_edges(head, tail)
    inner, west, east = interior(hidden, adjoint, back, got, kernel)
    return finish_edges(inner, west, east, left, right, kernel)[None]


def solution(mesh):
    placed = (
        P("member", None, "tile", None),
        P(None, "member", None, "tile", None),
        P(),
        P(),
        P(),
        P(),
        P(),
        P(None, "tile", None, None),
        P(None, "tile", None),
        P(None, "tile", None, None, None),
        P(None, "tile", None, None),
    )
    return jax.shard_map(
        per_device,
        mesh=mesh,
        in_specs=placed,
        out_specs=P("member", None, "tile", None),
        check_vma=False,
    )
```

```python
import functools
import math

import jax
import jax.numpy as jnp
from jax import lax
from jax.experimental import pallas as pl
from jax.experimental.pallas import tpu as pltpu
from jax.sharding import PartitionSpec as P

slope_coef = math.sqrt(2.0 / math.pi)
cubic_coef = 0.044715
norm_eps = 1e-06

LAT = 32
WID = 32
CH = 192
HID = 768
CAP = 16
CELLS = LAT * WID
SLOTS = LAT * CAP
BLK = 8
ROWS = BLK * WID
UNROLL = 4
f32 = jnp.float32
bf16 = jnp.bfloat16
NT = (((1,), (1,)), ((), ()))
TN = (((0,), (0,)), ((), ()))


def gelu_slope(preact):
    square = preact * preact
    tanh_val = jnp.tanh(preact * (slope_coef + (slope_coef * cubic_coef) * square))
    tail = preact * (0.5 * slope_coef + (1.5 * slope_coef * cubic_coef) * square)
    return (0.5 + 0.5 * tanh_val) + tail * (1.0 - tanh_val * tanh_val)


def limit(mebibytes):
    return pltpu.CompilerParams(vmem_limit_bytes=mebibytes * 1024 * 1024)


def mean_lanes(value):
    return jnp.sum(value, axis=-1, keepdims=True) * (1.0 / CH)


HBM = pl.BlockSpec(memory_space=pltpu.HBM)
VM = pl.BlockSpec(memory_space=pltpu.VMEM)


def fetch(pairs, sems):
    copies = [pltpu.make_async_copy(src, dst, sems.at[i]) for i, (src, dst) in enumerate(pairs)]
    for copy in copies:
        copy.start()
    return copies


def clear_rims(shifts, count, width):
    for edge in range(3):
        zeros = jnp.zeros((width, CH), f32)
        for col in range(count):
            shifts[col, edge] = zeros
            shifts[col, LAT + 3 + edge] = zeros


def build_shifts(shifts, padded, centre, left=None, right=None):
    clear_rims(shifts, 7, WID)
    if left is None:
        padded[...] = jnp.zeros(padded.shape, f32)

    def some_rows(index, carry):
        for lane in range(UNROLL):
            row = index * UNROLL + lane
            if left is not None:
                padded[lane, 0:3] = left(row).astype(f32)
                padded[lane, WID + 3 : WID + 6] = right(row).astype(f32)
            padded[lane, 3 : WID + 3] = centre(row).astype(f32)
        for lane in range(UNROLL):
            row = index * UNROLL + lane
            for col in range(7):
                shifts[col, row + 3] = padded[lane, col : col + WID]
        return carry

    lax.fori_loop(0, LAT // UNROLL, some_rows, 0)


def convolve(shifts, kernel_ref, first, flip, emit, cols=range(7), width=WID):
    for low, high in ((0, 128), (128, CH)):
        sums = [None] * BLK
        for place, col in enumerate(cols):
            taps = []
            for row in range(7):
                down, across = (6 - row, 6 - col) if flip else (row, col)
                taps.append(jnp.broadcast_to(kernel_ref[down, across : across + 1, low:high], (width, high - low)))
            for source in range(BLK + 6):
                field = shifts[place, first + source, :, low:high]
                for row in range(7):
                    target = source - row
                    if 0 <= target < BLK:
                        term = taps[row] * field
                        sums[target] = term if sums[target] is None else sums[target] + term
        for target in range(BLK):
            emit(target, low, high, sums[target])


def pack_kernel(cell_ref, count_ref, value_ref, error_ref, out_ref):
    member = lax.axis_index("member")
    tiles = cell_ref.shape[2]
    slot = lax.broadcasted_iota(jnp.int32, (CAP, tiles), 0)
    across = lax.broadcasted_iota(jnp.int32, (CAP, CAP), 1)
    same = jnp.where(lax.broadcasted_iota(jnp.int32, (CAP, CAP), 0) == across, 1.0, 0.0).astype(bf16)
    own = jnp.where(lax.broadcasted_iota(jnp.int32, (CAP, CAP), 0) == member, 1.0, 0.0).astype(bf16)
    deep = lax.broadcasted_iota(jnp.int32, (tiles, CAP, CH), 1)
    for step in range(2):
        live = slot < count_ref[step]
        cells = jnp.where(live, cell_ref[step], -1).astype(f32).astype(bf16)
        values = jnp.sum(jnp.where(deep == member, value_ref[step, 0].astype(f32), 0.0), axis=1)
        turn = lambda array, pick: lax.dot_general(array, pick, TN, preferred_element_type=f32)
        out_ref[:, 2 * step, :] = values[:, 0:128]
        out_ref[:, 2 * step + 1, :] = jnp.concatenate(
            [values[:, 128:CH], turn(cells, same), turn(error_ref[step], own), turn(cells, own), jnp.zeros((tiles, CAP), f32)],
            axis=1)


def pack_observations(cells, counts, values, errors):
    return pl.pallas_call(
        pack_kernel,
        out_shape=jax.ShapeDtypeStruct((cells.shape[2], 4, 128), f32),
        compiler_params=limit(6),
    )(cells, counts, values, errors)


def one_hot(step, got_ref, group):
    cells = got_ref[group * BLK : (group + 1) * BLK, 2 * step + 1, 64 : 64 + CAP]
    lane = lax.broadcasted_iota(jnp.int32, (BLK, ROWS), 1)
    band = lax.broadcasted_iota(jnp.int32, (BLK, ROWS), 0)
    offset = (lane - band * WID).astype(f32)
    rows = [jnp.where(offset == cells[:, slot : slot + 1], 1.0, 0.0) for slot in range(CAP)]
    return jnp.concatenate(rows, axis=0).astype(bf16)


def gather_kernel(got_ref, state_ref, out_ref):
    for step in range(2):
        for pair in range(2):
            found = []
            for group in (2 * pair, 2 * pair + 1):
                field = state_ref[step, 0, group * BLK : (group + 1) * BLK].reshape(ROWS, CH)
                rows = jnp.dot(one_hot(step, got_ref, group), field, preferred_element_type=f32)
                found.append(rows.reshape(CAP, BLK, CH))
            both = jnp.concatenate(found, axis=1).astype(bf16)
            out_ref[:, 2 * BLK * pair : 2 * BLK * (pair + 1), step * CH : (step + 1) * CH] = both


def gather_rows(got, states):
    return pl.pallas_call(
        gather_kernel,
        out_shape=jax.ShapeDtypeStruct((CAP, LAT, 2 * CH), bf16),
        compiler_params=limit(6),
        cost_estimate=pl.CostEstimate(flops=1000000, bytes_accessed=2000000, transcendentals=0),
    )(got, states)


def departure_kernel(rows_ref, got_ref, out_ref):
    for step in range(2):
        lanes = slice(step * CH, (step + 1) * CH)
        sampled = rows_ref[:, :, lanes].astype(f32)
        members = sampled.shape[0]
        other = got_ref[:, 2 * step + 1, :]
        values = jnp.concatenate([got_ref[:, 2 * step, :], other[:, 0:64]], axis=1)
        ens_mean = jnp.sum(sampled, axis=0) * (1.0 / members)
        ens_var = jnp.sum(sampled * sampled, axis=0) * (1.0 / members) - ens_mean * ens_mean
        weight = 1.0 / (other[:, 64 + CAP : 65 + CAP] + ens_var)
        ratio = (sampled - values[None]) * weight[None]
        live = other[:, 64 + 2 * CAP : 65 + 2 * CAP] >= 0.0
        out_ref[:, :, lanes] = jnp.where(live[None], ratio, 0.0).astype(bf16)


def departures(rows, got):
    return pl.pallas_call(
        departure_kernel,
        out_shape=jax.ShapeDtypeStruct((CAP, LAT, 2 * CH), bf16),
        compiler_params=limit(6),
        cost_estimate=pl.CostEstimate(flops=1200000, bytes_accessed=1200000, transcendentals=0),
    )(rows, got)


def forcing_of(step, rows_ref, got_ref, group):
    rows = rows_ref[:, :, step * CH : (step + 1) * CH].astype(f32)[:, group * BLK : (group + 1) * BLK]
    rows = rows.reshape(CAP * BLK, CH).astype(bf16)
    return lax.dot_general(one_hot(step, got_ref, group), rows, TN, preferred_element_type=f32)


def normalise(hidden):
    centred = hidden - mean_lanes(hidden)
    inv_std = lax.rsqrt(mean_lanes(centred * centred) + norm_eps)
    return centred * inv_std, inv_std


def backward(adjoint, slope_at, down_ref, up_ref, gain, unit):
    adj_norm = jnp.zeros((ROWS, CH), f32)
    for part in range(3):
        cols = slice(part * 256, (part + 1) * 256)
        act = jnp.dot(adjoint, down_ref[:, cols], preferred_element_type=f32)
        pre = (act * slope_at(cols)).astype(bf16)
        adj_norm = adj_norm + lax.dot_general(pre, up_ref[:, cols], NT, preferred_element_type=f32)
    scaled = adj_norm * gain
    return scaled - mean_lanes(scaled) - unit * mean_lanes(scaled * unit)


def put_hidden(adj_hidden, first, out_ref, tail_ref, head_ref):
    block = adj_hidden.astype(bf16).reshape(BLK, WID, CH)
    out_ref[pl.ds(first, BLK)] = block
    head_ref[pl.ds(first, BLK)] = block[:, 0:3]
    tail_ref[pl.ds(first, BLK)] = block[:, WID - 3 : WID]


def forward_kernel(
    state_ref, right_ref, left_ref, kernel_ref, gain_ref, up_ref, bias_ref, down_ref, adjoint_ref,
    hidden_out, tail_out, head_out, slope_out, unit_out,
    shifts, padded, hidden,
):
    gain = gain_ref[...]
    for step in range(2):
        build_shifts(
            shifts, padded,
            lambda row: state_ref[step, 0, row],
            lambda row: left_ref[step, row],
            lambda row: right_ref[step, row],
        )

        def block(index, carry):
            first = index * BLK

            def emit(target, low, high, value):
                hidden[target, :, low:high] = value

            convolve(shifts, kernel_ref, first, False, emit)
            unit, inv_std = normalise(hidden[...].reshape(ROWS, CH))
            normed = (unit * gain).astype(bf16)

            def slope_at(cols):
                preact = jnp.dot(normed, up_ref[:, cols], preferred_element_type=f32)
                return gelu_slope(preact + bias_ref[:, cols]) * inv_std

            if step == 0:
                adjoint = adjoint_ref[0, pl.ds(first, BLK)].reshape(ROWS, CH)
                result = backward(adjoint, slope_at, down_ref, up_ref, gain, unit)
                put_hidden(result, first, hidden_out, tail_out, head_out)
            else:
                rows = pl.ds(pl.multiple_of(index * ROWS, ROWS), ROWS)
                for part in range(3):
                    cols = slice(part * 256, (part + 1) * 256)
                    slope_out[rows, cols] = slope_at(cols).astype(bf16)
                unit_out[rows, :] = unit.astype(bf16)
            return carry

        lax.fori_loop(0, LAT // BLK, block, 0)


FAR_EDGE = pltpu.HBM((LAT, 3, CH), bf16)
EDGE = jax.ShapeDtypeStruct((LAT, 3, CH), bf16)
FIELD = jax.ShapeDtypeStruct((LAT, WID, CH), bf16)
SHIFT_SCRATCH = [pltpu.VMEM((7, LAT + 6, WID, CH), f32), pltpu.VMEM((UNROLL, WID + 8, CH), f32)]


def forward(*operands):
    return pl.pallas_call(
        forward_kernel,
        out_shape=(
            pltpu.HBM((LAT, WID, CH), bf16), FAR_EDGE, FAR_EDGE,
            pltpu.HBM((CELLS, HID), bf16),
            pltpu.HBM((CELLS, CH), bf16),
        ),
        out_specs=(VM,) * 5,
        scratch_shapes=SHIFT_SCRATCH + [pltpu.VMEM((BLK, WID, CH), f32)],
        compiler_params=limit(18),
        cost_estimate=pl.CostEstimate(flops=12 * CELLS * CH * HID, bytes_accessed=16000000, transcendentals=2 * CELLS * HID),
    )(*operands)


def spread_kernel(hidden_ref, right_ref, left_ref, base_ref, kernel_ref, out_ref, shifts, padded):
    build_shifts(
        shifts, padded,
        lambda row: hidden_ref[row],
        lambda row: left_ref[row],
        lambda row: right_ref[row],
    )

    def block(index, carry):
        first = index * BLK

        def emit(target, low, high, value):
            base = base_ref[0, first + target, :, low:high].astype(f32)
            out_ref[first + target, :, low:high] = base + value

        convolve(shifts, kernel_ref, first, True, emit)
        return carry

    lax.fori_loop(0, LAT // BLK, block, 0)


def spread_back(hidden, right, left, base, kernel):
    return pl.pallas_call(
        spread_kernel,
        out_shape=jax.ShapeDtypeStruct((LAT, WID, CH), f32),
        scratch_shapes=SHIFT_SCRATCH,
        compiler_params=limit(16),
        cost_estimate=pl.CostEstimate(flops=98 * CELLS * CH, bytes_accessed=3000000, transcendentals=0),
    )(hidden, right, left, base, kernel)


def second_kernel(
    partial_ref, rows_ref, got_ref, slope_ref, unit_ref, gain_ref, up_ref, down_ref,
    hidden_out, tail_out, head_out, adjoint_out, slope_buf, unit_buf, down_buf, sems,
):
    parts = [slice(group * ROWS, (group + 1) * ROWS) for group in range(LAT // BLK)]
    pairs = [(down_ref, down_buf), (unit_ref, unit_buf)]
    copies = fetch(pairs + [(slope_ref.at[rows], slope_buf.at[rows]) for rows in parts], sems)
    gain = gain_ref[...]
    for group in range(LAT // BLK):
        first = group * BLK
        rows = slice(group * ROWS, (group + 1) * ROWS)
        forcing = forcing_of(0, rows_ref, got_ref, group)
        adjoint = (partial_ref[first : first + BLK].reshape(ROWS, CH) + forcing).astype(bf16)
        adjoint_out[first : first + BLK] = adjoint.reshape(BLK, WID, CH)
        if group == 0:
            copies[0].wait()
            copies[1].wait()
        copies[2 + group].wait()
        result = backward(
            adjoint,
            lambda cols: slope_buf[rows, cols].astype(f32),
            down_buf, up_ref, gain,
            unit_buf[rows, :].astype(f32),
        )
        put_hidden(result, first, hidden_out, tail_out, head_out)


def far(array):
    return pltpu.with_memory_space_constraint(array, pltpu.HBM)


def second_step(partial, rows, got, slope, unit, gain, up, down):
    return pl.pallas_call(
        second_kernel,
        out_shape=(FIELD, EDGE, EDGE, FIELD),
        in_specs=[VM, VM, VM, HBM, HBM, VM, VM, HBM],
        scratch_shapes=[
            pltpu.VMEM((CELLS, HID), bf16), pltpu.VMEM((CELLS, CH), bf16), pltpu.VMEM((CH, HID), bf16),
            pltpu.SemaphoreType.DMA((6,)),
        ],
        compiler_params=limit(12),
        cost_estimate=pl.CostEstimate(flops=4 * CELLS * CH * HID, bytes_accessed=5000000, transcendentals=0),
    )(partial, rows, got, far(slope), far(unit), gain, up, far(down))


def interior_kernel(hidden_ref, adjoint_ref, rows_ref, got_ref, kernel_ref, out_ref, west_ref, east_ref, shifts, padded, total):
    build_shifts(shifts, padded, lambda row: hidden_ref[row])
    for group in range(LAT // BLK):
        first = group * BLK
        forcing = forcing_of(1, rows_ref, got_ref, group).reshape(BLK, WID, CH)
        total[first : first + BLK] = adjoint_ref[first : first + BLK].astype(f32) + forcing

    def block(index, carry):
        first = index * BLK

        def emit(target, low, high, value):
            value = total[first + target, :, low:high] + value
            out_ref[first + target, :, low:high] = value.astype(bf16)
            west_ref[first + target, :, low:high] = value[0:8]
            east_ref[first + target, :, low:high] = value[WID - 8 : WID]

        convolve(shifts, kernel_ref, first, True, emit)
        return carry

    lax.fori_loop(0, LAT // BLK, block, 0)


STRIP = jax.ShapeDtypeStruct((LAT, 8, CH), f32)


def interior(hidden, adjoint, rows, got, kernel):
    return pl.pallas_call(
        interior_kernel,
        out_shape=(FIELD, STRIP, STRIP),
        scratch_shapes=SHIFT_SCRATCH + [pltpu.VMEM((LAT, WID, CH), f32)],
        compiler_params=limit(16),
        cost_estimate=pl.CostEstimate(flops=98 * CELLS * CH, bytes_accessed=3000000, transcendentals=0),
    )(hidden, adjoint, rows, got, kernel)


def edge_kernel(inner_ref, west_ref, east_ref, right_ref, left_ref, kernel_ref, out_ref, shifts, padded):
    def side(halo_ref, strip_ref, place, offset, cols):
        clear_rims(shifts, 3, 8)
        padded[...] = jnp.zeros(padded.shape, f32)

        def some_rows(index, carry):
            for lane in range(BLK):
                padded[lane, place : place + 3] = halo_ref[index * BLK + lane].astype(f32)
            for lane in range(BLK):
                for col in range(3):
                    shifts[col, index * BLK + lane + 3] = padded[lane, col + offset : col + offset + 8]
            return carry

        lax.fori_loop(0, LAT // BLK, some_rows, 0)

        def block(index, carry):
            first = index * BLK

            def emit(target, low, high, value):
                out_ref[first + target, :, low:high] = (strip_ref[first + target, :, low:high] + value).astype(bf16)

            convolve(shifts, kernel_ref, first, True, emit, cols, 8)
            return carry

        lax.fori_loop(0, LAT // BLK, block, 0)

    @pl.when(pl.program_id(0) == 0)
    def _():
        side(left_ref, west_ref, 0, 0, range(0, 3))

    @pl.when(pl.program_id(0) == 1)
    def _():
        side(right_ref, east_ref, 8, 1, range(4, 7))


def finish_edges(inner, west, east, left, right, kernel):
    whole = lambda array: pl.BlockSpec(array.shape, lambda i: (0,) * array.ndim)
    return pl.pallas_call(
        edge_kernel,
        grid=(2,),
        in_specs=[pl.BlockSpec(memory_space=pl.ANY)] + [whole(x) for x in (west, east, right, left, kernel)],
        out_specs=pl.BlockSpec((LAT, 8, CH), lambda i: (0, 3 * i, 0)),
        out_shape=FIELD,
        input_output_aliases={0: 0},
        compiler_params=limit(4),
        scratch_shapes=[pltpu.VMEM((3, LAT + 6, 8, CH), f32), pltpu.VMEM((BLK, 16, CH), f32)],
        cost_estimate=pl.CostEstimate(flops=5000000, bytes_accessed=700000, transcendentals=0),
    )(inner, west, east, right, left, kernel)


def swap_edges(head, tail):
    peers = lax.axis_size("tile")
    up = [(i, (i + 1) % peers) for i in range(peers)]
    down = [(j, i) for i, j in up]
    right = lax.ppermute(head, "tile", down)
    left = lax.ppermute(tail, "tile", up)
    return left, right


def after(array, other):
    return lax.optimization_barrier((array, other))[0]


def exchange(array, axis):
    return lax.all_to_all(array, axis, split_axis=0, concat_axis=0, tiled=True)


def per_device(
    adjoint_final, states, kernel, norm_gain, up_weight, up_bias, down_weight,
    obs_cell, obs_count, obs_value, obs_error,
):
    gain = norm_gain[None]
    bias = up_bias[None]
    down = down_weight.T

    packed = pack_observations(
        obs_cell[:, 0].transpose(0, 2, 1), obs_count, obs_value, obs_error[:, 0].transpose(0, 2, 1)
    )
    got = exchange(packed, "tile")
    left, right = swap_edges(states[:, 0, :, 0:3], states[:, 0, :, WID - 3 : WID])

    rows = gather_rows(got, states)
    owned = exchange(after(rows, (right, left)), "member")

    hidden, tail, head, slope, unit = forward(
        states, after(right, rows), left, kernel, gain, up_weight, bias, down, adjoint_final
    )
    before, behind = swap_edges(head, tail)

    deps = departures(after(owned, slope), got)
    back = exchange(deps, "member")
    partial = spread_back(hidden, after(behind, deps), before, adjoint_final, kernel)

    hidden, tail, head, adjoint = second_step(
        partial, after(back, partial), got, slope, unit, gain, up_weight, down
    )
    left, right = swap_edges(head, tail)
    inner, west, east = interior(hidden, adjoint, back, got, kernel)
    return finish_edges(inner, west, east, left, right, kernel)[None]


def solution(mesh):
    placed = (
        P("member", None, "tile", None),
        P(None, "member", None, "tile", None),
        P(),
        P(),
        P(),
        P(),
        P(),
        P(None, "tile", None, None),
        P(None, "tile", None),
        P(None, "tile", None, None, None),
        P(None, "tile", None, None),
    )
    return jax.shard_map(
        per_device,
        mesh=mesh,
        in_specs=placed,
        out_specs=P("member", None, "tile", None),
        check_vma=False,
    )
```

```python
import functools
import math

import jax
import jax.numpy as jnp
from jax import lax
from jax.experimental import pallas as pl
from jax.experimental.pallas import tpu as pltpu
from jax.sharding import PartitionSpec as P

slope_coef = math.sqrt(2.0 / math.pi)
cubic_coef = 0.044715
norm_eps = 1e-06

LAT = 32
WID = 32
CH = 192
HID = 768
CAP = 16
CELLS = LAT * WID
SLOTS = LAT * CAP
BLK = 8
ROWS = BLK * WID
UNROLL = 4
f32 = jnp.float32
bf16 = jnp.bfloat16
NT = (((1,), (1,)), ((), ()))
TN = (((0,), (0,)), ((), ()))


def gelu_slope(preact):
    square = preact * preact
    tanh_val = jnp.tanh(preact * (slope_coef + (slope_coef * cubic_coef) * square))
    tail = preact * (0.5 * slope_coef + (1.5 * slope_coef * cubic_coef) * square)
    return (0.5 + 0.5 * tanh_val) + tail * (1.0 - tanh_val * tanh_val)


def limit(mebibytes):
    return pltpu.CompilerParams(vmem_limit_bytes=mebibytes * 1024 * 1024)


def mean_lanes(value):
    return jnp.sum(value, axis=-1, keepdims=True) * (1.0 / CH)


HBM = pl.BlockSpec(memory_space=pltpu.HBM)
VM = pl.BlockSpec(memory_space=pltpu.VMEM)


def fetch(pairs, sems):
    copies = [pltpu.make_async_copy(src, dst, sems.at[i]) for i, (src, dst) in enumerate(pairs)]
    for copy in copies:
        copy.start()
    return copies


def far(array):
    return pltpu.with_memory_space_constraint(array, pltpu.HBM)


def clear_rims(shifts, count, width):
    for edge in range(3):
        zeros = jnp.zeros((width, CH), f32)
        for col in range(count):
            shifts[col, edge] = zeros
            shifts[col, LAT + 3 + edge] = zeros


def build_shifts(shifts, padded, centre, left=None, right=None):
    clear_rims(shifts, 7, WID)
    if left is None:
        padded[...] = jnp.zeros(padded.shape, f32)

    def some_rows(index, carry):
        for lane in range(UNROLL):
            row = index * UNROLL + lane
            if left is not None:
                padded[lane, 0:3] = left(row).astype(f32)
                padded[lane, WID + 3 : WID + 6] = right(row).astype(f32)
            padded[lane, 3 : WID + 3] = centre(row).astype(f32)
        for lane in range(UNROLL):
            row = index * UNROLL + lane
            for col in range(7):
                shifts[col, row + 3] = padded[lane, col : col + WID]
        return carry

    lax.fori_loop(0, LAT // UNROLL, some_rows, 0)


def convolve(shifts, kernel_ref, first, flip, emit, cols=range(7), width=WID):
    for low, high in ((0, 128), (128, CH)):
        sums = [None] * BLK
        for place, col in enumerate(cols):
            taps = []
            for row in range(7):
                down, across = (6 - row, 6 - col) if flip else (row, col)
                taps.append(jnp.broadcast_to(kernel_ref[down, across : across + 1, low:high], (width, high - low)))
            for source in range(BLK + 6):
                field = shifts[place, first + source, :, low:high]
                for row in range(7):
                    target = source - row
                    if 0 <= target < BLK:
                        term = taps[row] * field
                        sums[target] = term if sums[target] is None else sums[target] + term
        for target in range(BLK):
            emit(target, low, high, sums[target])


def pack_kernel(cell_far, count_far, value_far, error_far, out_ref, cell_ref, count_ref, value_ref, error_ref, sems):
    pairs = [(cell_far, cell_ref), (count_far, count_ref), (value_far, value_ref), (error_far, error_ref)]
    for copy in fetch(pairs, sems):
        copy.wait()
    member = lax.axis_index("member")
    tiles = cell_ref.shape[2]
    slot = lax.broadcasted_iota(jnp.int32, (CAP, tiles), 0)
    across = lax.broadcasted_iota(jnp.int32, (CAP, CAP), 1)
    same = jnp.where(lax.broadcasted_iota(jnp.int32, (CAP, CAP), 0) == across, 1.0, 0.0).astype(bf16)
    own = jnp.where(lax.broadcasted_iota(jnp.int32, (CAP, CAP), 0) == member, 1.0, 0.0).astype(bf16)
    deep = lax.broadcasted_iota(jnp.int32, (tiles, CAP, CH), 1)
    for step in range(2):
        live = slot < count_ref[step]
        cells = jnp.where(live, cell_ref[step], -1).astype(f32).astype(bf16)
        values = jnp.sum(jnp.where(deep == member, value_ref[step, 0].astype(f32), 0.0), axis=1)
        turn = lambda array, pick: lax.dot_general(array, pick, TN, preferred_element_type=f32)
        out_ref[:, 2 * step, :] = values[:, 0:128]
        out_ref[:, 2 * step + 1, :] = jnp.concatenate(
            [values[:, 128:CH], turn(cells, same), turn(error_ref[step], own), turn(cells, own), jnp.zeros((tiles, CAP), f32)],
            axis=1)


def pack_observations(cells, counts, values, errors):
    return pl.pallas_call(
        pack_kernel,
        out_shape=pltpu.HBM((cells.shape[2], 4, 128), f32),
        in_specs=[HBM] * 4,
        out_specs=VM,
        scratch_shapes=[pltpu.VMEM(array.shape, array.dtype) for array in (cells, counts, values, errors)]
        + [pltpu.SemaphoreType.DMA((4,))],
        compiler_params=limit(6),
    )(far(cells), far(counts), far(values), far(errors))


def one_hot(step, got_ref, group):
    cells = got_ref[group * BLK : (group + 1) * BLK, 2 * step + 1, 64 : 64 + CAP]
    lane = lax.broadcasted_iota(jnp.int32, (BLK, ROWS), 1)
    band = lax.broadcasted_iota(jnp.int32, (BLK, ROWS), 0)
    offset = (lane - band * WID).astype(f32)
    rows = [jnp.where(offset == cells[:, slot : slot + 1], 1.0, 0.0) for slot in range(CAP)]
    return jnp.concatenate(rows, axis=0).astype(bf16)


def gather_kernel(got_ref, state_far, out_ref, state_ref, sems):
    pairs = []
    for step in range(2):
        for half in range(2):
            rows = slice(half * LAT // 2, (half + 1) * LAT // 2)
            pairs.append((state_far.at[step, 0, rows], state_ref.at[step, rows]))
    copies = fetch(pairs, sems)
    for step in range(2):
        hots = [one_hot(step, got_ref, group) for group in range(LAT // BLK)]
        for pair in range(2):
            copies[2 * step + pair].wait()
            found = []
            for group in (2 * pair, 2 * pair + 1):
                field = state_ref[step, group * BLK : (group + 1) * BLK].reshape(ROWS, CH)
                rows = jnp.dot(hots[group], field, preferred_element_type=f32)
                found.append(rows.reshape(CAP, BLK, CH))
            both = jnp.concatenate(found, axis=1).astype(bf16)
            out_ref[:, 2 * BLK * pair : 2 * BLK * (pair + 1), step * CH : (step + 1) * CH] = both


def gather_rows(got, states):
    return pl.pallas_call(
        gather_kernel,
        out_shape=jax.ShapeDtypeStruct((CAP, LAT, 2 * CH), bf16),
        in_specs=[VM, HBM],
        scratch_shapes=[pltpu.VMEM((2, LAT, WID, CH), bf16), pltpu.SemaphoreType.DMA((4,))],
        compiler_params=limit(6),
        cost_estimate=pl.CostEstimate(flops=1000000, bytes_accessed=2000000, transcendentals=0),
    )(got, far(states))


def departure_kernel(rows_ref, got_ref, out_ref):
    for step in range(2):
        lanes = slice(step * CH, (step + 1) * CH)
        sampled = rows_ref[:, :, lanes].astype(f32)
        members = sampled.shape[0]
        other = got_ref[:, 2 * step + 1, :]
        values = jnp.concatenate([got_ref[:, 2 * step, :], other[:, 0:64]], axis=1)
        ens_mean = jnp.sum(sampled, axis=0) * (1.0 / members)
        ens_var = jnp.sum(sampled * sampled, axis=0) * (1.0 / members) - ens_mean * ens_mean
        weight = 1.0 / (other[:, 64 + CAP : 65 + CAP] + ens_var)
        ratio = (sampled - values[None]) * weight[None]
        live = other[:, 64 + 2 * CAP : 65 + 2 * CAP] >= 0.0
        out_ref[:, :, lanes] = jnp.where(live[None], ratio, 0.0).astype(bf16)


def departures(rows, got):
    return pl.pallas_call(
        departure_kernel,
        out_shape=jax.ShapeDtypeStruct((CAP, LAT, 2 * CH), bf16),
        compiler_params=limit(6),
        cost_estimate=pl.CostEstimate(flops=1200000, bytes_accessed=1200000, transcendentals=0),
    )(rows, got)


def forcing_of(step, rows_ref, got_ref, group):
    rows = rows_ref[:, :, step * CH : (step + 1) * CH].astype(f32)[:, group * BLK : (group + 1) * BLK]
    rows = rows.reshape(CAP * BLK, CH).astype(bf16)
    return lax.dot_general(one_hot(step, got_ref, group), rows, TN, preferred_element_type=f32)


def normalise(hidden):
    centred = hidden - mean_lanes(hidden)
    inv_std = lax.rsqrt(mean_lanes(centred * centred) + norm_eps)
    return centred * inv_std, inv_std


def backward(adjoint, slope_at, down_ref, up_ref, gain, unit):
    adj_norm = jnp.zeros((ROWS, CH), f32)
    for part in range(3):
        cols = slice(part * 256, (part + 1) * 256)
        act = jnp.dot(adjoint, down_ref[:, cols], preferred_element_type=f32)
        pre = (act * slope_at(cols)).astype(bf16)
        adj_norm = adj_norm + lax.dot_general(pre, up_ref[:, cols], NT, preferred_element_type=f32)
    scaled = adj_norm * gain
    return scaled - mean_lanes(scaled) - unit * mean_lanes(scaled * unit)


def put_hidden(adj_hidden, first, out_ref, tail_ref, head_ref):
    block = adj_hidden.astype(bf16).reshape(BLK, WID, CH)
    out_ref[pl.ds(first, BLK)] = block
    head_ref[pl.ds(first, BLK)] = block[:, 0:3]
    tail_ref[pl.ds(first, BLK)] = block[:, WID - 3 : WID]


def forward_kernel(step, state_ref, left_ref, right_ref, kernel_ref, gain_ref, up_ref, bias_ref, *rest):
    shifts, padded, hidden = rest[-3:]
    if step == 0:
        later_right, later_left = rest[5:7]
        later_right[...] = right_ref[1]
        later_left[...] = left_ref[1]
        right_ref, left_ref = right_ref.at[0], left_ref.at[0]
    gain = gain_ref[...]
    build_shifts(
        shifts, padded,
        lambda row: state_ref[step, 0, row],
        lambda row: left_ref[row],
        lambda row: right_ref[row],
    )

    def block(index, carry):
        first = index * BLK

        def emit(target, low, high, value):
            hidden[target, :, low:high] = value

        convolve(shifts, kernel_ref, first, False, emit)
        unit, inv_std = normalise(hidden[...].reshape(ROWS, CH))
        normed = (unit * gain).astype(bf16)

        def slope_at(cols):
            preact = jnp.dot(normed, up_ref[:, cols], preferred_element_type=f32)
            return gelu_slope(preact + bias_ref[:, cols]) * inv_std

        if step == 0:
            down_ref, adjoint_ref, hidden_out, tail_out, head_out = rest[:5]
            adjoint = adjoint_ref[0, pl.ds(first, BLK)].reshape(ROWS, CH)
            result = backward(adjoint, slope_at, down_ref, up_ref, gain, unit)
            put_hidden(result, first, hidden_out, tail_out, head_out)
        else:
            slope_out, unit_out = rest[:2]
            rows = pl.ds(pl.multiple_of(index * ROWS, ROWS), ROWS)
            for part in range(3):
                cols = slice(part * 256, (part + 1) * 256)
                slope_out[rows, cols] = slope_at(cols).astype(bf16)
            unit_out[rows, :] = unit.astype(bf16)
        return carry

    lax.fori_loop(0, LAT // BLK, block, 0)


FAR_EDGE = pltpu.HBM((LAT, 3, CH), bf16)
EDGE = jax.ShapeDtypeStruct((LAT, 3, CH), bf16)
FIELD = jax.ShapeDtypeStruct((LAT, WID, CH), bf16)
SHIFT_SCRATCH = [pltpu.VMEM((7, LAT + 6, WID, CH), f32), pltpu.VMEM((UNROLL, WID + 8, CH), f32)]


def forward(step, states, left, right, *others):
    shapes = (pltpu.HBM((LAT, WID, CH), bf16),) + (FAR_EDGE,) * 4 if step == 0 else (
        pltpu.HBM((CELLS, HID), bf16), pltpu.HBM((CELLS, CH), bf16)
    )
    return pl.pallas_call(
        functools.partial(forward_kernel, step),
        out_shape=shapes,
        out_specs=(VM,) * len(shapes),
        scratch_shapes=SHIFT_SCRATCH + [pltpu.VMEM((BLK, WID, CH), f32)],
        compiler_params=limit(16),
        cost_estimate=pl.CostEstimate(flops=6 * CELLS * CH * HID, bytes_accessed=8000000, transcendentals=CELLS * HID),
    )(states, left, right, *others)


def spread_kernel(hidden_ref, right_ref, left_ref, base_ref, kernel_ref, out_ref, shifts, padded):
    build_shifts(
        shifts, padded,
        lambda row: hidden_ref[row],
        lambda row: left_ref[row],
        lambda row: right_ref[row],
    )

    def block(index, carry):
        first = index * BLK

        def emit(target, low, high, value):
            base = base_ref[0, first + target, :, low:high].astype(f32)
            out_ref[first + target, :, low:high] = base + value

        convolve(shifts, kernel_ref, first, True, emit)
        return carry

    lax.fori_loop(0, LAT // BLK, block, 0)


def spread_back(hidden, right, left, base, kernel):
    return pl.pallas_call(
        spread_kernel,
        out_shape=jax.ShapeDtypeStruct((LAT, WID, CH), f32),
        scratch_shapes=SHIFT_SCRATCH,
        compiler_params=limit(16),
        cost_estimate=pl.CostEstimate(flops=98 * CELLS * CH, bytes_accessed=3000000, transcendentals=0),
    )(hidden, right, left, base, kernel)


def second_kernel(
    partial_ref, rows_ref, got_ref, slope_ref, unit_ref, gain_ref, up_ref, down_ref,
    hidden_out, tail_out, head_out, adjoint_out, slope_buf, unit_buf, down_buf, sems,
):
    parts = [slice(group * ROWS, (group + 1) * ROWS) for group in range(LAT // BLK)]
    pairs = [(down_ref, down_buf), (unit_ref, unit_buf)]
    copies = fetch(pairs + [(slope_ref.at[rows], slope_buf.at[rows]) for rows in parts], sems)
    gain = gain_ref[...]
    for group in range(LAT // BLK):
        first = group * BLK
        rows = slice(group * ROWS, (group + 1) * ROWS)
        forcing = forcing_of(0, rows_ref, got_ref, group)
        adjoint = (partial_ref[first : first + BLK].reshape(ROWS, CH) + forcing).astype(bf16)
        adjoint_out[first : first + BLK] = adjoint.reshape(BLK, WID, CH)
        if group == 0:
            copies[0].wait()
            copies[1].wait()
        copies[2 + group].wait()
        result = backward(
            adjoint,
            lambda cols: slope_buf[rows, cols].astype(f32),
            down_buf, up_ref, gain,
            unit_buf[rows, :].astype(f32),
        )
        put_hidden(result, first, hidden_out, tail_out, head_out)


def second_step(partial, rows, got, slope, unit, gain, up, down):
    return pl.pallas_call(
        second_kernel,
        out_shape=(FIELD, EDGE, EDGE, FIELD),
        in_specs=[VM, VM, VM, HBM, HBM, VM, VM, HBM],
        scratch_shapes=[
            pltpu.VMEM((CELLS, HID), bf16), pltpu.VMEM((CELLS, CH), bf16), pltpu.VMEM((CH, HID), bf16),
            pltpu.SemaphoreType.DMA((6,)),
        ],
        compiler_params=limit(12),
        cost_estimate=pl.CostEstimate(flops=4 * CELLS * CH * HID, bytes_accessed=5000000, transcendentals=0),
    )(partial, rows, got, far(slope), far(unit), gain, up, far(down))


def interior_kernel(hidden_ref, adjoint_ref, rows_ref, got_ref, kernel_ref, out_ref, west_ref, east_ref, shifts, padded, total):
    build_shifts(shifts, padded, lambda row: hidden_ref[row])
    for group in range(LAT // BLK):
        first = group * BLK
        forcing = forcing_of(1, rows_ref, got_ref, group).reshape(BLK, WID, CH)
        total[first : first + BLK] = adjoint_ref[first : first + BLK].astype(f32) + forcing

    def block(index, carry):
        first = index * BLK

        def emit(target, low, high, value):
            value = total[first + target, :, low:high] + value
            out_ref[first + target, :, low:high] = value.astype(bf16)
            west_ref[first + target, :, low:high] = value[0:8]
            east_ref[first + target, :, low:high] = value[WID - 8 : WID]

        convolve(shifts, kernel_ref, first, True, emit)
        return carry

    lax.fori_loop(0, LAT // BLK, block, 0)


STRIP = jax.ShapeDtypeStruct((LAT, 8, CH), f32)


def interior(hidden, adjoint, rows, got, kernel):
    return pl.pallas_call(
        interior_kernel,
        out_shape=(FIELD, STRIP, STRIP),
        scratch_shapes=SHIFT_SCRATCH + [pltpu.VMEM((LAT, WID, CH), f32)],
        compiler_params=limit(16),
        cost_estimate=pl.CostEstimate(flops=98 * CELLS * CH, bytes_accessed=3000000, transcendentals=0),
    )(hidden, adjoint, rows, got, kernel)


def edge_kernel(inner_ref, west_ref, east_ref, right_ref, left_ref, kernel_ref, out_ref, shifts, padded):
    def side(halo_ref, strip_ref, place, offset, cols):
        clear_rims(shifts, 3, 8)
        padded[...] = jnp.zeros(padded.shape, f32)

        def some_rows(index, carry):
            for lane in range(BLK):
                padded[lane, place : place + 3] = halo_ref[index * BLK + lane].astype(f32)
            for lane in range(BLK):
                for col in range(3):
                    shifts[col, index * BLK + lane + 3] = padded[lane, col + offset : col + offset + 8]
            return carry

        lax.fori_loop(0, LAT // BLK, some_rows, 0)

        def block(index, carry):
            first = index * BLK

            def emit(target, low, high, value):
                out_ref[first + target, :, low:high] = (strip_ref[first + target, :, low:high] + value).astype(bf16)

            convolve(shifts, kernel_ref, first, True, emit, cols, 8)
            return carry

        lax.fori_loop(0, LAT // BLK, block, 0)

    @pl.when(pl.program_id(0) == 0)
    def _():
        side(left_ref, west_ref, 0, 0, range(0, 3))

    @pl.when(pl.program_id(0) == 1)
    def _():
        side(right_ref, east_ref, 8, 1, range(4, 7))


def finish_edges(inner, west, east, left, right, kernel):
    whole = lambda array: pl.BlockSpec(array.shape, lambda i: (0,) * array.ndim)
    return pl.pallas_call(
        edge_kernel,
        grid=(2,),
        in_specs=[pl.BlockSpec(memory_space=pl.ANY)] + [whole(x) for x in (west, east, right, left, kernel)],
        out_specs=pl.BlockSpec((LAT, 8, CH), lambda i: (0, 3 * i, 0)),
        out_shape=FIELD,
        input_output_aliases={0: 0},
        compiler_params=limit(4),
        scratch_shapes=[pltpu.VMEM((3, LAT + 6, 8, CH), f32), pltpu.VMEM((BLK, 16, CH), f32)],
        cost_estimate=pl.CostEstimate(flops=5000000, bytes_accessed=700000, transcendentals=0),
    )(inner, west, east, right, left, kernel)


def swap_edges(head, tail):
    peers = lax.axis_size("tile")
    up = [(i, (i + 1) % peers) for i in range(peers)]
    down = [(j, i) for i, j in up]
    right = lax.ppermute(head, "tile", down)
    left = lax.ppermute(tail, "tile", up)
    return left, right


def after(array, other):
    return lax.optimization_barrier((array, other))[0]


def exchange(array, axis):
    return lax.all_to_all(array, axis, split_axis=0, concat_axis=0, tiled=True)


def per_device(
    adjoint_final, states, kernel, norm_gain, up_weight, up_bias, down_weight,
    obs_cell, obs_count, obs_value, obs_error,
):
    gain = norm_gain[None]
    bias = up_bias[None]
    down = down_weight.T

    packed = pack_observations(
        obs_cell[:, 0].transpose(0, 2, 1), obs_count, obs_value, obs_error[:, 0].transpose(0, 2, 1)
    )
    got = exchange(packed, "tile")
    rows = gather_rows(got, states)
    owned = exchange(rows, "member")

    source = after(states, rows)[:, 0]
    left, right = swap_edges(source[:, :, 0:3], source[:, :, WID - 3 : WID])
    hidden, tail, head, later_right, later_left = forward(
        0, states, left, right, kernel, gain, up_weight, bias, down, adjoint_final
    )
    deps = departures(after(owned, hidden), got)
    back = exchange(deps, "member")

    before, behind = swap_edges(*after((head, tail), deps))
    slope, unit = forward(1, after(states, deps), later_left, later_right, kernel, gain, up_weight, bias)
    partial = spread_back(hidden, after(behind, slope), before, adjoint_final, kernel)

    hidden, tail, head, adjoint = second_step(
        partial, after(back, partial), got, slope, unit, gain, up_weight, down
    )
    left, right = swap_edges(head, tail)
    inner, west, east = interior(hidden, adjoint, back, got, kernel)
    return finish_edges(inner, west, east, left, right, kernel)[None]


def solution(mesh):
    placed = (
        P("member", None, "tile", None),
        P(None, "member", None, "tile", None),
        P(),
        P(),
        P(),
        P(),
        P(),
        P(None, "tile", None, None),
        P(None, "tile", None),
        P(None, "tile", None, None, None),
        P(None, "tile", None, None),
    )
    return jax.shard_map(
        per_device,
        mesh=mesh,
        in_specs=placed,
        out_specs=P("member", None, "tile", None),
        check_vma=False,
    )
```

```python
import functools
import math

import jax
import jax.numpy as jnp
from jax import lax
from jax.experimental import pallas as pl
from jax.experimental.pallas import tpu as pltpu
from jax.sharding import PartitionSpec as P

slope_coef = math.sqrt(2.0 / math.pi)
cubic_coef = 0.044715
norm_eps = 1e-06

LAT = 32
WID = 32
CH = 192
HID = 768
CAP = 16
CELLS = LAT * WID
SLOTS = LAT * CAP
BLK = 8
ROWS = BLK * WID
UNROLL = 4
HALF = LAT // 2
f32 = jnp.float32
bf16 = jnp.bfloat16
NT = (((1,), (1,)), ((), ()))
TN = (((0,), (0,)), ((), ()))


def gelu_slope(preact):
    square = preact * preact
    tanh_val = jnp.tanh(preact * (slope_coef + (slope_coef * cubic_coef) * square))
    tail = preact * (0.5 * slope_coef + (1.5 * slope_coef * cubic_coef) * square)
    return (0.5 + 0.5 * tanh_val) + tail * (1.0 - tanh_val * tanh_val)


def limit(mebibytes):
    return pltpu.CompilerParams(vmem_limit_bytes=mebibytes * 1024 * 1024)


def mean_lanes(value):
    return jnp.sum(value, axis=-1, keepdims=True) * (1.0 / CH)


HBM = pl.BlockSpec(memory_space=pltpu.HBM)
VM = pl.BlockSpec(memory_space=pltpu.VMEM)


def fetch(pairs, sems):
    copies = [pltpu.make_async_copy(src, dst, sems.at[i]) for i, (src, dst) in enumerate(pairs)]
    for copy in copies:
        copy.start()
    return copies


def far(array):
    return pltpu.with_memory_space_constraint(array, pltpu.HBM)


def clear_rims(shifts, count, width):
    for edge in range(3):
        zeros = jnp.zeros((width, CH), f32)
        for col in range(count):
            shifts[col, edge] = zeros
            shifts[col, LAT + 3 + edge] = zeros


def build_shifts(low, high, padded, centre, left=None, right=None):
    zeros = jnp.zeros((WID, 128), f32)
    for edge in range(3):
        for col in range(7):
            low[col, edge] = zeros
            low[col, LAT + 3 + edge] = zeros
    if left is None:
        padded[...] = jnp.zeros(padded.shape, f32)

    def spread_rows(rows, part, target, offset):
        for lane, row in enumerate(rows):
            if left is not None:
                padded[lane, 0:3] = part(left, row)
                padded[lane, WID + 3 : WID + 6] = part(right, row)
            padded[lane, 3 : WID + 3] = part(centre, row)
        for lane, row in enumerate(rows):
            for col in range(7):
                target[col, row + offset] = padded[lane, col : col + WID]

    def low_part(source, row):
        return source(row)[:, 0:128].astype(f32)

    def high_part(source, row):
        first = source(row - 3)[:, 128:CH].astype(f32) if not isinstance(row, int) or row >= 3 else None
        second = source(row + HALF - 3)[:, 128:CH].astype(f32) if not isinstance(row, int) or row < 19 else None
        first = jnp.zeros_like(second) if first is None else first
        second = jnp.zeros_like(first) if second is None else second
        return jnp.concatenate([first, second], axis=1)

    def some_low(index, carry):
        spread_rows([index * UNROLL + lane for lane in range(UNROLL)], low_part, low, 3)
        return carry

    def some_high(index, carry):
        spread_rows([index * UNROLL + lane + 3 for lane in range(UNROLL)], high_part, high, 0)
        return carry

    lax.fori_loop(0, LAT // UNROLL, some_low, 0)
    lax.fori_loop(0, HALF // UNROLL, some_high, 0)
    spread_rows([0, 1, 2], high_part, high, 0)
    spread_rows([19, 20, 21], high_part, high, 0)


def block_sums(shifts, first, tap, cols=range(7), lanes=slice(0, 128)):
    sums = [None] * BLK
    for place, col in enumerate(cols):
        taps = [tap(row, col) for row in range(7)]
        for source in range(BLK + 6):
            field = shifts[place, first + source, :, lanes]
            for row in range(7):
                target = source - row
                if 0 <= target < BLK:
                    term = taps[row] * field
                    sums[target] = term if sums[target] is None else sums[target] + term
    return sums


def tap_of(kernel_ref, flip, lanes, width):
    def tap(row, col):
        down, across = (6 - row, 6 - col) if flip else (row, col)
        value = kernel_ref[down, across : across + 1, lanes]
        return jnp.broadcast_to(value, (width, value.shape[1]))

    return tap


def convolve(low, high, twice, kernel_ref, flip, emit):
    for row in range(7):
        upper = kernel_ref[row, :, 128:CH]
        twice[row, 0:7] = jnp.concatenate([upper, upper], axis=1)

    def low_block(index, carry):
        first = index * BLK
        sums = block_sums(low, first, tap_of(kernel_ref, flip, slice(0, 128), WID))
        for target in range(BLK):
            emit(first + target, 0, 128, sums[target])
        return carry

    def high_block(index, carry):
        first = index * BLK
        sums = block_sums(high, first, tap_of(twice, flip, slice(0, 128), WID))
        for target in range(BLK):
            emit(first + target, 128, CH, sums[target][:, 0:64])
            emit(first + target + HALF, 128, CH, sums[target][:, 64:128])
        return carry

    lax.fori_loop(0, LAT // BLK, low_block, 0)
    lax.fori_loop(0, HALF // BLK, high_block, 0)


def pack_kernel(cell_far, count_far, value_far, error_far, out_ref, cell_ref, count_ref, value_ref, error_ref, sems):
    pairs = [(cell_far, cell_ref), (count_far, count_ref), (value_far, value_ref), (error_far, error_ref)]
    for copy in fetch(pairs, sems):
        copy.wait()
    member = lax.axis_index("member")
    tiles = cell_ref.shape[2]
    slot = lax.broadcasted_iota(jnp.int32, (CAP, tiles), 0)
    across = lax.broadcasted_iota(jnp.int32, (CAP, CAP), 1)
    same = jnp.where(lax.broadcasted_iota(jnp.int32, (CAP, CAP), 0) == across, 1.0, 0.0).astype(bf16)
    own = jnp.where(lax.broadcasted_iota(jnp.int32, (CAP, CAP), 0) == member, 1.0, 0.0).astype(bf16)
    deep = lax.broadcasted_iota(jnp.int32, (tiles, CAP, CH), 1)
    for step in range(2):
        live = slot < count_ref[step]
        cells = jnp.where(live, cell_ref[step], -1).astype(f32).astype(bf16)
        values = jnp.sum(jnp.where(deep == member, value_ref[step, 0].astype(f32), 0.0), axis=1)
        turn = lambda array, pick: lax.dot_general(array, pick, TN, preferred_element_type=f32)
        out_ref[:, 2 * step, :] = values[:, 0:128]
        out_ref[:, 2 * step + 1, :] = jnp.concatenate(
            [values[:, 128:CH], turn(cells, same), turn(error_ref[step], own), turn(cells, own), jnp.zeros((tiles, CAP), f32)],
            axis=1)


def pack_observations(cells, counts, values, errors):
    return pl.pallas_call(
        pack_kernel,
        out_shape=pltpu.HBM((cells.shape[2], 4, 128), f32),
        in_specs=[HBM] * 4,
        out_specs=VM,
        scratch_shapes=[pltpu.VMEM(array.shape, array.dtype) for array in (cells, counts, values, errors)]
        + [pltpu.SemaphoreType.DMA((4,))],
        compiler_params=limit(6),
    )(far(cells), far(counts), far(values), far(errors))


def one_hot(step, got_ref, group):
    cells = got_ref[group * BLK : (group + 1) * BLK, 2 * step + 1, 64 : 64 + CAP]
    lane = lax.broadcasted_iota(jnp.int32, (BLK, ROWS), 1)
    band = lax.broadcasted_iota(jnp.int32, (BLK, ROWS), 0)
    offset = (lane - band * WID).astype(f32)
    rows = [jnp.where(offset == cells[:, slot : slot + 1], 1.0, 0.0) for slot in range(CAP)]
    return jnp.concatenate(rows, axis=0)


def gather_kernel(got_ref, state_far, out_ref, state_ref, sems):
    pairs = []
    for step in range(2):
        for half in range(2):
            rows = slice(half * LAT // 2, (half + 1) * LAT // 2)
            pairs.append((state_far.at[step, 0, rows], state_ref.at[step, rows]))
    copies = fetch(pairs, sems)
    for step in range(2):
        hots = [one_hot(step, got_ref, group).astype(bf16) for group in range(LAT // BLK)]
        for pair in range(2):
            copies[2 * step + pair].wait()
            found = []
            for group in (2 * pair, 2 * pair + 1):
                field = state_ref[step, group * BLK : (group + 1) * BLK].reshape(ROWS, CH)
                rows = jnp.dot(hots[group], field, preferred_element_type=f32)
                found.append(rows.reshape(CAP, BLK, CH))
            both = jnp.concatenate(found, axis=1).astype(bf16)
            out_ref[:, 2 * BLK * pair : 2 * BLK * (pair + 1), step * CH : (step + 1) * CH] = both


def gather_rows(got, states):
    return pl.pallas_call(
        gather_kernel,
        out_shape=jax.ShapeDtypeStruct((CAP, LAT, 2 * CH), bf16),
        in_specs=[VM, HBM],
        scratch_shapes=[pltpu.VMEM((2, LAT, WID, CH), bf16), pltpu.SemaphoreType.DMA((4,))],
        compiler_params=limit(6),
        cost_estimate=pl.CostEstimate(flops=1000000, bytes_accessed=2000000, transcendentals=0),
    )(got, far(states))


def departure_kernel(rows_ref, got_ref, out_ref):
    for step in range(2):
        lanes = slice(step * CH, (step + 1) * CH)
        sampled = rows_ref[:, :, lanes].astype(f32)
        members = sampled.shape[0]
        other = got_ref[:, 2 * step + 1, :]
        values = jnp.concatenate([got_ref[:, 2 * step, :], other[:, 0:64]], axis=1)
        ens_mean = jnp.sum(sampled, axis=0) * (1.0 / members)
        ens_var = jnp.sum(sampled * sampled, axis=0) * (1.0 / members) - ens_mean * ens_mean
        weight = 1.0 / (other[:, 64 + CAP : 65 + CAP] + ens_var)
        ratio = (sampled - values[None]) * weight[None]
        live = other[:, 64 + 2 * CAP : 65 + 2 * CAP] >= 0.0
        out_ref[:, :, lanes] = jnp.where(live[None], ratio, 0.0).astype(bf16)


def departures(rows, got):
    return pl.pallas_call(
        departure_kernel,
        out_shape=jax.ShapeDtypeStruct((CAP, LAT, 2 * CH), bf16),
        compiler_params=limit(6),
        cost_estimate=pl.CostEstimate(flops=1200000, bytes_accessed=1200000, transcendentals=0),
    )(rows, got)


def cell_row(step, got_ref, group):
    cells = got_ref[group * BLK : (group + 1) * BLK, 2 * step + 1, 64 : 64 + CAP]
    band = lax.broadcasted_iota(jnp.int32, (BLK, CAP), 0).astype(f32)
    cells = jnp.where(cells < 0.0, -1.0, cells + band * WID)
    column = jnp.concatenate([cells[:, slot : slot + 1] for slot in range(CAP)], axis=0)
    return jnp.broadcast_to(column, (CAP * BLK, CAP * BLK)).T[0:1]


def forcing_of(step, rows_ref, cell_ref, group):
    place = step * (LAT // BLK) + group
    cells = jnp.broadcast_to(cell_ref[place : place + 1, :], (ROWS, CAP * BLK))
    cell = lax.broadcasted_iota(jnp.int32, (ROWS, CAP * BLK), 0).astype(f32)
    hot = jnp.where(cell == cells, 1.0, 0.0).astype(bf16)
    rows = rows_ref[:, :, step * CH : (step + 1) * CH].astype(f32)[:, group * BLK : (group + 1) * BLK]
    rows = rows.reshape(CAP * BLK, CH).astype(bf16)
    return jnp.dot(hot, rows, preferred_element_type=f32)


def normalise(hidden):
    centred = hidden - mean_lanes(hidden)
    inv_std = lax.rsqrt(mean_lanes(centred * centred) + norm_eps)
    return centred * inv_std, inv_std


def backward(adjoint, slope_at, down_ref, up_ref, gain, unit):
    adj_norm = jnp.zeros((ROWS, CH), f32)
    for part in range(3):
        cols = slice(part * 256, (part + 1) * 256)
        act = jnp.dot(adjoint, down_ref[:, cols], preferred_element_type=f32)
        pre = (act * slope_at(cols)).astype(bf16)
        adj_norm = adj_norm + lax.dot_general(pre, up_ref[:, cols], NT, preferred_element_type=f32)
    scaled = adj_norm * gain
    return scaled - mean_lanes(scaled) - unit * mean_lanes(scaled * unit)


def put_hidden(adj_hidden, first, out_ref, tail_ref, head_ref):
    block = adj_hidden.astype(bf16).reshape(BLK, WID, CH)
    out_ref[pl.ds(first, BLK)] = block
    head_ref[pl.ds(first, BLK)] = block[:, 0:3]
    tail_ref[pl.ds(first, BLK)] = block[:, WID - 3 : WID]


def forward_kernel(step, state_ref, left_ref, right_ref, kernel_ref, gain_ref, up_ref, bias_ref, *rest):
    low, high, twice, padded, hidden = rest[-5:]
    if step == 0:
        later_right, later_left = rest[5:7]
        later_right[...] = right_ref[1]
        later_left[...] = left_ref[1]
        right_ref, left_ref = right_ref.at[0], left_ref.at[0]
    gain = gain_ref[...]
    build_shifts(
        low, high, padded,
        lambda row: state_ref[step, 0, row],
        lambda row: left_ref[row],
        lambda row: right_ref[row],
    )

    def emit(row, start, stop, value):
        hidden[row, :, start:stop] = value

    convolve(low, high, twice, kernel_ref, False, emit)

    def block(index, carry):
        first = index * BLK
        unit, inv_std = normalise(hidden[pl.ds(first, BLK)].reshape(ROWS, CH))
        normed = (unit * gain).astype(bf16)

        def slope_at(cols):
            preact = jnp.dot(normed, up_ref[:, cols], preferred_element_type=f32)
            return gelu_slope(preact + bias_ref[:, cols]) * inv_std

        if step == 0:
            down_ref, adjoint_ref, hidden_out, tail_out, head_out = rest[:5]
            adjoint = adjoint_ref[0, pl.ds(first, BLK)].reshape(ROWS, CH)
            result = backward(adjoint, slope_at, down_ref, up_ref, gain, unit)
            put_hidden(result, first, hidden_out, tail_out, head_out)
        else:
            slope_out, unit_out = rest[:2]
            rows = pl.ds(pl.multiple_of(index * ROWS, ROWS), ROWS)
            for part in range(3):
                cols = slice(part * 256, (part + 1) * 256)
                slope_out[rows, cols] = slope_at(cols).astype(bf16)
            unit_out[rows, :] = unit.astype(bf16)
        return carry

    lax.fori_loop(0, LAT // BLK, block, 0)


FAR_EDGE = pltpu.HBM((LAT, 3, CH), bf16)
EDGE = jax.ShapeDtypeStruct((LAT, 3, CH), bf16)
FIELD = jax.ShapeDtypeStruct((LAT, WID, CH), bf16)
SHIFT_SCRATCH = [
    pltpu.VMEM((7, LAT + 6, WID, 128), f32),
    pltpu.VMEM((7, HALF + 6, WID, 128), f32),
    pltpu.VMEM((7, 8, 128), f32),
    pltpu.VMEM((UNROLL, WID + 8, 128), f32),
]


def forward(step, states, left, right, *others):
    shapes = (pltpu.HBM((LAT, WID, CH), bf16),) + (FAR_EDGE,) * 4 if step == 0 else (
        pltpu.HBM((CELLS, HID), bf16), pltpu.HBM((CELLS, CH), bf16)
    )
    return pl.pallas_call(
        functools.partial(forward_kernel, step),
        out_shape=shapes,
        out_specs=(VM,) * len(shapes),
        scratch_shapes=SHIFT_SCRATCH + [pltpu.VMEM((LAT, WID, CH), f32)],
        compiler_params=limit(16),
        cost_estimate=pl.CostEstimate(flops=6 * CELLS * CH * HID, bytes_accessed=8000000, transcendentals=CELLS * HID),
    )(states, left, right, *others)


def spread_kernel(
    hidden_ref, right_ref, left_ref, base_ref, kernel_ref, got_ref, slope_far,
    out_ref, slope_out, cell_out,
    low, high, twice, padded, sems,
):
    copies = fetch([(slope_far, slope_out)], sems)
    for step in range(2):
        for group in range(LAT // BLK):
            place = step * (LAT // BLK) + group
            cell_out[place : place + 1, :] = cell_row(step, got_ref, group)
    build_shifts(
        low, high, padded,
        lambda row: hidden_ref[row],
        lambda row: left_ref[row],
        lambda row: right_ref[row],
    )

    def emit(row, start, stop, value):
        out_ref[row, :, start:stop] = base_ref[0, row, :, start:stop].astype(f32) + value

    convolve(low, high, twice, kernel_ref, True, emit)
    for copy in copies:
        copy.wait()


def spread_back(hidden, right, left, base, kernel, got, slope):
    return pl.pallas_call(
        spread_kernel,
        out_shape=(
            jax.ShapeDtypeStruct((LAT, WID, CH), f32),
            jax.ShapeDtypeStruct(slope.shape, bf16),
            jax.ShapeDtypeStruct((2 * LAT // BLK, CAP * BLK), f32),
        ),
        in_specs=[VM] * 6 + [HBM],
        scratch_shapes=SHIFT_SCRATCH + [pltpu.SemaphoreType.DMA((1,))],
        compiler_params=limit(18),
        cost_estimate=pl.CostEstimate(flops=98 * CELLS * CH, bytes_accessed=3000000, transcendentals=0),
    )(hidden, right, left, base, kernel, got, far(slope))


def second_kernel(
    partial_ref, rows_ref, hot_ref, slope_ref, unit_far, gain_ref, up_ref, down_far,
    hidden_out, tail_out, head_out, adjoint_out, unit_ref, down_ref, sems,
):
    copies = fetch([(down_far, down_ref), (unit_far, unit_ref)], sems)
    gain = gain_ref[...]
    for group in range(LAT // BLK):
        first = group * BLK
        rows = slice(group * ROWS, (group + 1) * ROWS)
        forcing = forcing_of(0, rows_ref, hot_ref, group)
        adjoint = (partial_ref[first : first + BLK].reshape(ROWS, CH) + forcing).astype(bf16)
        adjoint_out[first : first + BLK] = adjoint.reshape(BLK, WID, CH)
        if group == 0:
            for copy in copies:
                copy.wait()
        result = backward(
            adjoint,
            lambda cols: slope_ref[rows, cols].astype(f32),
            down_ref, up_ref, gain,
            unit_ref[rows, :].astype(f32),
        )
        put_hidden(result, first, hidden_out, tail_out, head_out)


def second_step(partial, rows, hot, slope, unit, gain, up, down):
    return pl.pallas_call(
        second_kernel,
        out_shape=(FIELD, EDGE, EDGE, FIELD),
        in_specs=[VM] * 4 + [HBM, VM, VM, HBM],
        scratch_shapes=[pltpu.VMEM((CELLS, CH), bf16), pltpu.VMEM((CH, HID), bf16), pltpu.SemaphoreType.DMA((2,))],
        compiler_params=limit(8),
        cost_estimate=pl.CostEstimate(flops=4 * CELLS * CH * HID, bytes_accessed=5000000, transcendentals=0),
    )(partial, rows, hot, slope, far(unit), gain, up, far(down))


def interior_kernel(
    hidden_ref, adjoint_ref, rows_ref, hot_ref, kernel_ref, out_ref, west_ref, east_ref,
    low, high, twice, padded, total,
):
    build_shifts(low, high, padded, lambda row: hidden_ref[row])
    for group in range(LAT // BLK):
        first = group * BLK
        forcing = forcing_of(1, rows_ref, hot_ref, group).reshape(BLK, WID, CH)
        total[first : first + BLK] = adjoint_ref[first : first + BLK].astype(f32) + forcing

    def emit(row, start, stop, value):
        value = total[row, :, start:stop] + value
        out_ref[row, :, start:stop] = value.astype(bf16)
        west_ref[row, :, start:stop] = value[0:8]
        east_ref[row, :, start:stop] = value[WID - 8 : WID]

    convolve(low, high, twice, kernel_ref, True, emit)


STRIP = jax.ShapeDtypeStruct((LAT, 8, CH), f32)


def interior(hidden, adjoint, rows, hot, kernel):
    return pl.pallas_call(
        interior_kernel,
        out_shape=(FIELD, STRIP, STRIP),
        scratch_shapes=SHIFT_SCRATCH + [pltpu.VMEM((LAT, WID, CH), f32)],
        compiler_params=limit(16),
        cost_estimate=pl.CostEstimate(flops=98 * CELLS * CH, bytes_accessed=3000000, transcendentals=0),
    )(hidden, adjoint, rows, hot, kernel)


def edge_kernel(inner_ref, west_ref, east_ref, right_ref, left_ref, kernel_ref, out_ref, shifts, padded):
    def side(halo_ref, strip_ref, place, offset, cols):
        clear_rims(shifts, 3, 8)
        padded[...] = jnp.zeros(padded.shape, f32)

        def some_rows(index, carry):
            for lane in range(BLK):
                padded[lane, place : place + 3] = halo_ref[index * BLK + lane].astype(f32)
            for lane in range(BLK):
                for col in range(3):
                    shifts[col, index * BLK + lane + 3] = padded[lane, col + offset : col + offset + 8]
            return carry

        lax.fori_loop(0, LAT // BLK, some_rows, 0)

        def block(index, carry):
            first = index * BLK

            for low, high in ((0, 128), (128, CH)):
                sums = block_sums(shifts, first, tap_of(kernel_ref, True, slice(low, high), 8), cols, slice(low, high))
                for target in range(BLK):
                    value = strip_ref[first + target, :, low:high] + sums[target]
                    out_ref[first + target, :, low:high] = value.astype(bf16)
            return carry

        lax.fori_loop(0, LAT // BLK, block, 0)

    @pl.when(pl.program_id(0) == 0)
    def _():
        side(left_ref, west_ref, 0, 0, range(0, 3))

    @pl.when(pl.program_id(0) == 1)
    def _():
        side(right_ref, east_ref, 8, 1, range(4, 7))


def finish_edges(inner, west, east, left, right, kernel):
    whole = lambda array: pl.BlockSpec(array.shape, lambda i: (0,) * array.ndim)
    return pl.pallas_call(
        edge_kernel,
        grid=(2,),
        in_specs=[pl.BlockSpec(memory_space=pl.ANY)] + [whole(x) for x in (west, east, right, left, kernel)],
        out_specs=pl.BlockSpec((LAT, 8, CH), lambda i: (0, 3 * i, 0)),
        out_shape=FIELD,
        input_output_aliases={0: 0},
        compiler_params=limit(4),
        scratch_shapes=[pltpu.VMEM((3, LAT + 6, 8, CH), f32), pltpu.VMEM((BLK, 16, CH), f32)],
        cost_estimate=pl.CostEstimate(flops=5000000, bytes_accessed=700000, transcendentals=0),
    )(inner, west, east, right, left, kernel)


def swap_edges(head, tail):
    peers = lax.axis_size("tile")
    up = [(i, (i + 1) % peers) for i in range(peers)]
    down = [(j, i) for i, j in up]
    right = lax.ppermute(head, "tile", down)
    left = lax.ppermute(tail, "tile", up)
    return left, right


def after(array, other):
    return lax.optimization_barrier((array, other))[0]


def exchange(array, axis):
    return lax.all_to_all(array, axis, split_axis=0, concat_axis=0, tiled=True)


def per_device(
    adjoint_final, states, kernel, norm_gain, up_weight, up_bias, down_weight,
    obs_cell, obs_count, obs_value, obs_error,
):
    gain = norm_gain[None]
    bias = up_bias[None]
    down = down_weight.T

    packed = pack_observations(
        obs_cell[:, 0].transpose(0, 2, 1), obs_count, obs_value, obs_error[:, 0].transpose(0, 2, 1)
    )
    got = exchange(packed, "tile")
    rows = gather_rows(got, states)
    owned = exchange(rows, "member")

    source = after(states, rows)[:, 0]
    left, right = swap_edges(source[:, :, 0:3], source[:, :, WID - 3 : WID])
    hidden, tail, head, later_right, later_left = forward(
        0, states, left, right, kernel, gain, up_weight, bias, down, adjoint_final
    )
    deps = departures(after(owned, hidden), got)
    back = exchange(deps, "member")

    before, behind = swap_edges(*after((head, tail), deps))
    slope, unit = forward(1, after(states, deps), later_left, later_right, kernel, gain, up_weight, bias)
    partial, slope, cells = spread_back(
        hidden, after(behind, slope), before, adjoint_final, kernel, got, slope
    )

    hidden, tail, head, adjoint = second_step(
        partial, after(back, partial), cells, slope, unit, gain, up_weight, down
    )
    left, right = swap_edges(head, tail)
    inner, west, east = interior(hidden, adjoint, back, cells, kernel)
    return finish_edges(inner, west, east, left, right, kernel)[None]


def solution(mesh):
    placed = (
        P("member", None, "tile", None),
        P(None, "member", None, "tile", None),
        P(),
        P(),
        P(),
        P(),
        P(),
        P(None, "tile", None, None),
        P(None, "tile", None),
        P(None, "tile", None, None, None),
        P(None, "tile", None, None),
    )
    return jax.shard_map(
        per_device,
        mesh=mesh,
        in_specs=placed,
        out_specs=P("member", None, "tile", None),
        check_vma=False,
    )
```

```python
import functools
import math

import jax
import jax.numpy as jnp
from jax import lax
from jax.experimental import pallas as pl
from jax.experimental.pallas import tpu as pltpu
from jax.sharding import PartitionSpec as P

slope_coef = math.sqrt(2.0 / math.pi)
cubic_coef = 0.044715
norm_eps = 1e-06

LAT = 32
WID = 32
CH = 192
HID = 768
CAP = 16
CELLS = LAT * WID
SLOTS = LAT * CAP
BLK = 8
ROWS = BLK * WID
UNROLL = 4
HALF = LAT // 2
f32 = jnp.float32
bf16 = jnp.bfloat16
NT = (((1,), (1,)), ((), ()))
TN = (((0,), (0,)), ((), ()))


def gelu_slope(preact):
    square = preact * preact
    tanh_val = jnp.tanh(preact * (slope_coef + (slope_coef * cubic_coef) * square))
    tail = preact * (0.5 * slope_coef + (1.5 * slope_coef * cubic_coef) * square)
    return (0.5 + 0.5 * tanh_val) + tail * (1.0 - tanh_val * tanh_val)


def limit(mebibytes):
    return pltpu.CompilerParams(vmem_limit_bytes=mebibytes * 1024 * 1024)


def mean_lanes(value):
    return jnp.sum(value, axis=-1, keepdims=True) * (1.0 / CH)


HBM = pl.BlockSpec(memory_space=pltpu.HBM)
VM = pl.BlockSpec(memory_space=pltpu.VMEM)


def fetch(pairs, sems):
    copies = [pltpu.make_async_copy(src, dst, sems.at[i]) for i, (src, dst) in enumerate(pairs)]
    for copy in copies:
        copy.start()
    return copies


def far(array):
    return pltpu.with_memory_space_constraint(array, pltpu.HBM)


def clear_rims(shifts, count, width):
    for edge in range(3):
        zeros = jnp.zeros((width, CH), f32)
        for col in range(count):
            shifts[col, edge] = zeros
            shifts[col, LAT + 3 + edge] = zeros


def build_shifts(low, high, padded, centre, left=None, right=None):
    zeros = jnp.zeros((WID, 128), f32)
    for edge in range(3):
        for col in range(7):
            low[col, edge] = zeros
            low[col, LAT + 3 + edge] = zeros
    if left is None:
        padded[...] = jnp.zeros(padded.shape, f32)

    def spread_rows(rows, part, target, offset):
        for lane, row in enumerate(rows):
            if left is not None:
                padded[lane, 0:3] = part(left, row)
                padded[lane, WID + 3 : WID + 6] = part(right, row)
            padded[lane, 3 : WID + 3] = part(centre, row)
        for lane, row in enumerate(rows):
            for col in range(7):
                target[col, row + offset] = padded[lane, col : col + WID]

    def low_part(source, row):
        return source(row)[:, 0:128].astype(f32)

    def high_part(source, row):
        first = source(row - 3)[:, 128:CH].astype(f32) if not isinstance(row, int) or row >= 3 else None
        second = source(row + HALF - 3)[:, 128:CH].astype(f32) if not isinstance(row, int) or row < 19 else None
        first = jnp.zeros_like(second) if first is None else first
        second = jnp.zeros_like(first) if second is None else second
        return jnp.concatenate([first, second], axis=1)

    def some_low(index, carry):
        spread_rows([index * UNROLL + lane for lane in range(UNROLL)], low_part, low, 3)
        return carry

    def some_high(index, carry):
        spread_rows([index * UNROLL + lane + 3 for lane in range(UNROLL)], high_part, high, 0)
        return carry

    lax.fori_loop(0, LAT // UNROLL, some_low, 0)
    lax.fori_loop(0, HALF // UNROLL, some_high, 0)
    spread_rows([0, 1, 2], high_part, high, 0)
    spread_rows([19, 20, 21], high_part, high, 0)


def block_sums(shifts, first, tap, cols=range(7), lanes=slice(0, 128)):
    sums = [None] * BLK
    for place, col in enumerate(cols):
        taps = [tap(row, col) for row in range(7)]
        for source in range(BLK + 6):
            field = shifts[place, first + source, :, lanes]
            for row in range(7):
                target = source - row
                if 0 <= target < BLK:
                    term = taps[row] * field
                    sums[target] = term if sums[target] is None else sums[target] + term
    return sums


def tap_of(kernel_ref, flip, lanes, width):
    def tap(row, col):
        down, across = (6 - row, 6 - col) if flip else (row, col)
        value = kernel_ref[down, across : across + 1, lanes]
        return jnp.broadcast_to(value, (width, value.shape[1]))

    return tap


def convolve(low, high, twice, kernel_ref, flip, emit):
    for row in range(7):
        upper = kernel_ref[row, :, 128:CH]
        twice[row, 0:7] = jnp.concatenate([upper, upper], axis=1)

    def low_block(index, carry):
        first = index * BLK
        sums = block_sums(low, first, tap_of(kernel_ref, flip, slice(0, 128), WID))
        for target in range(BLK):
            emit(first + target, 0, 128, sums[target])
        return carry

    def high_block(index, carry):
        first = index * BLK
        sums = block_sums(high, first, tap_of(twice, flip, slice(0, 128), WID))
        for target in range(BLK):
            emit(first + target, 128, CH, sums[target][:, 0:64])
            emit(first + target + HALF, 128, CH, sums[target][:, 64:128])
        return carry

    lax.fori_loop(0, LAT // BLK, low_block, 0)
    lax.fori_loop(0, HALF // BLK, high_block, 0)


def pack_kernel(
    cell_far, count_far, value_far, error_far, state_far,
    out_ref, near_ref, cell_ref, count_ref, value_ref, error_ref, sems,
):
    pairs = [(cell_far, cell_ref), (count_far, count_ref), (value_far, value_ref), (error_far, error_ref)]
    copies = fetch(pairs + [(state_far, near_ref)], sems)
    for copy in copies[:4]:
        copy.wait()
    member = lax.axis_index("member")
    tiles = cell_ref.shape[2]
    slot = lax.broadcasted_iota(jnp.int32, (CAP, tiles), 0)
    across = lax.broadcasted_iota(jnp.int32, (CAP, CAP), 1)
    same = jnp.where(lax.broadcasted_iota(jnp.int32, (CAP, CAP), 0) == across, 1.0, 0.0).astype(bf16)
    own = jnp.where(lax.broadcasted_iota(jnp.int32, (CAP, CAP), 0) == member, 1.0, 0.0).astype(bf16)
    deep = lax.broadcasted_iota(jnp.int32, (tiles, CAP, CH), 1)
    for step in range(2):
        live = slot < count_ref[step]
        cells = jnp.where(live, cell_ref[step], -1).astype(f32).astype(bf16)
        values = jnp.sum(jnp.where(deep == member, value_ref[step, 0].astype(f32), 0.0), axis=1)
        turn = lambda array, pick: lax.dot_general(array, pick, TN, preferred_element_type=f32)
        out_ref[:, 2 * step, :] = values[:, 0:128]
        out_ref[:, 2 * step + 1, :] = jnp.concatenate(
            [values[:, 128:CH], turn(cells, same), turn(error_ref[step], own), turn(cells, own), jnp.zeros((tiles, CAP), f32)],
            axis=1)
    copies[4].wait()


def pack_observations(cells, counts, values, errors, states):
    return pl.pallas_call(
        pack_kernel,
        out_shape=(pltpu.HBM((cells.shape[2], 4, 128), f32), pltpu.VMEM(states.shape, bf16)),
        in_specs=[HBM] * 5,
        out_specs=(VM, VM),
        scratch_shapes=[pltpu.VMEM(array.shape, array.dtype) for array in (cells, counts, values, errors)]
        + [pltpu.SemaphoreType.DMA((5,))],
        compiler_params=limit(6),
    )(far(cells), far(counts), far(values), far(errors), far(states))


def one_hot(step, got_ref, group):
    cells = got_ref[group * BLK : (group + 1) * BLK, 2 * step + 1, 64 : 64 + CAP]
    lane = lax.broadcasted_iota(jnp.int32, (BLK, ROWS), 1)
    band = lax.broadcasted_iota(jnp.int32, (BLK, ROWS), 0)
    offset = (lane - band * WID).astype(f32)
    rows = [jnp.where(offset == cells[:, slot : slot + 1], 1.0, 0.0) for slot in range(CAP)]
    return jnp.concatenate(rows, axis=0)


def gather_kernel(got_ref, state_ref, out_far, out_ref, sems):
    copies = []
    for step in range(2):
        for pair in range(2):
            found = []
            for group in (2 * pair, 2 * pair + 1):
                field = state_ref[step, 0, group * BLK : (group + 1) * BLK].reshape(ROWS, CH)
                hot = one_hot(step, got_ref, group).astype(bf16)
                rows = jnp.dot(hot, field, preferred_element_type=f32)
                found.append(rows.reshape(CAP, BLK, CH))
            both = jnp.concatenate(found, axis=1).astype(bf16)
            out_ref[:, 2 * BLK * pair : 2 * BLK * (pair + 1), step * CH : (step + 1) * CH] = both
    for half in range(2):
        part = slice(half * CAP // 2, (half + 1) * CAP // 2)
        copies.append(pltpu.make_async_copy(out_ref.at[part], out_far.at[part], sems.at[half]))
        copies[-1].start()
    for copy in copies:
        copy.wait()


def gather_rows(got, states):
    return pl.pallas_call(
        gather_kernel,
        out_shape=pltpu.HBM((CAP, LAT, 2 * CH), bf16),
        out_specs=HBM,
        scratch_shapes=[pltpu.VMEM((CAP, LAT, 2 * CH), bf16), pltpu.SemaphoreType.DMA((2,))],
        compiler_params=limit(6),
        cost_estimate=pl.CostEstimate(flops=1000000, bytes_accessed=2000000, transcendentals=0),
    )(got, states)


def departure_kernel(rows_ref, got_ref, out_ref):
    for step in range(2):
        lanes = slice(step * CH, (step + 1) * CH)
        sampled = rows_ref[:, :, lanes].astype(f32)
        members = sampled.shape[0]
        other = got_ref[:, 2 * step + 1, :]
        values = jnp.concatenate([got_ref[:, 2 * step, :], other[:, 0:64]], axis=1)
        ens_mean = jnp.sum(sampled, axis=0) * (1.0 / members)
        ens_var = jnp.sum(sampled * sampled, axis=0) * (1.0 / members) - ens_mean * ens_mean
        weight = 1.0 / (other[:, 64 + CAP : 65 + CAP] + ens_var)
        ratio = (sampled - values[None]) * weight[None]
        live = other[:, 64 + 2 * CAP : 65 + 2 * CAP] >= 0.0
        out_ref[:, :, lanes] = jnp.where(live[None], ratio, 0.0).astype(bf16)


def departures(rows, got):
    return pl.pallas_call(
        departure_kernel,
        out_shape=jax.ShapeDtypeStruct((CAP, LAT, 2 * CH), bf16),
        compiler_params=limit(6),
        cost_estimate=pl.CostEstimate(flops=1200000, bytes_accessed=1200000, transcendentals=0),
    )(rows, got)


def cell_row(step, got_ref, group):
    cells = got_ref[group * BLK : (group + 1) * BLK, 2 * step + 1, 64 : 64 + CAP]
    band = lax.broadcasted_iota(jnp.int32, (BLK, CAP), 0).astype(f32)
    cells = jnp.where(cells < 0.0, -1.0, cells + band * WID)
    column = jnp.concatenate([cells[:, slot : slot + 1] for slot in range(CAP)], axis=0)
    return jnp.broadcast_to(column, (CAP * BLK, CAP * BLK)).T[0:1]


def forcing_of(step, rows_ref, cell_ref, group):
    place = step * (LAT // BLK) + group
    cells = jnp.broadcast_to(cell_ref[place : place + 1, :], (ROWS, CAP * BLK))
    cell = lax.broadcasted_iota(jnp.int32, (ROWS, CAP * BLK), 0).astype(f32)
    hot = jnp.where(cell == cells, 1.0, 0.0).astype(bf16)
    rows = rows_ref[:, :, step * CH : (step + 1) * CH].astype(f32)[:, group * BLK : (group + 1) * BLK]
    rows = rows.reshape(CAP * BLK, CH).astype(bf16)
    return jnp.dot(hot, rows, preferred_element_type=f32)


def normalise(hidden):
    centred = hidden - mean_lanes(hidden)
    inv_std = lax.rsqrt(mean_lanes(centred * centred) + norm_eps)
    return centred * inv_std, inv_std


def backward(adjoint, slope_at, down_ref, up_ref, gain, unit):
    adj_norm = jnp.zeros((ROWS, CH), f32)
    for part in range(3):
        cols = slice(part * 256, (part + 1) * 256)
        act = jnp.dot(adjoint, down_ref[:, cols], preferred_element_type=f32)
        pre = (act * slope_at(cols)).astype(bf16)
        adj_norm = adj_norm + lax.dot_general(pre, up_ref[:, cols], NT, preferred_element_type=f32)
    scaled = adj_norm * gain
    return scaled - mean_lanes(scaled) - unit * mean_lanes(scaled * unit)


def put_hidden(adj_hidden, first, out_ref, tail_ref, head_ref):
    block = adj_hidden.astype(bf16).reshape(BLK, WID, CH)
    out_ref[pl.ds(first, BLK)] = block
    head_ref[pl.ds(first, BLK)] = block[:, 0:3]
    tail_ref[pl.ds(first, BLK)] = block[:, WID - 3 : WID]


def forward_kernel(step, state_ref, left_ref, right_ref, kernel_ref, gain_ref, up_ref, bias_ref, *rest):
    low, high, twice, padded, hidden = rest[-5:]
    if step == 0:
        later_right, later_left = rest[5:7]
        later_right[...] = right_ref[1]
        later_left[...] = left_ref[1]
        right_ref, left_ref = right_ref.at[0], left_ref.at[0]
    gain = gain_ref[...]
    build_shifts(
        low, high, padded,
        lambda row: state_ref[step, 0, row],
        lambda row: left_ref[row],
        lambda row: right_ref[row],
    )

    def emit(row, start, stop, value):
        hidden[row, :, start:stop] = value

    convolve(low, high, twice, kernel_ref, False, emit)

    def block(index, carry):
        first = index * BLK
        unit, inv_std = normalise(hidden[pl.ds(first, BLK)].reshape(ROWS, CH))
        normed = (unit * gain).astype(bf16)

        def slope_at(cols):
            preact = jnp.dot(normed, up_ref[:, cols], preferred_element_type=f32)
            return gelu_slope(preact + bias_ref[:, cols]) * inv_std

        if step == 0:
            down_ref, adjoint_ref, hidden_out, tail_out, head_out = rest[:5]
            adjoint = adjoint_ref[0, pl.ds(first, BLK)].reshape(ROWS, CH)
            result = backward(adjoint, slope_at, down_ref, up_ref, gain, unit)
            put_hidden(result, first, hidden_out, tail_out, head_out)
        else:
            slope_out, unit_out = rest[:2]
            rows = pl.ds(pl.multiple_of(index * ROWS, ROWS), ROWS)
            for part in range(3):
                cols = slice(part * 256, (part + 1) * 256)
                slope_out[rows, cols] = slope_at(cols).astype(bf16)
            unit_out[rows, :] = unit.astype(bf16)
        return carry

    lax.fori_loop(0, LAT // BLK, block, 0)


FAR_EDGE = pltpu.HBM((LAT, 3, CH), bf16)
EDGE = jax.ShapeDtypeStruct((LAT, 3, CH), bf16)
FIELD = jax.ShapeDtypeStruct((LAT, WID, CH), bf16)
SHIFT_SCRATCH = [
    pltpu.VMEM((7, LAT + 6, WID, 128), f32),
    pltpu.VMEM((7, HALF + 6, WID, 128), f32),
    pltpu.VMEM((7, 8, 128), f32),
    pltpu.VMEM((UNROLL, WID + 8, 128), f32),
]


def forward(step, states, left, right, *others):
    shapes = (pltpu.HBM((LAT, WID, CH), bf16),) + (FAR_EDGE,) * 4 if step == 0 else (
        pltpu.HBM((CELLS, HID), bf16), pltpu.HBM((CELLS, CH), bf16)
    )
    return pl.pallas_call(
        functools.partial(forward_kernel, step),
        out_shape=shapes,
        out_specs=(VM,) * len(shapes),
        scratch_shapes=SHIFT_SCRATCH + [pltpu.VMEM((LAT, WID, CH), f32)],
        compiler_params=limit(16),
        cost_estimate=pl.CostEstimate(flops=6 * CELLS * CH * HID, bytes_accessed=8000000, transcendentals=CELLS * HID),
    )(states, left, right, *others)


def spread_kernel(
    hidden_ref, right_ref, left_ref, base_ref, kernel_ref, got_ref, slope_far,
    out_ref, slope_out, cell_out,
    low, high, twice, padded, sems,
):
    copies = fetch([(slope_far, slope_out)], sems)
    for step in range(2):
        for group in range(LAT // BLK):
            place = step * (LAT // BLK) + group
            cell_out[place : place + 1, :] = cell_row(step, got_ref, group)
    build_shifts(
        low, high, padded,
        lambda row: hidden_ref[row],
        lambda row: left_ref[row],
        lambda row: right_ref[row],
    )

    def emit(row, start, stop, value):
        out_ref[row, :, start:stop] = base_ref[0, row, :, start:stop].astype(f32) + value

    convolve(low, high, twice, kernel_ref, True, emit)
    for copy in copies:
        copy.wait()


def spread_back(hidden, right, left, base, kernel, got, slope):
    return pl.pallas_call(
        spread_kernel,
        out_shape=(
            jax.ShapeDtypeStruct((LAT, WID, CH), f32),
            jax.ShapeDtypeStruct(slope.shape, bf16),
            jax.ShapeDtypeStruct((2 * LAT // BLK, CAP * BLK), f32),
        ),
        in_specs=[VM] * 6 + [HBM],
        scratch_shapes=SHIFT_SCRATCH + [pltpu.SemaphoreType.DMA((1,))],
        compiler_params=limit(18),
        cost_estimate=pl.CostEstimate(flops=98 * CELLS * CH, bytes_accessed=3000000, transcendentals=0),
    )(hidden, right, left, base, kernel, got, far(slope))


def second_kernel(
    partial_ref, rows_ref, cell_ref, slope_ref, unit_far, gain_ref, up_ref, down_far,
    hidden_out, tail_out, head_out, adjoint_out, unit_ref, down_ref, sems,
):
    copies = fetch([(down_far, down_ref), (unit_far, unit_ref)], sems)
    gain = gain_ref[...]
    for group in range(LAT // BLK):
        first = group * BLK
        forcing = forcing_of(0, rows_ref, cell_ref, group)
        adjoint = (partial_ref[first : first + BLK].reshape(ROWS, CH) + forcing).astype(bf16)
        adjoint_out[first : first + BLK] = adjoint.reshape(BLK, WID, CH)
    for copy in copies:
        copy.wait()
    for group in range(LAT // BLK):
        first = group * BLK
        rows = slice(group * ROWS, (group + 1) * ROWS)
        result = backward(
            adjoint_out[first : first + BLK].reshape(ROWS, CH),
            lambda cols: slope_ref[rows, cols].astype(f32),
            down_ref, up_ref, gain,
            unit_ref[rows, :].astype(f32),
        )
        put_hidden(result, first, hidden_out, tail_out, head_out)


def second_step(partial, rows, hot, slope, unit, gain, up, down):
    return pl.pallas_call(
        second_kernel,
        out_shape=(FIELD, EDGE, EDGE, FIELD),
        in_specs=[VM] * 4 + [HBM, VM, VM, HBM],
        scratch_shapes=[pltpu.VMEM((CELLS, CH), bf16), pltpu.VMEM((CH, HID), bf16), pltpu.SemaphoreType.DMA((2,))],
        compiler_params=limit(8),
        cost_estimate=pl.CostEstimate(flops=4 * CELLS * CH * HID, bytes_accessed=5000000, transcendentals=0),
    )(partial, rows, hot, slope, far(unit), gain, up, far(down))


def interior_kernel(
    hidden_ref, adjoint_ref, rows_ref, hot_ref, kernel_ref, out_ref, west_ref, east_ref,
    low, high, twice, padded, total,
):
    build_shifts(low, high, padded, lambda row: hidden_ref[row])
    for group in range(LAT // BLK):
        first = group * BLK
        forcing = forcing_of(1, rows_ref, hot_ref, group).reshape(BLK, WID, CH)
        total[first : first + BLK] = adjoint_ref[first : first + BLK].astype(f32) + forcing

    def emit(row, start, stop, value):
        value = total[row, :, start:stop] + value
        out_ref[row, :, start:stop] = value.astype(bf16)
        west_ref[row, :, start:stop] = value[0:8]
        east_ref[row, :, start:stop] = value[WID - 8 : WID]

    convolve(low, high, twice, kernel_ref, True, emit)


STRIP = jax.ShapeDtypeStruct((LAT, 8, CH), f32)


def interior(hidden, adjoint, rows, hot, kernel):
    return pl.pallas_call(
        interior_kernel,
        out_shape=(FIELD, STRIP, STRIP),
        scratch_shapes=SHIFT_SCRATCH + [pltpu.VMEM((LAT, WID, CH), f32)],
        compiler_params=limit(16),
        cost_estimate=pl.CostEstimate(flops=98 * CELLS * CH, bytes_accessed=3000000, transcendentals=0),
    )(hidden, adjoint, rows, hot, kernel)


def edge_kernel(
    inner_ref, west_ref, east_ref, right_ref, left_ref, kernel_ref, out_ref,
    shifts, padded, taps, strips, sems,
):
    clear_rims(shifts, 3, 8)
    padded[...] = jnp.zeros(padded.shape, f32)
    west_side = lax.broadcasted_iota(jnp.int32, (8, CH), 0) < 4
    for row in range(7):
        for turn in range(3):
            first = jnp.broadcast_to(kernel_ref[6 - row, 6 - turn : 7 - turn, :], (8, CH))
            last = jnp.broadcast_to(kernel_ref[6 - row, 2 - turn : 3 - turn, :], (8, CH))
            taps[turn, row] = jnp.where(west_side, first, last)

    def some_rows(index, carry):
        for lane in range(BLK):
            padded[lane, 0:3] = left_ref[index * BLK + lane].astype(f32)
            padded[lane, 7:10] = right_ref[index * BLK + lane].astype(f32)
        for lane in range(BLK):
            for turn in range(3):
                shifts[turn, index * BLK + lane + 3] = padded[lane, turn : turn + 8]
        return carry

    lax.fori_loop(0, LAT // BLK, some_rows, 0)

    def block(index, carry):
        first = index * BLK
        for low, high in ((0, 128), (128, CH)):
            lanes = slice(low, high)
            sums = block_sums(shifts, first, lambda row, turn: taps[turn, row, :, lanes], range(3), lanes)
            side = west_side[:, lanes]
            for target in range(BLK):
                west = west_ref[first + target, :, lanes] + jnp.where(side, sums[target], 0.0)
                east = east_ref[first + target, :, lanes] + jnp.where(side, 0.0, sums[target])
                strips[0, first + target, :, lanes] = west.astype(bf16)
                strips[1, first + target, :, lanes] = east.astype(bf16)
        return carry

    lax.fori_loop(0, LAT // BLK, block, 0)
    places = [(strips.at[0], out_ref.at[:, 0:8]), (strips.at[1], out_ref.at[:, WID - 8 : WID])]
    for copy in fetch(places, sems):
        copy.wait()


def finish_edges(inner, west, east, left, right, kernel):
    return pl.pallas_call(
        edge_kernel,
        in_specs=[pl.BlockSpec(memory_space=pl.ANY)] + [VM] * 5,
        out_specs=pl.BlockSpec(memory_space=pl.ANY),
        out_shape=FIELD,
        input_output_aliases={0: 0},
        compiler_params=limit(4),
        scratch_shapes=[
            pltpu.VMEM((3, LAT + 6, 8, CH), f32), pltpu.VMEM((BLK, 16, CH), f32), pltpu.VMEM((3, 7, 8, CH), f32),
            pltpu.VMEM((2, LAT, 8, CH), bf16), pltpu.SemaphoreType.DMA((2,)),
        ],
        cost_estimate=pl.CostEstimate(flops=5000000, bytes_accessed=700000, transcendentals=0),
    )(inner, west, east, right, left, kernel)


def swap_edges(head, tail):
    peers = lax.axis_size("tile")
    up = [(i, (i + 1) % peers) for i in range(peers)]
    down = [(j, i) for i, j in up]
    right = lax.ppermute(head, "tile", down)
    left = lax.ppermute(tail, "tile", up)
    return left, right


def after(array, other):
    return lax.optimization_barrier((array, other))[0]


def exchange(array, axis):
    return lax.all_to_all(array, axis, split_axis=0, concat_axis=0, tiled=True)


def per_device(
    adjoint_final, states, kernel, norm_gain, up_weight, up_bias, down_weight,
    obs_cell, obs_count, obs_value, obs_error,
):
    gain = norm_gain[None]
    bias = up_bias[None]
    down = down_weight.T

    packed, near = pack_observations(
        obs_cell[:, 0].transpose(0, 2, 1), obs_count, obs_value, obs_error[:, 0].transpose(0, 2, 1), states
    )
    got = exchange(packed, "tile")
    rows = gather_rows(got, near)
    owned = exchange(rows, "member")

    source = after(states, rows)[:, 0]
    left, right = swap_edges(source[:, :, 0:3], source[:, :, WID - 3 : WID])
    hidden, tail, head, later_right, later_left = forward(
        0, states, left, right, kernel, gain, up_weight, bias, down, adjoint_final
    )
    deps = departures(after(owned, hidden), got)
    back = exchange(deps, "member")

    before, behind = swap_edges(*after((head, tail), deps))
    slope, unit = forward(1, after(states, deps), later_left, later_right, kernel, gain, up_weight, bias)
    partial, slope, cells = spread_back(
        hidden, after(behind, slope), before, adjoint_final, kernel, got, slope
    )

    hidden, tail, head, adjoint = second_step(
        partial, after(back, partial), cells, slope, unit, gain, up_weight, down
    )
    left, right = swap_edges(head, tail)
    inner, west, east = interior(hidden, adjoint, back, cells, kernel)
    return finish_edges(inner, west, east, left, right, kernel)[None]


def solution(mesh):
    placed = (
        P("member", None, "tile", None),
        P(None, "member", None, "tile", None),
        P(),
        P(),
        P(),
        P(),
        P(),
        P(None, "tile", None, None),
        P(None, "tile", None),
        P(None, "tile", None, None, None),
        P(None, "tile", None, None),
    )
    return jax.shard_map(
        per_device,
        mesh=mesh,
        in_specs=placed,
        out_specs=P("member", None, "tile", None),
        check_vma=False,
    )
```

```python
import functools
import math

import jax
import jax.numpy as jnp
from jax import lax
from jax.experimental import pallas as pl
from jax.experimental.pallas import tpu as pltpu
from jax.sharding import PartitionSpec as P

slope_coef = math.sqrt(2.0 / math.pi)
cubic_coef = 0.044715
norm_eps = 1e-06

LAT = 32
WID = 32
CH = 192
HID = 768
CAP = 16
CELLS = LAT * WID
SLOTS = LAT * CAP
BLK = 8
ROWS = BLK * WID
UNROLL = 4
HALF = LAT // 2
f32 = jnp.float32
bf16 = jnp.bfloat16
NT = (((1,), (1,)), ((), ()))
TN = (((0,), (0,)), ((), ()))


def gelu_slope(preact):
    square = preact * preact
    tanh_val = jnp.tanh(preact * (slope_coef + (slope_coef * cubic_coef) * square))
    tail = preact * (0.5 * slope_coef + (1.5 * slope_coef * cubic_coef) * square)
    return (0.5 + 0.5 * tanh_val) + tail * (1.0 - tanh_val * tanh_val)


def limit(mebibytes):
    return pltpu.CompilerParams(vmem_limit_bytes=mebibytes * 1024 * 1024)


def mean_lanes(value):
    return jnp.sum(value, axis=-1, keepdims=True) * (1.0 / CH)


HBM = pl.BlockSpec(memory_space=pltpu.HBM)
VM = pl.BlockSpec(memory_space=pltpu.VMEM)


def fetch(pairs, sems):
    copies = [pltpu.make_async_copy(src, dst, sems.at[i]) for i, (src, dst) in enumerate(pairs)]
    for copy in copies:
        copy.start()
    return copies


def far(array):
    return pltpu.with_memory_space_constraint(array, pltpu.HBM)


def clear_rims(shifts, count, width):
    for edge in range(3):
        zeros = jnp.zeros((width, CH), f32)
        for col in range(count):
            shifts[col, edge] = zeros
            shifts[col, LAT + 3 + edge] = zeros


def build_shifts(low, high, padded, centre, left=None, right=None):
    zeros = jnp.zeros((WID, 128), f32)
    for edge in range(3):
        for col in range(7):
            low[col, edge] = zeros
            low[col, LAT + 3 + edge] = zeros
    if left is None:
        padded[...] = jnp.zeros(padded.shape, f32)

    def spread_rows(rows, part, target, offset):
        for lane, row in enumerate(rows):
            if left is not None:
                padded[lane, 0:3] = part(left, row)
                padded[lane, WID + 3 : WID + 6] = part(right, row)
            padded[lane, 3 : WID + 3] = part(centre, row)
        for lane, row in enumerate(rows):
            for col in range(7):
                target[col, row + offset] = padded[lane, col : col + WID]

    def low_part(source, row):
        return source(row)[:, 0:128].astype(f32)

    def high_part(source, row):
        first = source(row - 3)[:, 128:CH].astype(f32) if not isinstance(row, int) or row >= 3 else None
        second = source(row + HALF - 3)[:, 128:CH].astype(f32) if not isinstance(row, int) or row < 19 else None
        first = jnp.zeros_like(second) if first is None else first
        second = jnp.zeros_like(first) if second is None else second
        return jnp.concatenate([first, second], axis=1)

    def some_low(index, carry):
        spread_rows([index * UNROLL + lane for lane in range(UNROLL)], low_part, low, 3)
        return carry

    def some_high(index, carry):
        spread_rows([index * UNROLL + lane + 3 for lane in range(UNROLL)], high_part, high, 0)
        return carry

    lax.fori_loop(0, LAT // UNROLL, some_low, 0)
    lax.fori_loop(0, HALF // UNROLL, some_high, 0)
    spread_rows([0, 1, 2], high_part, high, 0)
    spread_rows([19, 20, 21], high_part, high, 0)


def block_sums(shifts, first, tap, cols=range(7), lanes=slice(0, 128)):
    sums = [None] * BLK
    for place, col in enumerate(cols):
        taps = [tap(row, col) for row in range(7)]
        for source in range(BLK + 6):
            field = shifts[place, first + source, :, lanes]
            for row in range(7):
                target = source - row
                if 0 <= target < BLK:
                    term = taps[row] * field
                    sums[target] = term if sums[target] is None else sums[target] + term
    return sums


def tap_of(kernel_ref, flip, lanes, width):
    def tap(row, col):
        down, across = (6 - row, 6 - col) if flip else (row, col)
        value = kernel_ref[down, across : across + 1, lanes]
        return jnp.broadcast_to(value, (width, value.shape[1]))

    return tap


def convolve(low, high, twice, kernel_ref, flip, emit, done=None):
    for row in range(7):
        upper = kernel_ref[row, :, 128:CH]
        twice[row, 0:7] = jnp.concatenate([upper, upper], axis=1)

    def low_block(index, carry):
        first = index * BLK
        sums = block_sums(low, first, tap_of(kernel_ref, flip, slice(0, 128), WID))
        for target in range(BLK):
            emit(first + target, 0, 128, sums[target])
        return carry

    def high_block(index, carry):
        first = index * BLK
        sums = block_sums(high, first, tap_of(twice, flip, slice(0, 128), WID))
        for target in range(BLK):
            emit(first + target, 128, CH, sums[target][:, 0:64])
            emit(first + target + HALF, 128, CH, sums[target][:, 64:128])
        if done is not None:
            done(index)
        return carry

    lax.fori_loop(0, LAT // BLK, low_block, 0)
    lax.fori_loop(0, HALF // BLK, high_block, 0)


def pack_kernel(
    cell_far, count_far, value_far, error_far, state_far,
    out_ref, near_ref, cell_ref, count_ref, value_ref, error_ref, sems,
):
    pairs = [(cell_far, cell_ref), (count_far, count_ref), (value_far, value_ref), (error_far, error_ref)]
    copies = fetch(pairs + [(state_far, near_ref)], sems)
    for copy in copies[:4]:
        copy.wait()
    member = lax.axis_index("member")
    tiles = cell_ref.shape[2]
    slot = lax.broadcasted_iota(jnp.int32, (CAP, tiles), 0)
    across = lax.broadcasted_iota(jnp.int32, (CAP, CAP), 1)
    same = jnp.where(lax.broadcasted_iota(jnp.int32, (CAP, CAP), 0) == across, 1.0, 0.0).astype(bf16)
    own = jnp.where(lax.broadcasted_iota(jnp.int32, (CAP, CAP), 0) == member, 1.0, 0.0).astype(bf16)
    deep = lax.broadcasted_iota(jnp.int32, (tiles, CAP, CH), 1)
    for step in range(2):
        live = slot < count_ref[step]
        cells = jnp.where(live, cell_ref[step], -1).astype(f32).astype(bf16)
        values = jnp.sum(jnp.where(deep == member, value_ref[step, 0].astype(f32), 0.0), axis=1)
        turn = lambda array, pick: lax.dot_general(array, pick, TN, preferred_element_type=f32)
        out_ref[:, 2 * step, :] = values[:, 0:128]
        out_ref[:, 2 * step + 1, :] = jnp.concatenate(
            [values[:, 128:CH], turn(cells, same), turn(error_ref[step], own), turn(cells, own), jnp.zeros((tiles, CAP), f32)],
            axis=1)
    copies[4].wait()


def pack_observations(cells, counts, values, errors, states):
    return pl.pallas_call(
        pack_kernel,
        out_shape=(jax.ShapeDtypeStruct((cells.shape[2], 4, 128), f32), pltpu.VMEM(states.shape, bf16)),
        in_specs=[HBM] * 5,
        out_specs=(VM, VM),
        scratch_shapes=[pltpu.VMEM(array.shape, array.dtype) for array in (cells, counts, values, errors)]
        + [pltpu.SemaphoreType.DMA((5,))],
        compiler_params=limit(6),
    )(far(cells), far(counts), far(values), far(errors), far(states))


def one_hot(step, got_ref, group):
    cells = got_ref[group * BLK : (group + 1) * BLK, 2 * step + 1, 64 : 64 + CAP]
    lane = lax.broadcasted_iota(jnp.int32, (BLK, ROWS), 1)
    band = lax.broadcasted_iota(jnp.int32, (BLK, ROWS), 0)
    offset = (lane - band * WID).astype(f32)
    rows = [jnp.where(offset == cells[:, slot : slot + 1], 1.0, 0.0) for slot in range(CAP)]
    return jnp.concatenate(rows, axis=0)


def gather_kernel(got_ref, state_ref, out_far, out_ref, sems):
    copies = []
    for step in range(2):
        for pair in range(2):
            found = []
            for group in (2 * pair, 2 * pair + 1):
                field = state_ref[step, 0, group * BLK : (group + 1) * BLK].reshape(ROWS, CH)
                hot = one_hot(step, got_ref, group).astype(bf16)
                rows = jnp.dot(hot, field, preferred_element_type=f32)
                found.append(rows.reshape(CAP, BLK, CH))
            both = jnp.concatenate(found, axis=1).astype(bf16)
            out_ref[:, 2 * BLK * pair : 2 * BLK * (pair + 1), step * CH : (step + 1) * CH] = both
            if step == 1:
                part = slice(2 * BLK * pair, 2 * BLK * (pair + 1))
                copies.append(pltpu.make_async_copy(out_ref.at[:, part], out_far.at[:, part], sems.at[pair]))
                copies[-1].start()
    for copy in copies:
        copy.wait()


def gather_rows(got, states):
    return pl.pallas_call(
        gather_kernel,
        out_shape=pltpu.HBM((CAP, LAT, 2 * CH), bf16),
        out_specs=HBM,
        scratch_shapes=[pltpu.VMEM((CAP, LAT, 2 * CH), bf16), pltpu.SemaphoreType.DMA((2,))],
        compiler_params=limit(6),
        cost_estimate=pl.CostEstimate(flops=1000000, bytes_accessed=2000000, transcendentals=0),
    )(got, states)


def departure_kernel(rows_ref, got_ref, out_far, out_ref, sems):
    stats = []
    for step in range(2):
        sampled = rows_ref[:, :, step * CH : (step + 1) * CH].astype(f32)
        members = sampled.shape[0]
        other = got_ref[:, 2 * step + 1, :]
        values = jnp.concatenate([got_ref[:, 2 * step, :], other[:, 0:64]], axis=1)
        ens_mean = jnp.sum(sampled, axis=0) * (1.0 / members)
        ens_var = jnp.sum(sampled * sampled, axis=0) * (1.0 / members) - ens_mean * ens_mean
        weight = 1.0 / (other[:, 64 + CAP : 65 + CAP] + ens_var)
        stats.append((values, weight, other[:, 64 + 2 * CAP : 65 + 2 * CAP] >= 0.0))
    copies = []
    for half in range(2):
        part = slice(half * CAP // 2, (half + 1) * CAP // 2)
        for step, (values, weight, live) in enumerate(stats):
            lanes = slice(step * CH, (step + 1) * CH)
            ratio = (rows_ref[part, :, lanes].astype(f32) - values[None]) * weight[None]
            out_ref[part, :, lanes] = jnp.where(live[None], ratio, 0.0).astype(bf16)
        copies.append(pltpu.make_async_copy(out_ref.at[part], out_far.at[part], sems.at[half]))
        copies[-1].start()
    for copy in copies:
        copy.wait()


def departures(rows, got):
    return pl.pallas_call(
        departure_kernel,
        out_shape=pltpu.HBM((CAP, LAT, 2 * CH), bf16),
        out_specs=HBM,
        scratch_shapes=[pltpu.VMEM((CAP, LAT, 2 * CH), bf16), pltpu.SemaphoreType.DMA((2,))],
        compiler_params=limit(6),
        cost_estimate=pl.CostEstimate(flops=1200000, bytes_accessed=1200000, transcendentals=0),
    )(rows, got)


def cell_row(step, got_ref, group):
    cells = got_ref[group * BLK : (group + 1) * BLK, 2 * step + 1, 64 : 64 + CAP]
    band = lax.broadcasted_iota(jnp.int32, (BLK, CAP), 0).astype(f32)
    cells = jnp.where(cells < 0.0, -1.0, cells + band * WID)
    column = jnp.concatenate([cells[:, slot : slot + 1] for slot in range(CAP)], axis=0)
    return jnp.broadcast_to(column, (CAP * BLK, CAP * BLK)).T[0:1]


def forcing_of(step, rows_ref, cell_ref, group):
    place = step * (LAT // BLK) + group
    cells = jnp.broadcast_to(cell_ref[place : place + 1, :], (ROWS, CAP * BLK))
    cell = lax.broadcasted_iota(jnp.int32, (ROWS, CAP * BLK), 0).astype(f32)
    hot = jnp.where(cell == cells, 1.0, 0.0).astype(bf16)
    rows = rows_ref[:, :, step * CH : (step + 1) * CH].astype(f32)[:, group * BLK : (group + 1) * BLK]
    rows = rows.reshape(CAP * BLK, CH).astype(bf16)
    return jnp.dot(hot, rows, preferred_element_type=f32)


def normalise(hidden):
    centred = hidden - mean_lanes(hidden)
    inv_std = lax.rsqrt(mean_lanes(centred * centred) + norm_eps)
    return centred * inv_std, inv_std


def backward(adjoint, slope_at, down_ref, up_ref, gain, unit):
    adj_norm = jnp.zeros((ROWS, CH), f32)
    for part in range(3):
        cols = slice(part * 256, (part + 1) * 256)
        act = jnp.dot(adjoint, down_ref[:, cols], preferred_element_type=f32)
        pre = (act * slope_at(cols)).astype(bf16)
        adj_norm = adj_norm + lax.dot_general(pre, up_ref[:, cols], NT, preferred_element_type=f32)
    scaled = adj_norm * gain
    return scaled - mean_lanes(scaled) - unit * mean_lanes(scaled * unit)


def put_hidden(adj_hidden, first, out_ref, tail_ref, head_ref):
    block = adj_hidden.astype(bf16).reshape(BLK, WID, CH)
    out_ref[pl.ds(first, BLK)] = block
    head_ref[pl.ds(first, BLK)] = block[:, 0:3]
    tail_ref[pl.ds(first, BLK)] = block[:, WID - 3 : WID]


def forward_kernel(step, state_ref, left_ref, right_ref, kernel_ref, gain_ref, up_ref, bias_ref, *rest):
    low, high, twice, padded, hidden = rest[-5:]
    if step == 0:
        later_right, later_left = rest[5:7]
        later_right[...] = right_ref[1]
        later_left[...] = left_ref[1]
        right_ref, left_ref = right_ref.at[0], left_ref.at[0]
    gain = gain_ref[...]
    build_shifts(
        low, high, padded,
        lambda row: state_ref[step, 0, row],
        lambda row: left_ref[row],
        lambda row: right_ref[row],
    )

    def emit(row, start, stop, value):
        hidden[row, :, start:stop] = value

    convolve(low, high, twice, kernel_ref, False, emit)

    def block(index, carry):
        first = index * BLK
        unit, inv_std = normalise(hidden[pl.ds(first, BLK)].reshape(ROWS, CH))
        normed = (unit * gain).astype(bf16)

        def slope_at(cols):
            preact = jnp.dot(normed, up_ref[:, cols], preferred_element_type=f32)
            return gelu_slope(preact + bias_ref[:, cols]) * inv_std

        if step == 0:
            down_ref, adjoint_ref, hidden_out, tail_out, head_out = rest[:5]
            adjoint = adjoint_ref[0, pl.ds(first, BLK)].reshape(ROWS, CH)
            result = backward(adjoint, slope_at, down_ref, up_ref, gain, unit)
            put_hidden(result, first, hidden_out, tail_out, head_out)
        else:
            slope_out, unit_out = rest[:2]
            rows = pl.ds(pl.multiple_of(index * ROWS, ROWS), ROWS)
            for part in range(3):
                cols = slice(part * 256, (part + 1) * 256)
                slope_out[rows, cols] = slope_at(cols).astype(bf16)
            unit_out[rows, :] = unit.astype(bf16)
        return carry

    lax.fori_loop(0, LAT // BLK, block, 0)


FAR_EDGE = pltpu.HBM((LAT, 3, CH), bf16)
EDGE = jax.ShapeDtypeStruct((LAT, 3, CH), bf16)
FIELD = jax.ShapeDtypeStruct((LAT, WID, CH), bf16)
SHIFT_SCRATCH = [
    pltpu.VMEM((7, LAT + 6, WID, 128), f32),
    pltpu.VMEM((7, HALF + 6, WID, 128), f32),
    pltpu.VMEM((7, 8, 128), f32),
    pltpu.VMEM((UNROLL, WID + 8, 128), f32),
]


def forward(step, states, left, right, *others):
    shapes = (pltpu.HBM((LAT, WID, CH), bf16),) + (FAR_EDGE,) * 4 if step == 0 else (
        pltpu.HBM((CELLS, HID), bf16), pltpu.HBM((CELLS, CH), bf16)
    )
    return pl.pallas_call(
        functools.partial(forward_kernel, step),
        out_shape=shapes,
        out_specs=(VM,) * len(shapes),
        scratch_shapes=SHIFT_SCRATCH + [pltpu.VMEM((LAT, WID, CH), f32)],
        compiler_params=limit(16),
        cost_estimate=pl.CostEstimate(flops=6 * CELLS * CH * HID, bytes_accessed=8000000, transcendentals=CELLS * HID),
    )(states, left, right, *others)


def spread_kernel(
    hidden_ref, right_ref, left_ref, base_ref, kernel_ref, got_ref, slope_far,
    out_ref, slope_out, cell_out,
    low, high, twice, padded, sems,
):
    copies = fetch([(slope_far, slope_out)], sems)
    for step in range(2):
        for group in range(LAT // BLK):
            place = step * (LAT // BLK) + group
            cell_out[place : place + 1, :] = cell_row(step, got_ref, group)
    build_shifts(
        low, high, padded,
        lambda row: hidden_ref[row],
        lambda row: left_ref[row],
        lambda row: right_ref[row],
    )

    def emit(row, start, stop, value):
        out_ref[row, :, start:stop] = base_ref[0, row, :, start:stop].astype(f32) + value

    convolve(low, high, twice, kernel_ref, True, emit)
    for copy in copies:
        copy.wait()


def spread_back(hidden, right, left, base, kernel, got, slope):
    return pl.pallas_call(
        spread_kernel,
        out_shape=(
            jax.ShapeDtypeStruct((LAT, WID, CH), f32),
            jax.ShapeDtypeStruct(slope.shape, bf16),
            jax.ShapeDtypeStruct((2 * LAT // BLK, CAP * BLK), f32),
        ),
        in_specs=[VM] * 6 + [HBM],
        scratch_shapes=SHIFT_SCRATCH + [pltpu.SemaphoreType.DMA((1,))],
        compiler_params=limit(18),
        cost_estimate=pl.CostEstimate(flops=98 * CELLS * CH, bytes_accessed=3000000, transcendentals=0),
    )(hidden, right, left, base, kernel, got, far(slope))


def second_kernel(
    partial_ref, rows_ref, cell_ref, slope_ref, unit_far, gain_ref, up_ref, down_far,
    hidden_out, tail_out, head_out, adjoint_out, unit_ref, down_ref, sems,
):
    copies = fetch([(down_far, down_ref), (unit_far, unit_ref)], sems)
    gain = gain_ref[...]
    for group in range(LAT // BLK):
        first = group * BLK
        forcing = forcing_of(0, rows_ref, cell_ref, group)
        adjoint = (partial_ref[first : first + BLK].reshape(ROWS, CH) + forcing).astype(bf16)
        adjoint_out[first : first + BLK] = adjoint.reshape(BLK, WID, CH)
    for copy in copies:
        copy.wait()
    for group in range(LAT // BLK):
        first = group * BLK
        rows = slice(group * ROWS, (group + 1) * ROWS)
        result = backward(
            adjoint_out[first : first + BLK].reshape(ROWS, CH),
            lambda cols: slope_ref[rows, cols].astype(f32),
            down_ref, up_ref, gain,
            unit_ref[rows, :].astype(f32),
        )
        put_hidden(result, first, hidden_out, tail_out, head_out)


def second_step(partial, rows, hot, slope, unit, gain, up, down):
    return pl.pallas_call(
        second_kernel,
        out_shape=(FIELD, EDGE, EDGE, FIELD),
        in_specs=[VM] * 4 + [HBM, VM, VM, HBM],
        scratch_shapes=[pltpu.VMEM((CELLS, CH), bf16), pltpu.VMEM((CH, HID), bf16), pltpu.SemaphoreType.DMA((2,))],
        compiler_params=limit(8),
        cost_estimate=pl.CostEstimate(flops=4 * CELLS * CH * HID, bytes_accessed=5000000, transcendentals=0),
    )(partial, rows, hot, slope, far(unit), gain, up, far(down))


def interior_kernel(
    hidden_ref, adjoint_ref, rows_ref, hot_ref, kernel_ref, out_far, west_ref, east_ref,
    low, high, twice, padded, total, out_ref, sems,
):
    build_shifts(low, high, padded, lambda row: hidden_ref[row])
    for group in range(LAT // BLK):
        first = group * BLK
        forcing = forcing_of(1, rows_ref, hot_ref, group).reshape(BLK, WID, CH)
        total[first : first + BLK] = adjoint_ref[first : first + BLK].astype(f32) + forcing

    def emit(row, start, stop, value):
        value = total[row, :, start:stop] + value
        out_ref[row, :, start:stop] = value[8 : WID - 8].astype(bf16)
        west_ref[row, :, start:stop] = value[0:8]
        east_ref[row, :, start:stop] = value[WID - 8 : WID]

    def copy_of(first, place):
        rows = pl.ds(first, BLK)
        return pltpu.make_async_copy(out_ref.at[rows], out_far.at[rows, 8 : WID - 8], sems.at[place])

    def done(index):
        copy_of(index * BLK, index).start()
        copy_of(index * BLK + HALF, index + 2).start()

    convolve(low, high, twice, kernel_ref, True, emit, done)
    for place, first in enumerate((0, BLK, HALF, HALF + BLK)):
        copy_of(first, place).wait()


STRIP = jax.ShapeDtypeStruct((LAT, 8, CH), f32)


def interior(hidden, adjoint, rows, hot, kernel):
    return pl.pallas_call(
        interior_kernel,
        out_shape=(pltpu.HBM((LAT, WID, CH), bf16), STRIP, STRIP),
        out_specs=(HBM, VM, VM),
        scratch_shapes=SHIFT_SCRATCH + [
            pltpu.VMEM((LAT, WID, CH), f32), pltpu.VMEM((LAT, WID - 16, CH), bf16), pltpu.SemaphoreType.DMA((4,)),
        ],
        compiler_params=limit(16),
        cost_estimate=pl.CostEstimate(flops=98 * CELLS * CH, bytes_accessed=3000000, transcendentals=0),
    )(hidden, adjoint, rows, hot, kernel)


def edge_kernel(
    inner_ref, west_ref, east_ref, right_ref, left_ref, kernel_ref, out_ref,
    shifts, padded, taps, strips, sems,
):
    clear_rims(shifts, 3, 8)
    padded[...] = jnp.zeros(padded.shape, f32)
    west_side = lax.broadcasted_iota(jnp.int32, (8, CH), 0) < 4
    for row in range(7):
        for turn in range(3):
            first = jnp.broadcast_to(kernel_ref[6 - row, 6 - turn : 7 - turn, :], (8, CH))
            last = jnp.broadcast_to(kernel_ref[6 - row, 2 - turn : 3 - turn, :], (8, CH))
            taps[turn, row] = jnp.where(west_side, first, last)

    def some_rows(index, carry):
        for lane in range(BLK):
            padded[lane, 0:3] = left_ref[index * BLK + lane].astype(f32)
            padded[lane, 7:10] = right_ref[index * BLK + lane].astype(f32)
        for lane in range(BLK):
            for turn in range(3):
                shifts[turn, index * BLK + lane + 3] = padded[lane, turn : turn + 8]
        return carry

    lax.fori_loop(0, LAT // BLK, some_rows, 0)

    def block(index, carry):
        first = index * BLK
        for low, high in ((0, 128), (128, CH)):
            lanes = slice(low, high)
            sums = block_sums(shifts, first, lambda row, turn: taps[turn, row, :, lanes], range(3), lanes)
            side = west_side[:, lanes]
            for target in range(BLK):
                west = west_ref[first + target, :, lanes] + jnp.where(side, sums[target], 0.0)
                east = east_ref[first + target, :, lanes] + jnp.where(side, 0.0, sums[target])
                strips[0, first + target, :, lanes] = west.astype(bf16)
                strips[1, first + target, :, lanes] = east.astype(bf16)
        return carry

    lax.fori_loop(0, LAT // BLK, block, 0)
    places = [(strips.at[0], out_ref.at[:, 0:8]), (strips.at[1], out_ref.at[:, WID - 8 : WID])]
    for copy in fetch(places, sems):
        copy.wait()


def finish_edges(inner, west, east, left, right, kernel):
    return pl.pallas_call(
        edge_kernel,
        in_specs=[pl.BlockSpec(memory_space=pl.ANY)] + [VM] * 5,
        out_specs=pl.BlockSpec(memory_space=pl.ANY),
        out_shape=FIELD,
        input_output_aliases={0: 0},
        compiler_params=limit(4),
        scratch_shapes=[
            pltpu.VMEM((3, LAT + 6, 8, CH), f32), pltpu.VMEM((BLK, 16, CH), f32), pltpu.VMEM((3, 7, 8, CH), f32),
            pltpu.VMEM((2, LAT, 8, CH), bf16), pltpu.SemaphoreType.DMA((2,)),
        ],
        cost_estimate=pl.CostEstimate(flops=5000000, bytes_accessed=700000, transcendentals=0),
    )(inner, west, east, right, left, kernel)


def swap_edges(head, tail):
    peers = lax.axis_size("tile")
    up = [(i, (i + 1) % peers) for i in range(peers)]
    down = [(j, i) for i, j in up]
    right = lax.ppermute(head, "tile", down)
    left = lax.ppermute(tail, "tile", up)
    return left, right


def after(array, other):
    return lax.optimization_barrier((array, other))[0]


def exchange(array, axis):
    return lax.all_to_all(array, axis, split_axis=0, concat_axis=0, tiled=True)


def per_device(
    adjoint_final, states, kernel, norm_gain, up_weight, up_bias, down_weight,
    obs_cell, obs_count, obs_value, obs_error,
):
    gain = norm_gain[None]
    bias = up_bias[None]
    down = down_weight.T

    packed, near = pack_observations(
        obs_cell[:, 0].transpose(0, 2, 1), obs_count, obs_value, obs_error[:, 0].transpose(0, 2, 1), states
    )
    got = exchange(packed, "tile")
    rows = gather_rows(got, near)
    owned = exchange(rows, "member")

    source = after(states, rows)[:, 0]
    left, right = swap_edges(source[:, :, 0:3], source[:, :, WID - 3 : WID])
    hidden, tail, head, later_right, later_left = forward(
        0, states, left, right, kernel, gain, up_weight, bias, down, adjoint_final
    )
    deps = departures(after(owned, hidden), got)
    back = exchange(deps, "member")

    before, behind = swap_edges(*after((head, tail), deps))
    slope, unit = forward(1, after(states, deps), later_left, later_right, kernel, gain, up_weight, bias)
    partial, slope, cells = spread_back(
        hidden, after(behind, slope), before, adjoint_final, kernel, got, slope
    )

    hidden, tail, head, adjoint = second_step(
        partial, after(back, partial), cells, slope, unit, gain, up_weight, down
    )
    left, right = swap_edges(head, tail)
    inner, west, east = interior(hidden, adjoint, back, cells, kernel)
    return finish_edges(inner, west, east, left, right, kernel)[None]


def solution(mesh):
    placed = (
        P("member", None, "tile", None),
        P(None, "member", None, "tile", None),
        P(),
        P(),
        P(),
        P(),
        P(),
        P(None, "tile", None, None),
        P(None, "tile", None),
        P(None, "tile", None, None, None),
        P(None, "tile", None, None),
    )
    return jax.shard_map(
        per_device,
        mesh=mesh,
        in_specs=placed,
        out_specs=P("member", None, "tile", None),
        check_vma=False,
    )
```

```python
import functools
import math

import jax
import jax.numpy as jnp
from jax import lax
from jax.experimental import pallas as pl
from jax.experimental.pallas import tpu as pltpu
from jax.sharding import PartitionSpec as P

slope_coef = math.sqrt(2.0 / math.pi)
cubic_coef = 0.044715
norm_eps = 1e-06

LAT = 32
WID = 32
CH = 192
HID = 768
CAP = 16
CELLS = LAT * WID
SLOTS = LAT * CAP
BLK = 8
ROWS = BLK * WID
UNROLL = 4
HALF = LAT // 2
f32 = jnp.float32
bf16 = jnp.bfloat16
NT = (((1,), (1,)), ((), ()))
TN = (((0,), (0,)), ((), ()))


def gelu_slope(preact):
    square = preact * preact
    tanh_val = jnp.tanh(preact * (slope_coef + (slope_coef * cubic_coef) * square))
    tail = preact * (0.5 * slope_coef + (1.5 * slope_coef * cubic_coef) * square)
    return (0.5 + 0.5 * tanh_val) + tail * (1.0 - tanh_val * tanh_val)


def limit(mebibytes):
    return pltpu.CompilerParams(vmem_limit_bytes=mebibytes * 1024 * 1024)


def mean_lanes(value):
    return jnp.sum(value, axis=-1, keepdims=True) * (1.0 / CH)


HBM = pl.BlockSpec(memory_space=pltpu.HBM)
VM = pl.BlockSpec(memory_space=pltpu.VMEM)


def fetch(pairs, sems):
    copies = [pltpu.make_async_copy(src, dst, sems.at[i]) for i, (src, dst) in enumerate(pairs)]
    for copy in copies:
        copy.start()
    return copies


def far(array):
    return pltpu.with_memory_space_constraint(array, pltpu.HBM)


def clear_rims(shifts, count, width):
    for edge in range(3):
        zeros = jnp.zeros((width, CH), f32)
        for col in range(count):
            shifts[col, edge] = zeros
            shifts[col, LAT + 3 + edge] = zeros


def build_shifts(low, high, padded, centre, left=None, right=None):
    zeros = jnp.zeros((WID, 128), f32)
    for edge in range(3):
        for col in range(7):
            low[col, edge] = zeros
            low[col, LAT + 3 + edge] = zeros
    if left is None:
        padded[...] = jnp.zeros(padded.shape, f32)

    def spread_rows(rows, part, target, offset):
        for lane, row in enumerate(rows):
            if left is not None:
                padded[lane, 0:3] = part(left, row)
                padded[lane, WID + 3 : WID + 6] = part(right, row)
            padded[lane, 3 : WID + 3] = part(centre, row)
        for lane, row in enumerate(rows):
            for col in range(7):
                target[col, row + offset] = padded[lane, col : col + WID]

    def low_part(source, row):
        return source(row)[:, 0:128].astype(f32)

    def high_part(source, row):
        first = source(row - 3)[:, 128:CH].astype(f32) if not isinstance(row, int) or row >= 3 else None
        second = source(row + HALF - 3)[:, 128:CH].astype(f32) if not isinstance(row, int) or row < 19 else None
        first = jnp.zeros_like(second) if first is None else first
        second = jnp.zeros_like(first) if second is None else second
        return jnp.concatenate([first, second], axis=1)

    def some_low(index, carry):
        spread_rows([index * UNROLL + lane for lane in range(UNROLL)], low_part, low, 3)
        return carry

    def some_high(index, carry):
        spread_rows([index * UNROLL + lane + 3 for lane in range(UNROLL)], high_part, high, 0)
        return carry

    lax.fori_loop(0, LAT // UNROLL, some_low, 0)
    lax.fori_loop(0, HALF // UNROLL, some_high, 0)
    spread_rows([0, 1, 2], high_part, high, 0)
    spread_rows([19, 20, 21], high_part, high, 0)


def block_sums(shifts, first, tap, cols=range(7), lanes=slice(0, 128)):
    sums = [None] * BLK
    for place, col in enumerate(cols):
        taps = [tap(row, col) for row in range(7)]
        for source in range(BLK + 6):
            field = shifts[place, first + source, :, lanes]
            for row in range(7):
                target = source - row
                if 0 <= target < BLK:
                    term = taps[row] * field
                    sums[target] = term if sums[target] is None else sums[target] + term
    return sums


def tap_of(kernel_ref, flip, lanes, width):
    def tap(row, col):
        down, across = (6 - row, 6 - col) if flip else (row, col)
        value = kernel_ref[down, across : across + 1, lanes]
        return jnp.broadcast_to(value, (width, value.shape[1]))

    return tap


def convolve(low, high, twice, kernel_ref, flip, emit, done=None):
    for row in range(7):
        upper = kernel_ref[row, :, 128:CH]
        twice[row, 0:7] = jnp.concatenate([upper, upper], axis=1)

    def low_block(index, carry):
        first = index * BLK
        sums = block_sums(low, first, tap_of(kernel_ref, flip, slice(0, 128), WID))
        for target in range(BLK):
            emit(first + target, 0, 128, sums[target])
        return carry

    def high_block(index, carry):
        first = index * BLK
        sums = block_sums(high, first, tap_of(twice, flip, slice(0, 128), WID))
        for target in range(BLK):
            emit(first + target, 128, CH, sums[target][:, 0:64])
            emit(first + target + HALF, 128, CH, sums[target][:, 64:128])
        if done is not None:
            done(index)
        return carry

    lax.fori_loop(0, LAT // BLK, low_block, 0)
    lax.fori_loop(0, HALF // BLK, high_block, 0)


def pack_kernel(
    cell_far, count_far, value_far, error_far, state_far,
    out_ref, near_ref, cell_ref, count_ref, value_ref, error_ref, sems,
):
    pairs = [(cell_far, cell_ref), (count_far, count_ref), (value_far, value_ref), (error_far, error_ref)]
    copies = fetch(pairs + [(state_far, near_ref)], sems)
    for copy in copies[:4]:
        copy.wait()
    member = lax.axis_index("member")
    tiles = cell_ref.shape[2]
    slot = lax.broadcasted_iota(jnp.int32, (CAP, tiles), 0)
    across = lax.broadcasted_iota(jnp.int32, (CAP, CAP), 1)
    same = jnp.where(lax.broadcasted_iota(jnp.int32, (CAP, CAP), 0) == across, 1.0, 0.0).astype(bf16)
    own = jnp.where(lax.broadcasted_iota(jnp.int32, (CAP, CAP), 0) == member, 1.0, 0.0).astype(bf16)
    deep = lax.broadcasted_iota(jnp.int32, (tiles, CAP, CH), 1)
    for step in range(2):
        live = slot < count_ref[step]
        cells = jnp.where(live, cell_ref[step], -1).astype(f32).astype(bf16)
        values = jnp.sum(jnp.where(deep == member, value_ref[step, 0].astype(f32), 0.0), axis=1)
        turn = lambda array, pick: lax.dot_general(array, pick, TN, preferred_element_type=f32)
        out_ref[:, 2 * step, :] = values[:, 0:128]
        out_ref[:, 2 * step + 1, :] = jnp.concatenate(
            [values[:, 128:CH], turn(cells, same), turn(error_ref[step], own), turn(cells, own), jnp.zeros((tiles, CAP), f32)],
            axis=1)
    copies[4].wait()


def pack_observations(cells, counts, values, errors, states):
    return pl.pallas_call(
        pack_kernel,
        out_shape=(jax.ShapeDtypeStruct((cells.shape[2], 4, 128), f32), pltpu.VMEM(states.shape, bf16)),
        in_specs=[HBM] * 5,
        out_specs=(VM, VM),
        scratch_shapes=[pltpu.VMEM(array.shape, array.dtype) for array in (cells, counts, values, errors)]
        + [pltpu.SemaphoreType.DMA((5,))],
        compiler_params=limit(6),
    )(far(cells), far(counts), far(values), far(errors), far(states))


def one_hot(step, got_ref, group):
    cells = got_ref[group * BLK : (group + 1) * BLK, 2 * step + 1, 64 : 64 + CAP]
    lane = lax.broadcasted_iota(jnp.int32, (BLK, ROWS), 1)
    band = lax.broadcasted_iota(jnp.int32, (BLK, ROWS), 0)
    offset = (lane - band * WID).astype(f32)
    rows = [jnp.where(offset == cells[:, slot : slot + 1], 1.0, 0.0) for slot in range(CAP)]
    return jnp.concatenate(rows, axis=0)


def take_step(ref, step, members=slice(None)):
    first = ref[members, :, step * 128 : (step + 1) * 128]
    last = ref[members, :, 256 + step * 64 : 320 + step * 64]
    return jnp.concatenate([first.astype(f32), last.astype(f32)], axis=2)


def put_step(ref, step, members, bands, value):
    ref[members, bands, step * 128 : (step + 1) * 128] = value[:, :, 0:128]
    ref[members, bands, 256 + step * 64 : 320 + step * 64] = value[:, :, 128:CH]


def gather_kernel(got_ref, state_ref, out_far, out_ref, sems):
    copies = []
    for step in range(2):
        for pair in range(2):
            found = []
            for group in (2 * pair, 2 * pair + 1):
                field = state_ref[step, 0, group * BLK : (group + 1) * BLK].reshape(ROWS, CH)
                hot = one_hot(step, got_ref, group).astype(bf16)
                rows = jnp.dot(hot, field, preferred_element_type=f32)
                found.append(rows.reshape(CAP, BLK, CH))
            both = jnp.concatenate(found, axis=1).astype(bf16)
            put_step(out_ref, step, slice(None), slice(2 * BLK * pair, 2 * BLK * (pair + 1)), both)
            if step == 1:
                part = slice(2 * BLK * pair, 2 * BLK * (pair + 1))
                copies.append(pltpu.make_async_copy(out_ref.at[:, part], out_far.at[:, part], sems.at[pair]))
                copies[-1].start()
    for copy in copies:
        copy.wait()


def gather_rows(got, states):
    return pl.pallas_call(
        gather_kernel,
        out_shape=pltpu.HBM((CAP, LAT, 2 * CH), bf16),
        out_specs=HBM,
        scratch_shapes=[pltpu.VMEM((CAP, LAT, 2 * CH), bf16), pltpu.SemaphoreType.DMA((2,))],
        compiler_params=limit(6),
        cost_estimate=pl.CostEstimate(flops=1000000, bytes_accessed=2000000, transcendentals=0),
    )(got, states)


def departure_kernel(rows_ref, got_ref, out_far, out_ref, sems):
    stats = []
    for step in range(2):
        sampled = take_step(rows_ref, step)
        members = sampled.shape[0]
        other = got_ref[:, 2 * step + 1, :]
        values = jnp.concatenate([got_ref[:, 2 * step, :], other[:, 0:64]], axis=1)
        ens_mean = jnp.sum(sampled, axis=0) * (1.0 / members)
        ens_var = jnp.sum(sampled * sampled, axis=0) * (1.0 / members) - ens_mean * ens_mean
        weight = 1.0 / (other[:, 64 + CAP : 65 + CAP] + ens_var)
        stats.append((values, weight, other[:, 64 + 2 * CAP : 65 + 2 * CAP] >= 0.0))
    copies = []
    for half in range(2):
        part = slice(half * CAP // 2, (half + 1) * CAP // 2)
        for step, (values, weight, live) in enumerate(stats):
            ratio = (take_step(rows_ref, step, part) - values[None]) * weight[None]
            put_step(out_ref, step, part, slice(None), jnp.where(live[None], ratio, 0.0).astype(bf16))
        copies.append(pltpu.make_async_copy(out_ref.at[part], out_far.at[part], sems.at[half]))
        copies[-1].start()
    for copy in copies:
        copy.wait()


def departures(rows, got):
    return pl.pallas_call(
        departure_kernel,
        out_shape=pltpu.HBM((CAP, LAT, 2 * CH), bf16),
        out_specs=HBM,
        scratch_shapes=[pltpu.VMEM((CAP, LAT, 2 * CH), bf16), pltpu.SemaphoreType.DMA((2,))],
        compiler_params=limit(6),
        cost_estimate=pl.CostEstimate(flops=1200000, bytes_accessed=1200000, transcendentals=0),
    )(rows, got)


def cell_row(step, got_ref, group):
    cells = got_ref[group * BLK : (group + 1) * BLK, 2 * step + 1, 64 : 64 + CAP]
    band = lax.broadcasted_iota(jnp.int32, (BLK, CAP), 0).astype(f32)
    cells = jnp.where(cells < 0.0, -1.0, cells + band * WID)
    column = jnp.concatenate([cells[:, slot : slot + 1] for slot in range(CAP)], axis=0)
    return jnp.broadcast_to(column, (CAP * BLK, CAP * BLK)).T[0:1]


def forcing_of(step, rows_ref, cell_ref, group, cell=None):
    place = step * (LAT // BLK) + group
    if cell is None:
        cell = lax.broadcasted_iota(jnp.int32, (ROWS, CAP * BLK), 0).astype(f32)
    cells = jnp.broadcast_to(cell_ref[place : place + 1, :], cell.shape)
    hot = jnp.where(cell == cells, 1.0, 0.0).astype(bf16)
    rows = take_step(rows_ref, step)[:, group * BLK : (group + 1) * BLK]
    rows = rows.reshape(CAP * BLK, CH).astype(bf16)
    return jnp.dot(hot, rows, preferred_element_type=f32)


def normalise(hidden):
    centred = hidden - mean_lanes(hidden)
    inv_std = lax.rsqrt(mean_lanes(centred * centred) + norm_eps)
    return centred * inv_std, inv_std


def backward(adjoint, slope_at, down_ref, up_ref, gain, unit):
    adj_norm = jnp.zeros((ROWS, CH), f32)
    for part in range(3):
        cols = slice(part * 256, (part + 1) * 256)
        act = jnp.dot(adjoint, down_ref[:, cols], preferred_element_type=f32)
        pre = (act * slope_at(cols)).astype(bf16)
        adj_norm = adj_norm + lax.dot_general(pre, up_ref[:, cols], NT, preferred_element_type=f32)
    scaled = adj_norm * gain
    return scaled - mean_lanes(scaled) - unit * mean_lanes(scaled * unit)


def put_hidden(adj_hidden, first, out_ref, tail_ref, head_ref):
    block = adj_hidden.astype(bf16).reshape(BLK, WID, CH)
    out_ref[pl.ds(first, BLK)] = block
    head_ref[pl.ds(first, BLK)] = block[:, 0:3]
    tail_ref[pl.ds(first, BLK)] = block[:, WID - 3 : WID]


def forward_kernel(step, state_ref, left_ref, right_ref, kernel_ref, gain_ref, up_ref, bias_ref, *rest):
    low, high, twice, padded, hidden = rest[-5:]
    if step == 0:
        later_right, later_left = rest[5:7]
        later_right[...] = right_ref[1]
        later_left[...] = left_ref[1]
        right_ref, left_ref = right_ref.at[0], left_ref.at[0]
    gain = gain_ref[...]
    build_shifts(
        low, high, padded,
        lambda row: state_ref[step, 0, row],
        lambda row: left_ref[row],
        lambda row: right_ref[row],
    )

    def emit(row, start, stop, value):
        hidden[row, :, start:stop] = value

    convolve(low, high, twice, kernel_ref, False, emit)

    def block(index, carry):
        first = index * BLK
        unit, inv_std = normalise(hidden[pl.ds(first, BLK)].reshape(ROWS, CH))
        normed = (unit * gain).astype(bf16)

        def slope_at(cols):
            preact = jnp.dot(normed, up_ref[:, cols], preferred_element_type=f32)
            return gelu_slope(preact + bias_ref[:, cols]) * inv_std

        if step == 0:
            down_ref, adjoint_ref, hidden_out, tail_out, head_out = rest[:5]
            adjoint = adjoint_ref[0, pl.ds(first, BLK)].reshape(ROWS, CH)
            result = backward(adjoint, slope_at, down_ref, up_ref, gain, unit)
            put_hidden(result, first, hidden_out, tail_out, head_out)
        else:
            slope_out, unit_out = rest[:2]
            rows = pl.ds(pl.multiple_of(index * ROWS, ROWS), ROWS)
            for part in range(3):
                cols = slice(part * 256, (part + 1) * 256)
                slope_out[rows, cols] = slope_at(cols).astype(bf16)
            unit_out[rows, :] = unit.astype(bf16)
        return carry

    lax.fori_loop(0, LAT // BLK, block, 0)


FAR_EDGE = pltpu.HBM((LAT, 3, CH), bf16)
EDGE = jax.ShapeDtypeStruct((LAT, 3, CH), bf16)
FIELD = jax.ShapeDtypeStruct((LAT, WID, CH), bf16)
SHIFT_SCRATCH = [
    pltpu.VMEM((7, LAT + 6, WID, 128), f32),
    pltpu.VMEM((7, HALF + 6, WID, 128), f32),
    pltpu.VMEM((7, 8, 128), f32),
    pltpu.VMEM((UNROLL, WID + 8, 128), f32),
]


def forward(step, states, left, right, *others):
    shapes = (pltpu.HBM((LAT, WID, CH), bf16),) + (FAR_EDGE,) * 4 if step == 0 else (
        pltpu.HBM((CELLS, HID), bf16), pltpu.HBM((CELLS, CH), bf16)
    )
    return pl.pallas_call(
        functools.partial(forward_kernel, step),
        out_shape=shapes,
        out_specs=(VM,) * len(shapes),
        scratch_shapes=SHIFT_SCRATCH + [pltpu.VMEM((LAT, WID, CH), f32)],
        compiler_params=limit(16),
        cost_estimate=pl.CostEstimate(flops=6 * CELLS * CH * HID, bytes_accessed=8000000, transcendentals=CELLS * HID),
    )(states, left, right, *others)


def spread_kernel(
    hidden_ref, right_ref, left_ref, base_ref, kernel_ref, got_ref, slope_far,
    out_ref, slope_out, cell_out,
    low, high, twice, padded, sems,
):
    copies = fetch([(slope_far, slope_out)], sems)
    for step in range(2):
        for group in range(LAT // BLK):
            place = step * (LAT // BLK) + group
            cell_out[place : place + 1, :] = cell_row(step, got_ref, group)
    build_shifts(
        low, high, padded,
        lambda row: hidden_ref[row],
        lambda row: left_ref[row],
        lambda row: right_ref[row],
    )

    def emit(row, start, stop, value):
        out_ref[row, :, start:stop] = base_ref[0, row, :, start:stop].astype(f32) + value

    convolve(low, high, twice, kernel_ref, True, emit)
    for copy in copies:
        copy.wait()


def spread_back(hidden, right, left, base, kernel, got, slope):
    return pl.pallas_call(
        spread_kernel,
        out_shape=(
            jax.ShapeDtypeStruct((LAT, WID, CH), f32),
            jax.ShapeDtypeStruct(slope.shape, bf16),
            jax.ShapeDtypeStruct((2 * LAT // BLK, CAP * BLK), f32),
        ),
        in_specs=[VM] * 6 + [HBM],
        scratch_shapes=SHIFT_SCRATCH + [pltpu.SemaphoreType.DMA((1,))],
        compiler_params=limit(18),
        cost_estimate=pl.CostEstimate(flops=98 * CELLS * CH, bytes_accessed=3000000, transcendentals=0),
    )(hidden, right, left, base, kernel, got, far(slope))


STRIPS = {"edge": ((0, 8), (WID - 8, WID)), "middle": ((8, WID - 8),)}
DEEP = 2 * BLK


def second_kernel(
    part, partial_ref, rows_ref, cell_ref, slope_ref, unit_far, gain_ref, up_ref, down_far,
    hidden_out, adjoint_out, *rest,
):
    unit_ref, down_ref, sems = rest[-3:]
    strips = STRIPS[part]

    def pick(ref, first, lanes=slice(None)):
        found = [ref[first : first + DEEP, low:high, lanes] for low, high in strips]
        whole = found[0].astype(f32) if len(found) == 1 else jnp.concatenate([x.astype(f32) for x in found], axis=1)
        return whole.reshape(ROWS, whole.shape[2])

    copies = fetch([(down_far, down_ref), (unit_far, unit_ref)], sems)
    gain = gain_ref[...]
    row = lax.broadcasted_iota(jnp.int32, (CAP * BLK, CAP * BLK), 0)
    place = row % 16
    lon = jnp.where(place < 8, place, place + 16) if part == "edge" else place + 8
    cell = ((row // 16) * WID + lon).astype(f32)
    for index in range(LAT // DEEP):
        first = index * DEEP
        forcing = [forcing_of(0, rows_ref, cell_ref, 2 * index + half, cell) for half in range(2)]
        adjoint = (pick(partial_ref, first) + jnp.concatenate(forcing, axis=0)).astype(bf16)
        adjoint_out[first : first + DEEP] = adjoint.reshape(DEEP, 16, CH)
    for copy in copies:
        copy.wait()
    for index in range(LAT // DEEP):
        first = index * DEEP
        result = backward(
            adjoint_out[first : first + DEEP].reshape(ROWS, CH),
            lambda cols: pick(slope_ref, first, cols),
            down_ref, up_ref, gain,
            pick(unit_ref, first),
        )
        block = result.astype(bf16).reshape(DEEP, 16, CH)
        hidden_out[first : first + DEEP] = block
        if part == "edge":
            tail_out, head_out = rest[:2]
            head_out[first : first + DEEP] = block[:, 0:3]
            tail_out[first : first + DEEP] = block[:, 13:16]


def second_step(part, partial, rows, cells, slope, unit, gain, up, down):
    half = jax.ShapeDtypeStruct((LAT, 16, CH), bf16)
    return pl.pallas_call(
        functools.partial(second_kernel, part),
        out_shape=(half, half) + ((EDGE, EDGE) if part == "edge" else ()),
        in_specs=[VM] * 4 + [HBM, VM, VM, HBM],
        scratch_shapes=[pltpu.VMEM((LAT, WID, CH), bf16), pltpu.VMEM((CH, HID), bf16), pltpu.SemaphoreType.DMA((2,))],
        compiler_params=limit(8),
        cost_estimate=pl.CostEstimate(flops=2 * CELLS * CH * HID, bytes_accessed=2500000, transcendentals=0),
    )(partial, rows, cells, slope, far(unit), gain, up, far(down))


def interior_kernel(
    rim_ref, inner_ref, rim_adjoint, inner_adjoint, rows_ref, hot_ref, kernel_ref, out_far, west_ref, east_ref,
    low, high, twice, padded, total, out_ref, sems,
):
    def whole(rim, inner):
        axis = rim.ndim - 2
        first, last = lax.slice_in_dim(rim, 0, 8, axis=axis), lax.slice_in_dim(rim, 8, 16, axis=axis)
        return jnp.concatenate([first, inner, last], axis=axis)

    build_shifts(low, high, padded, lambda row: whole(rim_ref[row].astype(f32), inner_ref[row].astype(f32)))
    for group in range(LAT // BLK):
        first = group * BLK
        forcing = forcing_of(1, rows_ref, hot_ref, group).reshape(BLK, WID, CH)
        band = slice(first, first + BLK)
        total[band] = whole(rim_adjoint[band].astype(f32), inner_adjoint[band].astype(f32)) + forcing

    def emit(row, start, stop, value):
        value = total[row, :, start:stop] + value
        out_ref[row, :, start:stop] = value[8 : WID - 8].astype(bf16)
        west_ref[row, :, start:stop] = value[0:8]
        east_ref[row, :, start:stop] = value[WID - 8 : WID]

    def copy_of(first, place):
        rows = pl.ds(first, BLK)
        return pltpu.make_async_copy(out_ref.at[rows], out_far.at[rows, 8 : WID - 8], sems.at[place])

    def done(index):
        copy_of(index * BLK, index).start()
        copy_of(index * BLK + HALF, index + 2).start()

    convolve(low, high, twice, kernel_ref, True, emit, done)
    for place, first in enumerate((0, BLK, HALF, HALF + BLK)):
        copy_of(first, place).wait()


STRIP = jax.ShapeDtypeStruct((LAT, 8, CH), f32)


def interior(rim, inner, rim_adjoint, inner_adjoint, rows, hot, kernel):
    return pl.pallas_call(
        interior_kernel,
        out_shape=(pltpu.HBM((LAT, WID, CH), bf16), STRIP, STRIP),
        out_specs=(HBM, VM, VM),
        scratch_shapes=SHIFT_SCRATCH + [
            pltpu.VMEM((LAT, WID, CH), f32), pltpu.VMEM((LAT, WID - 16, CH), bf16), pltpu.SemaphoreType.DMA((4,)),
        ],
        compiler_params=limit(16),
        cost_estimate=pl.CostEstimate(flops=98 * CELLS * CH, bytes_accessed=3000000, transcendentals=0),
    )(rim, inner, rim_adjoint, inner_adjoint, rows, hot, kernel)


def edge_kernel(
    inner_ref, west_ref, east_ref, left_ref, right_ref, kernel_ref, out_ref,
    shifts, padded, taps, strips, sems,
):
    clear_rims(shifts, 3, 8)
    padded[...] = jnp.zeros(padded.shape, f32)
    west_side = lax.broadcasted_iota(jnp.int32, (8, CH), 0) < 4
    for row in range(7):
        for turn in range(3):
            first = jnp.broadcast_to(kernel_ref[6 - row, 6 - turn : 7 - turn, :], (8, CH))
            last = jnp.broadcast_to(kernel_ref[6 - row, 2 - turn : 3 - turn, :], (8, CH))
            taps[turn, row] = jnp.where(west_side, first, last)

    def some_rows(index, carry):
        for lane in range(BLK):
            padded[lane, 0:3] = left_ref[index * BLK + lane].astype(f32)
            padded[lane, 7:10] = right_ref[index * BLK + lane].astype(f32)
        for lane in range(BLK):
            for turn in range(3):
                shifts[turn, index * BLK + lane + 3] = padded[lane, turn : turn + 8]
        return carry

    lax.fori_loop(0, LAT // BLK, some_rows, 0)

    def block(index, carry):
        first = index * BLK
        for low, high in ((0, 128), (128, CH)):
            lanes = slice(low, high)
            sums = block_sums(shifts, first, lambda row, turn: taps[turn, row, :, lanes], range(3), lanes)
            side = west_side[:, lanes]
            for target in range(BLK):
                west = west_ref[first + target, :, lanes] + jnp.where(side, sums[target], 0.0)
                east = east_ref[first + target, :, lanes] + jnp.where(side, 0.0, sums[target])
                strips[0, first + target, :, lanes] = west.astype(bf16)
                strips[1, first + target, :, lanes] = east.astype(bf16)
        return carry

    lax.fori_loop(0, LAT // BLK, block, 0)
    places = [(strips.at[0], out_ref.at[:, 0:8]), (strips.at[1], out_ref.at[:, WID - 8 : WID])]
    for copy in fetch(places, sems):
        copy.wait()


def finish_edges(inner, west, east, left, right, kernel):
    return pl.pallas_call(
        edge_kernel,
        in_specs=[pl.BlockSpec(memory_space=pl.ANY)] + [VM] * 5,
        out_specs=pl.BlockSpec(memory_space=pl.ANY),
        out_shape=FIELD,
        input_output_aliases={0: 0},
        compiler_params=limit(4),
        scratch_shapes=[
            pltpu.VMEM((3, LAT + 6, 8, CH), f32), pltpu.VMEM((BLK, 16, CH), f32), pltpu.VMEM((3, 7, 8, CH), f32),
            pltpu.VMEM((2, LAT, 8, CH), bf16), pltpu.SemaphoreType.DMA((2,)),
        ],
        cost_estimate=pl.CostEstimate(flops=5000000, bytes_accessed=700000, transcendentals=0),
    )(inner, west, east, left, right, kernel)


def swap_edges(head, tail):
    peers = lax.axis_size("tile")
    up = [(i, (i + 1) % peers) for i in range(peers)]
    down = [(j, i) for i, j in up]
    right = lax.ppermute(head, "tile", down)
    left = lax.ppermute(tail, "tile", up)
    return left, right


def after(array, other):
    return lax.optimization_barrier((array, other))[0]


def exchange(array, axis):
    return lax.all_to_all(array, axis, split_axis=0, concat_axis=0, tiled=True)


def per_device(
    adjoint_final, states, kernel, norm_gain, up_weight, up_bias, down_weight,
    obs_cell, obs_count, obs_value, obs_error,
):
    gain = norm_gain[None]
    bias = up_bias[None]
    down = down_weight.T

    packed, near = pack_observations(
        obs_cell[:, 0].transpose(0, 2, 1), obs_count, obs_value, obs_error[:, 0].transpose(0, 2, 1), states
    )
    got = exchange(packed, "tile")
    rows = gather_rows(got, near)
    owned = exchange(rows, "member")

    source = after(states, rows)[:, 0]
    left, right = swap_edges(source[:, :, 0:3], source[:, :, WID - 3 : WID])
    hidden, tail, head, later_right, later_left = forward(
        0, states, left, right, kernel, gain, up_weight, bias, down, adjoint_final
    )
    deps = departures(after(owned, hidden), got)
    back = exchange(deps, "member")

    before, behind = swap_edges(*after((head, tail), deps))
    slope, unit = forward(1, after(states, deps), later_left, later_right, kernel, gain, up_weight, bias)
    partial, slope, cells = spread_back(
        hidden, after(behind, slope), before, adjoint_final, kernel, got, slope
    )

    back = after(back, partial)
    fields = (slope.reshape(LAT, WID, HID), unit.reshape(LAT, WID, CH), gain, up_weight, down)
    rim, rim_adjoint, tail, head = second_step("edge", partial, back, cells, *fields)
    left, right = swap_edges(head, tail)
    inner, inner_adjoint = second_step("middle", partial, after(back, tail), cells, *fields)
    field, west, east = interior(rim, inner, rim_adjoint, inner_adjoint, back, cells, kernel)
    return finish_edges(field, west, east, left, right, kernel)[None]


def solution(mesh):
    placed = (
        P("member", None, "tile", None),
        P(None, "member", None, "tile", None),
        P(),
        P(),
        P(),
        P(),
        P(),
        P(None, "tile", None, None),
        P(None, "tile", None),
        P(None, "tile", None, None, None),
        P(None, "tile", None, None),
    )
    return jax.shard_map(
        per_device,
        mesh=mesh,
        in_specs=placed,
        out_specs=P("member", None, "tile", None),
        check_vma=False,
    )
```

```python
import functools
import math

import jax
import jax.numpy as jnp
from jax import lax
from jax.experimental import pallas as pl
from jax.experimental.pallas import tpu as pltpu
from jax.sharding import PartitionSpec as P

slope_coef = math.sqrt(2.0 / math.pi)
cubic_coef = 0.044715
norm_eps = 1e-06

LAT = 32
WID = 32
CH = 192
HID = 768
CAP = 16
CELLS = LAT * WID
SLOTS = LAT * CAP
BLK = 8
ROWS = BLK * WID
UNROLL = 8
HALF = LAT // 2
f32 = jnp.float32
bf16 = jnp.bfloat16
NT = (((1,), (1,)), ((), ()))
TN = (((0,), (0,)), ((), ()))


def gelu_slope(preact):
    square = preact * preact
    tanh_val = jnp.tanh(preact * (slope_coef + (slope_coef * cubic_coef) * square))
    tail = preact * (0.5 * slope_coef + (1.5 * slope_coef * cubic_coef) * square)
    return (0.5 + 0.5 * tanh_val) + tail * (1.0 - tanh_val * tanh_val)


def limit(mebibytes):
    return pltpu.CompilerParams(vmem_limit_bytes=mebibytes * 1024 * 1024)


def mean_lanes(value):
    return jnp.sum(value, axis=-1, keepdims=True) * (1.0 / CH)


HBM = pl.BlockSpec(memory_space=pltpu.HBM)
VM = pl.BlockSpec(memory_space=pltpu.VMEM)


def fetch(pairs, sems):
    copies = [pltpu.make_async_copy(src, dst, sems.at[i]) for i, (src, dst) in enumerate(pairs)]
    for copy in copies:
        copy.start()
    return copies


def far(array):
    return pltpu.with_memory_space_constraint(array, pltpu.HBM)


def clear_rims(shifts, count, width):
    for edge in range(3):
        zeros = jnp.zeros((width, CH), f32)
        for col in range(count):
            shifts[col, edge] = zeros
            shifts[col, LAT + 3 + edge] = zeros


def build_shifts(low, high, padded, centre, left=None, right=None):
    zeros = jnp.zeros((WID, 128), f32)
    for edge in range(3):
        for col in range(7):
            low[col, edge] = zeros
            low[col, LAT + 3 + edge] = zeros
    if left is None:
        padded[...] = jnp.zeros(padded.shape, f32)

    def spread_rows(rows, part, target, offset):
        for lane, row in enumerate(rows):
            if left is not None:
                padded[lane, 0:3] = part(left, row)
                padded[lane, WID + 3 : WID + 6] = part(right, row)
            padded[lane, 3 : WID + 3] = part(centre, row)
        for lane, row in enumerate(rows):
            for col in range(7):
                target[col, row + offset] = padded[lane, col : col + WID]

    def low_part(source, row):
        return source(row)[:, 0:128].astype(f32)

    def high_part(source, row):
        first = source(row - 3)[:, 128:CH].astype(f32) if not isinstance(row, int) or row >= 3 else None
        second = source(row + HALF - 3)[:, 128:CH].astype(f32) if not isinstance(row, int) or row < 19 else None
        first = jnp.zeros_like(second) if first is None else first
        second = jnp.zeros_like(first) if second is None else second
        return jnp.concatenate([first, second], axis=1)

    def some_low(index, carry):
        spread_rows([index * UNROLL + lane for lane in range(UNROLL)], low_part, low, 3)
        return carry

    def some_high(index, carry):
        spread_rows([index * UNROLL + lane + 3 for lane in range(UNROLL)], high_part, high, 0)
        return carry

    lax.fori_loop(0, LAT // UNROLL, some_low, 0)
    lax.fori_loop(0, HALF // UNROLL, some_high, 0)
    spread_rows([0, 1, 2], high_part, high, 0)
    spread_rows([19, 20, 21], high_part, high, 0)


def block_sums(shifts, first, tap, cols=range(7), lanes=slice(0, 128)):
    sums = [None] * BLK
    for place, col in enumerate(cols):
        taps = [tap(row, col) for row in range(7)]
        for source in range(BLK + 6):
            field = shifts[place, first + source, :, lanes]
            for row in range(7):
                target = source - row
                if 0 <= target < BLK:
                    term = taps[row] * field
                    sums[target] = term if sums[target] is None else sums[target] + term
    return sums


def tap_of(kernel_ref, flip, lanes, width):
    def tap(row, col):
        down, across = (6 - row, 6 - col) if flip else (row, col)
        value = kernel_ref[down, across : across + 1, lanes]
        return jnp.broadcast_to(value, (width, value.shape[1]))

    return tap


def convolve(low, high, twice, kernel_ref, flip, emit, done=None):
    for row in range(7):
        upper = kernel_ref[row, :, 128:CH]
        twice[row, 0:7] = jnp.concatenate([upper, upper], axis=1)

    def low_block(index, carry):
        first = index * BLK
        sums = block_sums(low, first, tap_of(kernel_ref, flip, slice(0, 128), WID))
        for target in range(BLK):
            emit(first + target, 0, 128, sums[target])
        return carry

    def high_block(index, carry):
        first = index * BLK
        sums = block_sums(high, first, tap_of(twice, flip, slice(0, 128), WID))
        for target in range(BLK):
            emit(first + target, 128, CH, sums[target][:, 0:64])
            emit(first + target + HALF, 128, CH, sums[target][:, 64:128])
        if done is not None:
            done(index)
        return carry

    lax.fori_loop(0, LAT // BLK, low_block, 0)
    lax.fori_loop(0, HALF // BLK, high_block, 0)


def pack_kernel(
    cell_far, count_far, value_far, error_far, state_far,
    out_ref, near_ref, cell_ref, count_ref, value_ref, error_ref, sems,
):
    member = lax.axis_index("member")
    base = pl.multiple_of(member // 8 * 8, 8)
    near_slots = value_far.at[:, :, :, pl.ds(base, 8), :]
    pairs = [(cell_far, cell_ref), (count_far, count_ref), (near_slots, value_ref), (error_far, error_ref)]
    copies = fetch(pairs + [(state_far, near_ref)], sems)
    for copy in copies[:4]:
        copy.wait()
    tiles = cell_ref.shape[2]
    slot = lax.broadcasted_iota(jnp.int32, (CAP, tiles), 0)
    across = lax.broadcasted_iota(jnp.int32, (CAP, CAP), 1)
    same = jnp.where(lax.broadcasted_iota(jnp.int32, (CAP, CAP), 0) == across, 1.0, 0.0).astype(bf16)
    own = jnp.where(lax.broadcasted_iota(jnp.int32, (CAP, CAP), 0) == member, 1.0, 0.0).astype(bf16)
    deep = lax.broadcasted_iota(jnp.int32, (tiles, 8, CH), 1) + base
    for step in range(2):
        live = slot < count_ref[step]
        cells = jnp.where(live, cell_ref[step], -1).astype(f32).astype(bf16)
        values = jnp.sum(jnp.where(deep == member, value_ref[step, 0].astype(f32), 0.0), axis=1)
        turn = lambda array, pick: lax.dot_general(array, pick, TN, preferred_element_type=f32)
        out_ref[:, 2 * step, :] = values[:, 0:128]
        out_ref[:, 2 * step + 1, :] = jnp.concatenate(
            [values[:, 128:CH], turn(cells, same), turn(error_ref[step], own), turn(cells, own), jnp.zeros((tiles, CAP), f32)],
            axis=1)
    copies[4].wait()


def pack_observations(cells, counts, values, errors, states):
    return pl.pallas_call(
        pack_kernel,
        out_shape=(jax.ShapeDtypeStruct((cells.shape[2], 4, 128), f32), pltpu.VMEM(states.shape, bf16)),
        in_specs=[HBM] * 5,
        out_specs=(VM, VM),
        scratch_shapes=[pltpu.VMEM(array.shape, array.dtype) for array in (cells, counts, values[:, :, :, :8], errors)]
        + [pltpu.SemaphoreType.DMA((5,))],
        compiler_params=limit(6),
    )(far(cells), far(counts), far(values), far(errors), far(states))


def one_hot(step, got_ref, group):
    cells = got_ref[group * BLK : (group + 1) * BLK, 2 * step + 1, 64 : 64 + CAP]
    lane = lax.broadcasted_iota(jnp.int32, (BLK, ROWS), 1)
    band = lax.broadcasted_iota(jnp.int32, (BLK, ROWS), 0)
    offset = (lane - band * WID).astype(f32)
    rows = [jnp.where(offset == cells[:, slot : slot + 1], 1.0, 0.0) for slot in range(CAP)]
    return jnp.concatenate(rows, axis=0)


def gather_kernel(got_ref, state_ref, out_far, out_ref, sems):
    copies = []
    for step in range(2):
        for pair in range(2):
            found = []
            for group in (2 * pair, 2 * pair + 1):
                field = state_ref[step, 0, group * BLK : (group + 1) * BLK].reshape(ROWS, CH)
                hot = one_hot(step, got_ref, group).astype(bf16)
                rows = jnp.dot(hot, field, preferred_element_type=f32)
                found.append(rows.reshape(CAP, BLK, CH))
            both = jnp.concatenate(found, axis=1).astype(bf16)
            out_ref[:, 2 * BLK * pair : 2 * BLK * (pair + 1), step * CH : (step + 1) * CH] = both
            if step == 1:
                part = slice(2 * BLK * pair, 2 * BLK * (pair + 1))
                copies.append(pltpu.make_async_copy(out_ref.at[:, part], out_far.at[:, part], sems.at[pair]))
                copies[-1].start()
    for copy in copies:
        copy.wait()


def gather_rows(got, states):
    return pl.pallas_call(
        gather_kernel,
        out_shape=pltpu.HBM((CAP, LAT, 2 * CH), bf16),
        out_specs=HBM,
        scratch_shapes=[pltpu.VMEM((CAP, LAT, 2 * CH), bf16), pltpu.SemaphoreType.DMA((2,))],
        compiler_params=limit(6),
        cost_estimate=pl.CostEstimate(flops=1000000, bytes_accessed=2000000, transcendentals=0),
    )(got, states)


def departure_kernel(rows_ref, got_ref, out_far, out_ref, sems):
    stats = []
    for step in range(2):
        sampled = rows_ref[:, :, step * CH : (step + 1) * CH].astype(f32)
        members = sampled.shape[0]
        other = got_ref[:, 2 * step + 1, :]
        values = jnp.concatenate([got_ref[:, 2 * step, :], other[:, 0:64]], axis=1)
        ens_mean = jnp.sum(sampled, axis=0) * (1.0 / members)
        ens_var = jnp.sum(sampled * sampled, axis=0) * (1.0 / members) - ens_mean * ens_mean
        weight = 1.0 / (other[:, 64 + CAP : 65 + CAP] + ens_var)
        stats.append((values, weight, other[:, 64 + 2 * CAP : 65 + 2 * CAP] >= 0.0))
    copies = []
    for half in range(2):
        part = slice(half * CAP // 2, (half + 1) * CAP // 2)
        for step, (values, weight, live) in enumerate(stats):
            lanes = slice(step * CH, (step + 1) * CH)
            ratio = (rows_ref[part, :, lanes].astype(f32) - values[None]) * weight[None]
            out_ref[part, :, lanes] = jnp.where(live[None], ratio, 0.0).astype(bf16)
        copies.append(pltpu.make_async_copy(out_ref.at[part], out_far.at[part], sems.at[half]))
        copies[-1].start()
    for copy in copies:
        copy.wait()


def departures(rows, got):
    return pl.pallas_call(
        departure_kernel,
        out_shape=pltpu.HBM((CAP, LAT, 2 * CH), bf16),
        out_specs=HBM,
        scratch_shapes=[pltpu.VMEM((CAP, LAT, 2 * CH), bf16), pltpu.SemaphoreType.DMA((2,))],
        compiler_params=limit(6),
        cost_estimate=pl.CostEstimate(flops=1200000, bytes_accessed=1200000, transcendentals=0),
    )(rows, got)


def cell_row(step, got_ref, group):
    cells = got_ref[group * BLK : (group + 1) * BLK, 2 * step + 1, 64 : 64 + CAP]
    band = lax.broadcasted_iota(jnp.int32, (BLK, CAP), 0).astype(f32)
    cells = jnp.where(cells < 0.0, -1.0, cells + band * WID)
    column = jnp.concatenate([cells[:, slot : slot + 1] for slot in range(CAP)], axis=0)
    return jnp.broadcast_to(column, (CAP * BLK, CAP * BLK)).T[0:1]


def forcing_of(step, rows_ref, cell_ref, group):
    place = step * (LAT // BLK) + group
    cells = jnp.broadcast_to(cell_ref[place : place + 1, :], (ROWS, CAP * BLK))
    cell = lax.broadcasted_iota(jnp.int32, (ROWS, CAP * BLK), 0).astype(f32)
    hot = jnp.where(cell == cells, 1.0, 0.0).astype(bf16)
    rows = rows_ref[:, :, step * CH : (step + 1) * CH].astype(f32)[:, group * BLK : (group + 1) * BLK]
    rows = rows.reshape(CAP * BLK, CH).astype(bf16)
    return jnp.dot(hot, rows, preferred_element_type=f32)


def normalise(hidden):
    centred = hidden - mean_lanes(hidden)
    inv_std = lax.rsqrt(mean_lanes(centred * centred) + norm_eps)
    return centred * inv_std, inv_std


def backward(adjoint, slope_at, down_ref, up_ref, gain, unit):
    adj_norm = jnp.zeros((ROWS, CH), f32)
    for part in range(3):
        cols = slice(part * 256, (part + 1) * 256)
        act = jnp.dot(adjoint, down_ref[:, cols], preferred_element_type=f32)
        pre = (act * slope_at(cols)).astype(bf16)
        adj_norm = adj_norm + lax.dot_general(pre, up_ref[:, cols], NT, preferred_element_type=f32)
    scaled = adj_norm * gain
    return scaled - mean_lanes(scaled) - unit * mean_lanes(scaled * unit)


def put_hidden(adj_hidden, first, out_ref, tail_ref, head_ref):
    block = adj_hidden.astype(bf16).reshape(BLK, WID, CH)
    out_ref[pl.ds(first, BLK)] = block
    head_ref[pl.ds(first, BLK)] = block[:, 0:3]
    tail_ref[pl.ds(first, BLK)] = block[:, WID - 3 : WID]


def forward_kernel(step, state_ref, left_ref, right_ref, kernel_ref, gain_ref, up_ref, bias_ref, *rest):
    low, high, twice, padded, hidden = rest[-5:]
    if step == 0:
        later_right, later_left = rest[5:7]
        later_right[...] = right_ref[1]
        later_left[...] = left_ref[1]
        right_ref, left_ref = right_ref.at[0], left_ref.at[0]
    gain = gain_ref[...]
    build_shifts(
        low, high, padded,
        lambda row: state_ref[step, 0, row],
        lambda row: left_ref[row],
        lambda row: right_ref[row],
    )

    def emit(row, start, stop, value):
        hidden[row, :, start:stop] = value

    convolve(low, high, twice, kernel_ref, False, emit)

    def block(index, carry):
        first = index * BLK
        unit, inv_std = normalise(hidden[pl.ds(first, BLK)].reshape(ROWS, CH))
        normed = (unit * gain).astype(bf16)

        def slope_at(cols):
            preact = jnp.dot(normed, up_ref[:, cols], preferred_element_type=f32)
            return gelu_slope(preact + bias_ref[:, cols]) * inv_std

        if step == 0:
            down_ref, adjoint_ref, hidden_out, tail_out, head_out = rest[:5]
            adjoint = adjoint_ref[0, pl.ds(first, BLK)].reshape(ROWS, CH)
            result = backward(adjoint, slope_at, down_ref, up_ref, gain, unit)
            put_hidden(result, first, hidden_out, tail_out, head_out)
        else:
            slope_out, unit_out = rest[:2]
            rows = pl.ds(pl.multiple_of(index * ROWS, ROWS), ROWS)
            for part in range(3):
                cols = slice(part * 256, (part + 1) * 256)
                slope_out[rows, cols] = slope_at(cols).astype(bf16)
            unit_out[rows, :] = unit.astype(bf16)
        return carry

    lax.fori_loop(0, LAT // BLK, block, 0)


FAR_EDGE = pltpu.HBM((LAT, 3, CH), bf16)
EDGE = jax.ShapeDtypeStruct((LAT, 3, CH), bf16)
FIELD = jax.ShapeDtypeStruct((LAT, WID, CH), bf16)
SHIFT_SCRATCH = [
    pltpu.VMEM((7, LAT + 6, WID, 128), f32),
    pltpu.VMEM((7, HALF + 6, WID, 128), f32),
    pltpu.VMEM((7, 8, 128), f32),
    pltpu.VMEM((UNROLL, WID + 8, 128), f32),
]


def forward(step, states, left, right, *others):
    shapes = (pltpu.HBM((LAT, WID, CH), bf16),) + (FAR_EDGE,) * 4 if step == 0 else (
        pltpu.HBM((CELLS, HID), bf16), pltpu.HBM((CELLS, CH), bf16)
    )
    return pl.pallas_call(
        functools.partial(forward_kernel, step),
        out_shape=shapes,
        out_specs=(VM,) * len(shapes),
        scratch_shapes=SHIFT_SCRATCH + [pltpu.VMEM((LAT, WID, CH), f32)],
        compiler_params=limit(16),
        cost_estimate=pl.CostEstimate(flops=6 * CELLS * CH * HID, bytes_accessed=8000000, transcendentals=CELLS * HID),
    )(states, left, right, *others)


def spread_kernel(
    hidden_ref, right_ref, left_ref, base_ref, kernel_ref, got_ref, slope_far,
    out_ref, slope_out, cell_out,
    low, high, twice, padded, sems,
):
    copies = fetch([(slope_far, slope_out)], sems)
    for step in range(2):
        for group in range(LAT // BLK):
            place = step * (LAT // BLK) + group
            cell_out[place : place + 1, :] = cell_row(step, got_ref, group)
    build_shifts(
        low, high, padded,
        lambda row: hidden_ref[row],
        lambda row: left_ref[row],
        lambda row: right_ref[row],
    )

    def emit(row, start, stop, value):
        out_ref[row, :, start:stop] = base_ref[0, row, :, start:stop].astype(f32) + value

    convolve(low, high, twice, kernel_ref, True, emit)
    for copy in copies:
        copy.wait()


def spread_back(hidden, right, left, base, kernel, got, slope):
    return pl.pallas_call(
        spread_kernel,
        out_shape=(
            jax.ShapeDtypeStruct((LAT, WID, CH), f32),
            jax.ShapeDtypeStruct(slope.shape, bf16),
            jax.ShapeDtypeStruct((2 * LAT // BLK, CAP * BLK), f32),
        ),
        in_specs=[VM] * 6 + [HBM],
        scratch_shapes=SHIFT_SCRATCH + [pltpu.SemaphoreType.DMA((1,))],
        compiler_params=limit(18),
        cost_estimate=pl.CostEstimate(flops=98 * CELLS * CH, bytes_accessed=3000000, transcendentals=0),
    )(hidden, right, left, base, kernel, got, far(slope))


def second_kernel(
    partial_ref, rows_ref, cell_ref, slope_ref, unit_far, gain_ref, up_ref, down_far,
    hidden_out, tail_out, head_out, adjoint_out, unit_ref, down_ref, sems,
):
    copies = fetch([(down_far, down_ref), (unit_far, unit_ref)], sems)
    gain = gain_ref[...]
    for group in range(LAT // BLK):
        first = group * BLK
        forcing = forcing_of(0, rows_ref, cell_ref, group)
        adjoint = (partial_ref[first : first + BLK].reshape(ROWS, CH) + forcing).astype(bf16)
        adjoint_out[first : first + BLK] = adjoint.reshape(BLK, WID, CH)
    for copy in copies:
        copy.wait()
    for group in range(LAT // BLK):
        first = group * BLK
        rows = slice(group * ROWS, (group + 1) * ROWS)
        result = backward(
            adjoint_out[first : first + BLK].reshape(ROWS, CH),
            lambda cols: slope_ref[rows, cols].astype(f32),
            down_ref, up_ref, gain,
            unit_ref[rows, :].astype(f32),
        )
        put_hidden(result, first, hidden_out, tail_out, head_out)


def second_step(partial, rows, hot, slope, unit, gain, up, down):
    return pl.pallas_call(
        second_kernel,
        out_shape=(FIELD, EDGE, EDGE, FIELD),
        in_specs=[VM] * 4 + [HBM, VM, VM, HBM],
        scratch_shapes=[pltpu.VMEM((CELLS, CH), bf16), pltpu.VMEM((CH, HID), bf16), pltpu.SemaphoreType.DMA((2,))],
        compiler_params=limit(8),
        cost_estimate=pl.CostEstimate(flops=4 * CELLS * CH * HID, bytes_accessed=5000000, transcendentals=0),
    )(partial, rows, hot, slope, far(unit), gain, up, far(down))


def interior_kernel(
    hidden_ref, adjoint_ref, rows_ref, hot_ref, kernel_ref, out_far, west_ref, east_ref,
    low, high, twice, padded, total, out_ref, sems,
):
    build_shifts(low, high, padded, lambda row: hidden_ref[row])
    for group in range(LAT // BLK):
        first = group * BLK
        forcing = forcing_of(1, rows_ref, hot_ref, group).reshape(BLK, WID, CH)
        total[first : first + BLK] = adjoint_ref[first : first + BLK].astype(f32) + forcing

    def emit(row, start, stop, value):
        value = total[row, :, start:stop] + value
        out_ref[row, :, start:stop] = value[8 : WID - 8].astype(bf16)
        west_ref[row, :, start:stop] = value[0:8]
        east_ref[row, :, start:stop] = value[WID - 8 : WID]

    def copy_of(first, place):
        rows = pl.ds(first, BLK)
        return pltpu.make_async_copy(out_ref.at[rows], out_far.at[rows, 8 : WID - 8], sems.at[place])

    def done(index):
        copy_of(index * BLK, index).start()
        copy_of(index * BLK + HALF, index + 2).start()

    convolve(low, high, twice, kernel_ref, True, emit, done)
    for place, first in enumerate((0, BLK, HALF, HALF + BLK)):
        copy_of(first, place).wait()


STRIP = jax.ShapeDtypeStruct((LAT, 8, CH), f32)


def interior(hidden, adjoint, rows, hot, kernel):
    return pl.pallas_call(
        interior_kernel,
        out_shape=(pltpu.HBM((LAT, WID, CH), bf16), STRIP, STRIP),
        out_specs=(HBM, VM, VM),
        scratch_shapes=SHIFT_SCRATCH + [
            pltpu.VMEM((LAT, WID, CH), f32), pltpu.VMEM((LAT, WID - 16, CH), bf16), pltpu.SemaphoreType.DMA((4,)),
        ],
        compiler_params=limit(16),
        cost_estimate=pl.CostEstimate(flops=98 * CELLS * CH, bytes_accessed=3000000, transcendentals=0),
    )(hidden, adjoint, rows, hot, kernel)


def edge_kernel(
    inner_ref, west_ref, east_ref, right_ref, left_ref, kernel_ref, out_ref,
    shifts, padded, taps, strips, sems,
):
    clear_rims(shifts, 3, 8)
    padded[...] = jnp.zeros(padded.shape, f32)
    west_side = lax.broadcasted_iota(jnp.int32, (8, CH), 0) < 4
    for row in range(7):
        for turn in range(3):
            first = jnp.broadcast_to(kernel_ref[6 - row, 6 - turn : 7 - turn, :], (8, CH))
            last = jnp.broadcast_to(kernel_ref[6 - row, 2 - turn : 3 - turn, :], (8, CH))
            taps[turn, row] = jnp.where(west_side, first, last)

    def some_rows(index, carry):
        for lane in range(BLK):
            padded[lane, 0:3] = left_ref[index * BLK + lane].astype(f32)
            padded[lane, 7:10] = right_ref[index * BLK + lane].astype(f32)
        for lane in range(BLK):
            for turn in range(3):
                shifts[turn, index * BLK + lane + 3] = padded[lane, turn : turn + 8]
        return carry

    lax.fori_loop(0, LAT // BLK, some_rows, 0)

    def block(index, carry):
        first = index * BLK
        for low, high in ((0, 128), (128, CH)):
            lanes = slice(low, high)
            sums = block_sums(shifts, first, lambda row, turn: taps[turn, row, :, lanes], range(3), lanes)
            side = west_side[:, lanes]
            for target in range(BLK):
                west = west_ref[first + target, :, lanes] + jnp.where(side, sums[target], 0.0)
                east = east_ref[first + target, :, lanes] + jnp.where(side, 0.0, sums[target])
                strips[0, first + target, :, lanes] = west.astype(bf16)
                strips[1, first + target, :, lanes] = east.astype(bf16)
        return carry

    lax.fori_loop(0, LAT // BLK, block, 0)
    places = [(strips.at[0], out_ref.at[:, 0:8]), (strips.at[1], out_ref.at[:, WID - 8 : WID])]
    for copy in fetch(places, sems):
        copy.wait()


def finish_edges(inner, west, east, left, right, kernel):
    return pl.pallas_call(
        edge_kernel,
        in_specs=[pl.BlockSpec(memory_space=pl.ANY)] + [VM] * 5,
        out_specs=pl.BlockSpec(memory_space=pl.ANY),
        out_shape=FIELD,
        input_output_aliases={0: 0},
        compiler_params=limit(4),
        scratch_shapes=[
            pltpu.VMEM((3, LAT + 6, 8, CH), f32), pltpu.VMEM((BLK, 16, CH), f32), pltpu.VMEM((3, 7, 8, CH), f32),
            pltpu.VMEM((2, LAT, 8, CH), bf16), pltpu.SemaphoreType.DMA((2,)),
        ],
        cost_estimate=pl.CostEstimate(flops=5000000, bytes_accessed=700000, transcendentals=0),
    )(inner, west, east, right, left, kernel)


def swap_edges(head, tail):
    peers = lax.axis_size("tile")
    up = [(i, (i + 1) % peers) for i in range(peers)]
    down = [(j, i) for i, j in up]
    right = lax.ppermute(head, "tile", down)
    left = lax.ppermute(tail, "tile", up)
    return left, right


def after(array, other):
    return lax.optimization_barrier((array, other))[0]


def exchange(array, axis):
    return lax.all_to_all(array, axis, split_axis=0, concat_axis=0, tiled=True)


def per_device(
    adjoint_final, states, kernel, norm_gain, up_weight, up_bias, down_weight,
    obs_cell, obs_count, obs_value, obs_error,
):
    gain = norm_gain[None]
    bias = up_bias[None]
    down = down_weight.T

    packed, near = pack_observations(
        obs_cell[:, 0].transpose(0, 2, 1), obs_count, obs_value, obs_error[:, 0].transpose(0, 2, 1), states
    )
    got = exchange(packed, "tile")
    rows = gather_rows(got, near)
    owned = exchange(rows, "member")

    source = after(states, rows)[:, 0]
    left, right = swap_edges(source[:, :, 0:3], source[:, :, WID - 3 : WID])
    hidden, tail, head, later_right, later_left = forward(
        0, states, left, right, kernel, gain, up_weight, bias, down, adjoint_final
    )
    deps = departures(after(owned, hidden), got)
    back = exchange(deps, "member")

    before, behind = swap_edges(*after((head, tail), deps))
    slope, unit = forward(1, after(states, deps), later_left, later_right, kernel, gain, up_weight, bias)
    partial, slope, cells = spread_back(
        hidden, after(behind, slope), before, adjoint_final, kernel, got, slope
    )

    hidden, tail, head, adjoint = second_step(
        partial, after(back, partial), cells, slope, unit, gain, up_weight, down
    )
    left, right = swap_edges(head, tail)
    inner, west, east = interior(hidden, adjoint, back, cells, kernel)
    return finish_edges(inner, west, east, left, right, kernel)[None]


def solution(mesh):
    placed = (
        P("member", None, "tile", None),
        P(None, "member", None, "tile", None),
        P(),
        P(),
        P(),
        P(),
        P(),
        P(None, "tile", None, None),
        P(None, "tile", None),
        P(None, "tile", None, None, None),
        P(None, "tile", None, None),
    )
    return jax.shard_map(
        per_device,
        mesh=mesh,
        in_specs=placed,
        out_specs=P("member", None, "tile", None),
        check_vma=False,
    )
```

```python
import functools
import math

import jax
import jax.numpy as jnp
from jax import lax
from jax.experimental import pallas as pl
from jax.experimental.pallas import tpu as pltpu
from jax.sharding import PartitionSpec as P

slope_coef = math.sqrt(2.0 / math.pi)
cubic_coef = 0.044715
norm_eps = 1e-06

LAT = 32
WID = 32
CH = 192
HID = 768
CAP = 16
CELLS = LAT * WID
SLOTS = LAT * CAP
BLK = 8
ROWS = BLK * WID
UNROLL = 16
HALF = LAT // 2
f32 = jnp.float32
bf16 = jnp.bfloat16
NT = (((1,), (1,)), ((), ()))
TN = (((0,), (0,)), ((), ()))


def gelu_slope(preact):
    square = preact * preact
    tanh_val = jnp.tanh(preact * (slope_coef + (slope_coef * cubic_coef) * square))
    tail = preact * (0.5 * slope_coef + (1.5 * slope_coef * cubic_coef) * square)
    return (0.5 + 0.5 * tanh_val) + tail * (1.0 - tanh_val * tanh_val)


def limit(mebibytes):
    return pltpu.CompilerParams(vmem_limit_bytes=mebibytes * 1024 * 1024)


def mean_lanes(value):
    return jnp.sum(value, axis=-1, keepdims=True) * (1.0 / CH)


HBM = pl.BlockSpec(memory_space=pltpu.HBM)
VM = pl.BlockSpec(memory_space=pltpu.VMEM)


def fetch(pairs, sems):
    copies = [pltpu.make_async_copy(src, dst, sems.at[i]) for i, (src, dst) in enumerate(pairs)]
    for copy in copies:
        copy.start()
    return copies


def far(array):
    return pltpu.with_memory_space_constraint(array, pltpu.HBM)


def clear_rims(shifts, count, width):
    for edge in range(3):
        zeros = jnp.zeros((width, CH), f32)
        for col in range(count):
            shifts[col, edge] = zeros
            shifts[col, LAT + 3 + edge] = zeros


def build_shifts(low, high, padded, centre, left=None, right=None):
    zeros = jnp.zeros((WID, 128), f32)
    for edge in range(3):
        for col in range(7):
            low[col, edge] = zeros
            low[col, LAT + 3 + edge] = zeros
    if left is None:
        padded[...] = jnp.zeros(padded.shape, f32)

    def spread_rows(rows, part, target, offset):
        for lane, row in enumerate(rows):
            if left is not None:
                padded[lane, 0:3] = part(left, row)
                padded[lane, WID + 3 : WID + 6] = part(right, row)
            padded[lane, 3 : WID + 3] = part(centre, row)
        for lane, row in enumerate(rows):
            for col in range(7):
                target[col, row + offset] = padded[lane, col : col + WID]

    def low_part(source, row):
        return source(row)[:, 0:128].astype(f32)

    def high_part(source, row):
        first = source(row - 3)[:, 128:CH].astype(f32) if not isinstance(row, int) or row >= 3 else None
        second = source(row + HALF - 3)[:, 128:CH].astype(f32) if not isinstance(row, int) or row < 19 else None
        first = jnp.zeros_like(second) if first is None else first
        second = jnp.zeros_like(first) if second is None else second
        return jnp.concatenate([first, second], axis=1)

    def some_low(index, carry):
        spread_rows([index * UNROLL + lane for lane in range(UNROLL)], low_part, low, 3)
        return carry

    def some_high(index, carry):
        spread_rows([index * UNROLL + lane + 3 for lane in range(UNROLL)], high_part, high, 0)
        return carry

    lax.fori_loop(0, LAT // UNROLL, some_low, 0)
    lax.fori_loop(0, HALF // UNROLL, some_high, 0)
    spread_rows([0, 1, 2], high_part, high, 0)
    spread_rows([19, 20, 21], high_part, high, 0)


def block_sums(shifts, first, tap, cols=range(7), lanes=slice(0, 128)):
    sums = [None] * BLK
    for place, col in enumerate(cols):
        taps = [tap(row, col) for row in range(7)]
        for source in range(BLK + 6):
            field = shifts[place, first + source, :, lanes]
            for row in range(7):
                target = source - row
                if 0 <= target < BLK:
                    term = taps[row] * field
                    sums[target] = term if sums[target] is None else sums[target] + term
    return sums


def tap_of(kernel_ref, flip, lanes, width):
    def tap(row, col):
        down, across = (6 - row, 6 - col) if flip else (row, col)
        value = kernel_ref[down, across : across + 1, lanes]
        return jnp.broadcast_to(value, (width, value.shape[1]))

    return tap


def convolve(low, high, twice, kernel_ref, flip, emit, done=None):
    for row in range(7):
        upper = kernel_ref[row, :, 128:CH]
        twice[row, 0:7] = jnp.concatenate([upper, upper], axis=1)

    def low_block(index, carry):
        first = index * BLK
        sums = block_sums(low, first, tap_of(kernel_ref, flip, slice(0, 128), WID))
        for target in range(BLK):
            emit(first + target, 0, 128, sums[target])
        return carry

    def high_block(index, carry):
        first = index * BLK
        sums = block_sums(high, first, tap_of(twice, flip, slice(0, 128), WID))
        for target in range(BLK):
            emit(first + target, 128, CH, sums[target][:, 0:64])
            emit(first + target + HALF, 128, CH, sums[target][:, 64:128])
        if done is not None:
            done(index)
        return carry

    lax.fori_loop(0, LAT // BLK, low_block, 0)
    lax.fori_loop(0, HALF // BLK, high_block, 0)


def pack_kernel(
    cell_far, count_far, value_far, error_far, state_far,
    out_ref, near_ref, cell_ref, count_ref, value_ref, error_ref, sems,
):
    member = lax.axis_index("member")
    base = pl.multiple_of(member // 8 * 8, 8)
    near_slots = value_far.at[:, :, :, pl.ds(base, 8), :]
    pairs = [(cell_far, cell_ref), (count_far, count_ref), (near_slots, value_ref), (error_far, error_ref)]
    copies = fetch(pairs + [(state_far, near_ref)], sems)
    for copy in copies[:4]:
        copy.wait()
    tiles = cell_ref.shape[2]
    slot = lax.broadcasted_iota(jnp.int32, (CAP, tiles), 0)
    across = lax.broadcasted_iota(jnp.int32, (CAP, CAP), 1)
    same = jnp.where(lax.broadcasted_iota(jnp.int32, (CAP, CAP), 0) == across, 1.0, 0.0).astype(bf16)
    own = jnp.where(lax.broadcasted_iota(jnp.int32, (CAP, CAP), 0) == member, 1.0, 0.0).astype(bf16)
    deep = lax.broadcasted_iota(jnp.int32, (tiles, 8, CH), 1) + base
    for step in range(2):
        live = slot < count_ref[step]
        cells = jnp.where(live, cell_ref[step], -1).astype(f32).astype(bf16)
        values = jnp.sum(jnp.where(deep == member, value_ref[step, 0].astype(f32), 0.0), axis=1)
        turn = lambda array, pick: lax.dot_general(array, pick, TN, preferred_element_type=f32)
        out_ref[:, 2 * step, :] = values[:, 0:128]
        out_ref[:, 2 * step + 1, :] = jnp.concatenate(
            [values[:, 128:CH], turn(cells, same), turn(error_ref[step], own), turn(cells, own), jnp.zeros((tiles, CAP), f32)],
            axis=1)
    copies[4].wait()


def pack_observations(cells, counts, values, errors, states):
    return pl.pallas_call(
        pack_kernel,
        out_shape=(jax.ShapeDtypeStruct((cells.shape[2], 4, 128), f32), pltpu.VMEM(states.shape, bf16)),
        in_specs=[HBM] * 5,
        out_specs=(VM, VM),
        scratch_shapes=[pltpu.VMEM(array.shape, array.dtype) for array in (cells, counts, values[:, :, :, :8], errors)]
        + [pltpu.SemaphoreType.DMA((5,))],
        compiler_params=limit(6),
    )(far(cells), far(counts), far(values), far(errors), far(states))


def one_hot(step, got_ref, group):
    cells = got_ref[group * BLK : (group + 1) * BLK, 2 * step + 1, 64 : 64 + CAP]
    lane = lax.broadcasted_iota(jnp.int32, (BLK, ROWS), 1)
    band = lax.broadcasted_iota(jnp.int32, (BLK, ROWS), 0)
    offset = (lane - band * WID).astype(f32)
    rows = [jnp.where(offset == cells[:, slot : slot + 1], 1.0, 0.0) for slot in range(CAP)]
    return jnp.concatenate(rows, axis=0)


def gather_kernel(got_ref, state_ref, out_far, out_ref, sems):
    copies = []
    for step in range(2):
        for pair in range(2):
            found = []
            for group in (2 * pair, 2 * pair + 1):
                field = state_ref[step, 0, group * BLK : (group + 1) * BLK].reshape(ROWS, CH)
                hot = one_hot(step, got_ref, group).astype(bf16)
                rows = jnp.dot(hot, field, preferred_element_type=f32)
                found.append(rows.reshape(CAP, BLK, CH))
            both = jnp.concatenate(found, axis=1).astype(bf16)
            out_ref[:, 2 * BLK * pair : 2 * BLK * (pair + 1), step * CH : (step + 1) * CH] = both
            if step == 1:
                part = slice(2 * BLK * pair, 2 * BLK * (pair + 1))
                copies.append(pltpu.make_async_copy(out_ref.at[:, part], out_far.at[:, part], sems.at[pair]))
                copies[-1].start()
    for copy in copies:
        copy.wait()


def gather_rows(got, states):
    return pl.pallas_call(
        gather_kernel,
        out_shape=pltpu.HBM((CAP, LAT, 2 * CH), bf16),
        out_specs=HBM,
        scratch_shapes=[pltpu.VMEM((CAP, LAT, 2 * CH), bf16), pltpu.SemaphoreType.DMA((2,))],
        compiler_params=limit(6),
        cost_estimate=pl.CostEstimate(flops=1000000, bytes_accessed=2000000, transcendentals=0),
    )(got, states)


def departure_kernel(rows_ref, got_ref, out_far, out_ref, sems):
    stats = []
    for step in range(2):
        sampled = rows_ref[:, :, step * CH : (step + 1) * CH].astype(f32)
        members = sampled.shape[0]
        other = got_ref[:, 2 * step + 1, :]
        values = jnp.concatenate([got_ref[:, 2 * step, :], other[:, 0:64]], axis=1)
        ens_mean = jnp.sum(sampled, axis=0) * (1.0 / members)
        ens_var = jnp.sum(sampled * sampled, axis=0) * (1.0 / members) - ens_mean * ens_mean
        weight = 1.0 / (other[:, 64 + CAP : 65 + CAP] + ens_var)
        stats.append((values, weight, other[:, 64 + 2 * CAP : 65 + 2 * CAP] >= 0.0))
    copies = []
    for half in range(2):
        part = slice(half * CAP // 2, (half + 1) * CAP // 2)
        for step, (values, weight, live) in enumerate(stats):
            lanes = slice(step * CH, (step + 1) * CH)
            ratio = (rows_ref[part, :, lanes].astype(f32) - values[None]) * weight[None]
            out_ref[part, :, lanes] = jnp.where(live[None], ratio, 0.0).astype(bf16)
        copies.append(pltpu.make_async_copy(out_ref.at[part], out_far.at[part], sems.at[half]))
        copies[-1].start()
    for copy in copies:
        copy.wait()


def departures(rows, got):
    return pl.pallas_call(
        departure_kernel,
        out_shape=pltpu.HBM((CAP, LAT, 2 * CH), bf16),
        out_specs=HBM,
        scratch_shapes=[pltpu.VMEM((CAP, LAT, 2 * CH), bf16), pltpu.SemaphoreType.DMA((2,))],
        compiler_params=limit(6),
        cost_estimate=pl.CostEstimate(flops=1200000, bytes_accessed=1200000, transcendentals=0),
    )(rows, got)


def cell_row(step, got_ref, group):
    cells = got_ref[group * BLK : (group + 1) * BLK, 2 * step + 1, 64 : 64 + CAP]
    band = lax.broadcasted_iota(jnp.int32, (BLK, CAP), 0).astype(f32)
    cells = jnp.where(cells < 0.0, -1.0, cells + band * WID)
    column = jnp.concatenate([cells[:, slot : slot + 1] for slot in range(CAP)], axis=0)
    return jnp.broadcast_to(column, (CAP * BLK, CAP * BLK)).T[0:1]


def forcing_of(step, rows_ref, cell_ref, group):
    place = step * (LAT // BLK) + group
    cells = jnp.broadcast_to(cell_ref[place : place + 1, :], (ROWS, CAP * BLK))
    cell = lax.broadcasted_iota(jnp.int32, (ROWS, CAP * BLK), 0).astype(f32)
    hot = jnp.where(cell == cells, 1.0, 0.0).astype(bf16)
    rows = rows_ref[:, :, step * CH : (step + 1) * CH].astype(f32)[:, group * BLK : (group + 1) * BLK]
    rows = rows.reshape(CAP * BLK, CH).astype(bf16)
    return jnp.dot(hot, rows, preferred_element_type=f32)


def normalise(hidden):
    centred = hidden - mean_lanes(hidden)
    inv_std = lax.rsqrt(mean_lanes(centred * centred) + norm_eps)
    return centred * inv_std, inv_std


def backward(adjoint, slope_at, down_ref, up_ref, gain, unit):
    adj_norm = jnp.zeros((ROWS, CH), f32)
    for part in range(3):
        cols = slice(part * 256, (part + 1) * 256)
        act = jnp.dot(adjoint, down_ref[:, cols], preferred_element_type=f32)
        pre = (act * slope_at(cols)).astype(bf16)
        adj_norm = adj_norm + lax.dot_general(pre, up_ref[:, cols], NT, preferred_element_type=f32)
    scaled = adj_norm * gain
    return scaled - mean_lanes(scaled) - unit * mean_lanes(scaled * unit)


def put_hidden(adj_hidden, first, out_ref, tail_ref, head_ref):
    block = adj_hidden.astype(bf16).reshape(BLK, WID, CH)
    out_ref[pl.ds(first, BLK)] = block
    head_ref[pl.ds(first, BLK)] = block[:, 0:3]
    tail_ref[pl.ds(first, BLK)] = block[:, WID - 3 : WID]


def forward_kernel(step, state_ref, left_ref, right_ref, kernel_ref, gain_ref, up_ref, bias_ref, *rest):
    low, high, twice, padded, hidden = rest[-5:]
    if step == 0:
        later_right, later_left = rest[5:7]
        later_right[...] = right_ref[1]
        later_left[...] = left_ref[1]
        right_ref, left_ref = right_ref.at[0], left_ref.at[0]
    gain = gain_ref[...]
    build_shifts(
        low, high, padded,
        lambda row: state_ref[step, 0, row],
        lambda row: left_ref[row],
        lambda row: right_ref[row],
    )

    def emit(row, start, stop, value):
        hidden[row, :, start:stop] = value

    convolve(low, high, twice, kernel_ref, False, emit)

    def block(index, carry):
        first = index * BLK
        unit, inv_std = normalise(hidden[pl.ds(first, BLK)].reshape(ROWS, CH))
        normed = (unit * gain).astype(bf16)

        def slope_at(cols):
            preact = jnp.dot(normed, up_ref[:, cols], preferred_element_type=f32)
            return gelu_slope(preact + bias_ref[:, cols]) * inv_std

        if step == 0:
            down_ref, adjoint_ref, hidden_out, tail_out, head_out = rest[:5]
            adjoint = adjoint_ref[0, pl.ds(first, BLK)].reshape(ROWS, CH)
            result = backward(adjoint, slope_at, down_ref, up_ref, gain, unit)
            put_hidden(result, first, hidden_out, tail_out, head_out)
        else:
            slope_out, unit_out = rest[:2]
            rows = pl.ds(pl.multiple_of(index * ROWS, ROWS), ROWS)
            for part in range(3):
                cols = slice(part * 256, (part + 1) * 256)
                slope_out[rows, cols] = slope_at(cols).astype(bf16)
            unit_out[rows, :] = unit.astype(bf16)
        return carry

    lax.fori_loop(0, LAT // BLK, block, 0)


FAR_EDGE = pltpu.HBM((LAT, 3, CH), bf16)
EDGE = jax.ShapeDtypeStruct((LAT, 3, CH), bf16)
FIELD = jax.ShapeDtypeStruct((LAT, WID, CH), bf16)
SHIFT_SCRATCH = [
    pltpu.VMEM((7, LAT + 6, WID, 128), f32),
    pltpu.VMEM((7, HALF + 6, WID, 128), f32),
    pltpu.VMEM((7, 8, 128), f32),
    pltpu.VMEM((UNROLL, WID + 8, 128), f32),
]


def forward(step, states, left, right, *others):
    shapes = (pltpu.HBM((LAT, WID, CH), bf16),) + (FAR_EDGE,) * 4 if step == 0 else (
        pltpu.HBM((CELLS, HID), bf16), pltpu.HBM((CELLS, CH), bf16)
    )
    return pl.pallas_call(
        functools.partial(forward_kernel, step),
        out_shape=shapes,
        out_specs=(VM,) * len(shapes),
        scratch_shapes=SHIFT_SCRATCH + [pltpu.VMEM((LAT, WID, CH), f32)],
        compiler_params=limit(16),
        cost_estimate=pl.CostEstimate(flops=6 * CELLS * CH * HID, bytes_accessed=8000000, transcendentals=CELLS * HID),
    )(states, left, right, *others)


def spread_kernel(
    hidden_ref, right_ref, left_ref, base_ref, kernel_ref, got_ref, slope_far,
    out_ref, slope_out, cell_out,
    low, high, twice, padded, sems,
):
    copies = fetch([(slope_far, slope_out)], sems)
    for step in range(2):
        for group in range(LAT // BLK):
            place = step * (LAT // BLK) + group
            cell_out[place : place + 1, :] = cell_row(step, got_ref, group)
    build_shifts(
        low, high, padded,
        lambda row: hidden_ref[row],
        lambda row: left_ref[row],
        lambda row: right_ref[row],
    )

    def emit(row, start, stop, value):
        out_ref[row, :, start:stop] = base_ref[0, row, :, start:stop].astype(f32) + value

    convolve(low, high, twice, kernel_ref, True, emit)
    for copy in copies:
        copy.wait()


def spread_back(hidden, right, left, base, kernel, got, slope):
    return pl.pallas_call(
        spread_kernel,
        out_shape=(
            jax.ShapeDtypeStruct((LAT, WID, CH), f32),
            jax.ShapeDtypeStruct(slope.shape, bf16),
            jax.ShapeDtypeStruct((2 * LAT // BLK, CAP * BLK), f32),
        ),
        in_specs=[VM] * 6 + [HBM],
        scratch_shapes=SHIFT_SCRATCH + [pltpu.SemaphoreType.DMA((1,))],
        compiler_params=limit(18),
        cost_estimate=pl.CostEstimate(flops=98 * CELLS * CH, bytes_accessed=3000000, transcendentals=0),
    )(hidden, right, left, base, kernel, got, far(slope))


def second_kernel(
    partial_ref, rows_ref, cell_ref, slope_ref, unit_far, gain_ref, up_ref, down_far,
    hidden_out, tail_out, head_out, adjoint_out, unit_ref, down_ref, sems,
):
    copies = fetch([(down_far, down_ref), (unit_far, unit_ref)], sems)
    gain = gain_ref[...]
    for group in range(LAT // BLK):
        first = group * BLK
        forcing = forcing_of(0, rows_ref, cell_ref, group)
        adjoint = (partial_ref[first : first + BLK].reshape(ROWS, CH) + forcing).astype(bf16)
        adjoint_out[first : first + BLK] = adjoint.reshape(BLK, WID, CH)
    for copy in copies:
        copy.wait()
    for group in range(LAT // BLK):
        first = group * BLK
        rows = slice(group * ROWS, (group + 1) * ROWS)
        result = backward(
            adjoint_out[first : first + BLK].reshape(ROWS, CH),
            lambda cols: slope_ref[rows, cols].astype(f32),
            down_ref, up_ref, gain,
            unit_ref[rows, :].astype(f32),
        )
        put_hidden(result, first, hidden_out, tail_out, head_out)


def second_step(partial, rows, hot, slope, unit, gain, up, down):
    return pl.pallas_call(
        second_kernel,
        out_shape=(FIELD, EDGE, EDGE, FIELD),
        in_specs=[VM] * 4 + [HBM, VM, VM, HBM],
        scratch_shapes=[pltpu.VMEM((CELLS, CH), bf16), pltpu.VMEM((CH, HID), bf16), pltpu.SemaphoreType.DMA((2,))],
        compiler_params=limit(8),
        cost_estimate=pl.CostEstimate(flops=4 * CELLS * CH * HID, bytes_accessed=5000000, transcendentals=0),
    )(partial, rows, hot, slope, far(unit), gain, up, far(down))


def interior_kernel(
    hidden_ref, adjoint_ref, rows_ref, hot_ref, kernel_ref, out_far, west_ref, east_ref,
    low, high, twice, padded, total, out_ref, sems,
):
    build_shifts(low, high, padded, lambda row: hidden_ref[row])
    for group in range(LAT // BLK):
        first = group * BLK
        forcing = forcing_of(1, rows_ref, hot_ref, group).reshape(BLK, WID, CH)
        total[first : first + BLK] = adjoint_ref[first : first + BLK].astype(f32) + forcing

    def emit(row, start, stop, value):
        value = total[row, :, start:stop] + value
        out_ref[row, :, start:stop] = value[8 : WID - 8].astype(bf16)
        west_ref[row, :, start:stop] = value[0:8]
        east_ref[row, :, start:stop] = value[WID - 8 : WID]

    def copy_of(first, place):
        rows = pl.ds(first, BLK)
        return pltpu.make_async_copy(out_ref.at[rows], out_far.at[rows, 8 : WID - 8], sems.at[place])

    def done(index):
        copy_of(index * BLK, index).start()
        copy_of(index * BLK + HALF, index + 2).start()

    convolve(low, high, twice, kernel_ref, True, emit, done)
    for place, first in enumerate((0, BLK, HALF, HALF + BLK)):
        copy_of(first, place).wait()


STRIP = jax.ShapeDtypeStruct((LAT, 8, CH), f32)


def interior(hidden, adjoint, rows, hot, kernel):
    return pl.pallas_call(
        interior_kernel,
        out_shape=(pltpu.HBM((LAT, WID, CH), bf16), STRIP, STRIP),
        out_specs=(HBM, VM, VM),
        scratch_shapes=SHIFT_SCRATCH + [
            pltpu.VMEM((LAT, WID, CH), f32), pltpu.VMEM((LAT, WID - 16, CH), bf16), pltpu.SemaphoreType.DMA((4,)),
        ],
        compiler_params=limit(16),
        cost_estimate=pl.CostEstimate(flops=98 * CELLS * CH, bytes_accessed=3000000, transcendentals=0),
    )(hidden, adjoint, rows, hot, kernel)


def edge_kernel(
    inner_ref, west_ref, east_ref, right_ref, left_ref, kernel_ref, out_ref,
    shifts, padded, taps, strips, sems,
):
    clear_rims(shifts, 3, 8)
    padded[...] = jnp.zeros(padded.shape, f32)
    west_side = lax.broadcasted_iota(jnp.int32, (8, CH), 0) < 4
    for row in range(7):
        for turn in range(3):
            first = jnp.broadcast_to(kernel_ref[6 - row, 6 - turn : 7 - turn, :], (8, CH))
            last = jnp.broadcast_to(kernel_ref[6 - row, 2 - turn : 3 - turn, :], (8, CH))
            taps[turn, row] = jnp.where(west_side, first, last)

    def some_rows(index, carry):
        for lane in range(BLK):
            padded[lane, 0:3] = left_ref[index * BLK + lane].astype(f32)
            padded[lane, 7:10] = right_ref[index * BLK + lane].astype(f32)
        for lane in range(BLK):
            for turn in range(3):
                shifts[turn, index * BLK + lane + 3] = padded[lane, turn : turn + 8]
        return carry

    lax.fori_loop(0, LAT // BLK, some_rows, 0)

    def block(index, carry):
        first = index * BLK
        for low, high in ((0, 128), (128, CH)):
            lanes = slice(low, high)
            sums = block_sums(shifts, first, lambda row, turn: taps[turn, row, :, lanes], range(3), lanes)
            side = west_side[:, lanes]
            for target in range(BLK):
                west = west_ref[first + target, :, lanes] + jnp.where(side, sums[target], 0.0)
                east = east_ref[first + target, :, lanes] + jnp.where(side, 0.0, sums[target])
                strips[0, first + target, :, lanes] = west.astype(bf16)
                strips[1, first + target, :, lanes] = east.astype(bf16)
        return carry

    lax.fori_loop(0, LAT // BLK, block, 0)
    places = [(strips.at[0], out_ref.at[:, 0:8]), (strips.at[1], out_ref.at[:, WID - 8 : WID])]
    for copy in fetch(places, sems):
        copy.wait()


def finish_edges(inner, west, east, left, right, kernel):
    return pl.pallas_call(
        edge_kernel,
        in_specs=[pl.BlockSpec(memory_space=pl.ANY)] + [VM] * 5,
        out_specs=pl.BlockSpec(memory_space=pl.ANY),
        out_shape=FIELD,
        input_output_aliases={0: 0},
        compiler_params=limit(4),
        scratch_shapes=[
            pltpu.VMEM((3, LAT + 6, 8, CH), f32), pltpu.VMEM((BLK, 16, CH), f32), pltpu.VMEM((3, 7, 8, CH), f32),
            pltpu.VMEM((2, LAT, 8, CH), bf16), pltpu.SemaphoreType.DMA((2,)),
        ],
        cost_estimate=pl.CostEstimate(flops=5000000, bytes_accessed=700000, transcendentals=0),
    )(inner, west, east, right, left, kernel)


def swap_edges(head, tail):
    peers = lax.axis_size("tile")
    up = [(i, (i + 1) % peers) for i in range(peers)]
    down = [(j, i) for i, j in up]
    right = lax.ppermute(head, "tile", down)
    left = lax.ppermute(tail, "tile", up)
    return left, right


def after(array, other):
    return lax.optimization_barrier((array, other))[0]


def exchange(array, axis):
    return lax.all_to_all(array, axis, split_axis=0, concat_axis=0, tiled=True)


def per_device(
    adjoint_final, states, kernel, norm_gain, up_weight, up_bias, down_weight,
    obs_cell, obs_count, obs_value, obs_error,
):
    gain = norm_gain[None]
    bias = up_bias[None]
    down = down_weight.T

    packed, near = pack_observations(
        obs_cell[:, 0].transpose(0, 2, 1), obs_count, obs_value, obs_error[:, 0].transpose(0, 2, 1), states
    )
    got = exchange(packed, "tile")
    rows = gather_rows(got, near)
    owned = exchange(rows, "member")

    source = after(states, rows)[:, 0]
    left, right = swap_edges(source[:, :, 0:3], source[:, :, WID - 3 : WID])
    hidden, tail, head, later_right, later_left = forward(
        0, states, left, right, kernel, gain, up_weight, bias, down, adjoint_final
    )
    deps = departures(after(owned, hidden), got)
    back = exchange(deps, "member")

    before, behind = swap_edges(*after((head, tail), deps))
    slope, unit = forward(1, after(states, deps), later_left, later_right, kernel, gain, up_weight, bias)
    partial, slope, cells = spread_back(
        hidden, after(behind, slope), before, adjoint_final, kernel, got, slope
    )

    hidden, tail, head, adjoint = second_step(
        partial, after(back, partial), cells, slope, unit, gain, up_weight, down
    )
    left, right = swap_edges(head, tail)
    inner, west, east = interior(hidden, adjoint, back, cells, kernel)
    return finish_edges(inner, west, east, left, right, kernel)[None]


def solution(mesh):
    placed = (
        P("member", None, "tile", None),
        P(None, "member", None, "tile", None),
        P(),
        P(),
        P(),
        P(),
        P(),
        P(None, "tile", None, None),
        P(None, "tile", None),
        P(None, "tile", None, None, None),
        P(None, "tile", None, None),
    )
    return jax.shard_map(
        per_device,
        mesh=mesh,
        in_specs=placed,
        out_specs=P("member", None, "tile", None),
        check_vma=False,
    )
```
